32 devices in a mesh: section: 4 (over y, x), dp: 8 (over z, core).
Axes of the slice: x: 2, y: 2, z: 4, core: 2. Of those that a mesh axis runs over, the one named last changes fastest.
Arguments:
- big_crops: bfloat16 [8, 16, 14, 14, 384], P(None, 'dp'), may hold values from -6 to 6
- small_crops: bfloat16 [8, 48, 6, 6, 384], P(None, 'dp'), may hold values from -6 to 6
- big_cot: bfloat16 [8, 16, 7, 7, 768], P(None, 'dp'), may hold values from -6 to 6
- small_cot: bfloat16 [8, 48, 3, 3, 768], P(None, 'dp'), may hold values from -6 to 6
- drop_mask: int32 [8, 8], P(None, 'dp'), may hold values 0 or 1
- kernel_w: float32 [49, 384], P(None, 'dp'), may hold values from -4 to 4
- kernel_mom: float32 [49, 384], P(None, 'dp'), may hold values from -69.041437 to 69.041437
- kernel_avg: float32 [49, 384], P(None, 'dp'), may hold values from -4 to 4
- vector_w: float32 [13, 384], P(None, 'dp'), may hold values from -1 to 2
- vector_mom: float32 [13, 384], P(None, 'dp'), may hold values from -394.5225 to 394.5225
- vector_avg: float32 [13, 384], P(None, 'dp'), may hold values from -1 to 2
- up_w: float32 [384, 1536], P(None, 'dp'), may hold values from -4 to 4
- up_mom: float32 [384, 1536], P(None, 'dp'), may hold values from -10.066446 to 10.066446
- up_avg: float32 [384, 1536], P(None, 'dp'), may hold values from -4 to 4
- down_w: float32 [1536, 384], P('dp'), may hold values from -4 to 4
- down_mom: float32 [1536, 384], P('dp'), may hold values from -10.066446 to 10.066446
- down_avg: float32 [1536, 384], P('dp'), may hold values from -4 to 4
- strided_w: float32 [1536, 768], P('dp'), may hold values from -4 to 4
- strided_mom: float32 [1536, 768], P('dp'), may hold values from -10.066446 to 10.066446
- strided_avg: float32 [1536, 768], P('dp'), may hold values from -4 to 4
Outputs:
- out_big: float32 [8, 16, 7, 7, 768], P('section', 'dp')
- out_small: float32 [8, 48, 3, 3, 768], P('section', 'dp')
- grad_big: float32 [8, 16, 14, 14, 384], P('section', 'dp')
- grad_small: float32 [8, 48, 6, 6, 384], P('section', 'dp')
- kernel_next: float32 [49, 384], P(None, 'dp')
- kernel_mom_next: float32 [49, 384], P(None, 'dp')
- kernel_avg_next: float32 [49, 384], P(None, 'dp')
- vector_next: float32 [13, 384], P(None, 'dp')
- vector_mom_next: float32 [13, 384], P(None, 'dp')
- vector_avg_next: float32 [13, 384], P(None, 'dp')
- up_next: float32 [384, 1536], P(None, 'dp')
- up_mom_next: float32 [384, 1536], P(None, 'dp')
- up_avg_next: float32 [384, 1536], P(None, 'dp')
- down_next: float32 [1536, 384], P('dp')
- down_mom_next: float32 [1536, 384], P('dp')
- down_avg_next: float32 [1536, 384], P('dp')
- strided_next: float32 [1536, 768], P('dp')
- strided_mom_next: float32 [1536, 768], P('dp')
- strided_avg_next: float32 [1536, 768], P('dp')
The draws below stay inside these ranges and needn't reach their ends.
All inputs are finite; a program needn't handle non-finite values. No bound on the sum of `drop_mask` on one device may be relied on, other than what follows from the above.
Results may differ from the reference program's by a relative error of at most 0.0094.
Values may be sent and summed in bfloat16 or wider, within the bound.
A program may use at most 192 MiB of HBM per device.

```python
import math
import jax
import jax.numpy as jnp
from jax import lax

C = 384
FF = 1536
C2 = 768
KS = 7
SB = 14
SS = 6
BIG_IMG = 2
SMALL_IMG = 6
MICRO = 8
IMG_MB = 8
BIG_MB = 16
SMALL_MB = 48
PIXELS = 38912


def base_noise(key, grid_shape):
    return jax.random.truncated_normal(key, -4.0, 4.0, grid_shape, jnp.float32)


def vector_law(key):
    first_key, second_key = jax.random.split(key)
    up_rows = FF // C
    total_rows = 7 + up_rows + C2 // C
    grid_shape = (total_rows, C)
    row_ids = jnp.arange(total_rows)[:, None]
    spread = jax.random.uniform(first_key, grid_shape, jnp.float32)
    gain_rows = (row_ids == 1) | (row_ids == 5 + up_rows)
    scale_rows = row_ids == 4 + up_rows
    return jnp.where(gain_rows, 0.6 + 0.8 * spread, jnp.where(scale_rows, 1.0 + spread, 0.25 * base_noise(second_key, grid_shape)))


def draw_vector_w(key, part):
    return vector_law(jax.random.fold_in(key, 11))


def draw_vector_avg(key, part):
    return vector_law(jax.random.fold_in(key, 12))


def draw_kernel_mom(key, part):
    return 0.6 * math.sqrt(PIXELS / (KS * KS)) * base_noise(jax.random.fold_in(key, 21), (KS * KS, C))


def draw_vector_mom(key, part):
    return 0.5 * math.sqrt(PIXELS) * base_noise(jax.random.fold_in(key, 22), (7 + FF // C + C2 // C, C))


def draw_up_mom(key, part):
    return 0.25 * math.sqrt(PIXELS / C) * base_noise(jax.random.fold_in(key, 23), (C, FF))


def draw_down_mom(key, part):
    return 0.5 * math.sqrt(PIXELS / FF) * base_noise(jax.random.fold_in(key, 24), (FF, C))


def draw_strided_mom(key, part):
    return 0.5 * math.sqrt(PIXELS / (4 * C)) * base_noise(jax.random.fold_in(key, 25), (4 * C, C2))


def set_ends(values, key, smallest, largest):
    extent = values.shape
    spot = [jax.random.randint(jax.random.fold_in(key, axis), (), 0, extent[axis]) for axis in range(len(extent))]
    values = values.at[tuple(spot)].set(smallest)
    longest = extent.index(max(extent))
    spot[longest] = (spot[longest] + 1) % extent[longest]
    return values.at[tuple(spot)].set(largest)


def levels(stream_key, extent, cuts, low, top_value):
    gain, own = 1.0, jax.random.fold_in(stream_key, 6)
    for dim, parts in cuts:
        heights = jnp.exp(jax.random.uniform(jax.random.fold_in(own, dim), (parts,), jnp.float32, low / len(cuts), top_value / len(cuts)))
        gain = gain * jnp.repeat(heights, extent[dim] // parts).reshape([-1 if axis == dim else 1 for axis in range(len(extent))])
    return gain


def noise(own_key, extent, deviation, reach, cuts=(), kind=jnp.bfloat16):
    loudness = levels(own_key, extent, cuts, -0.22, 0.18) if cuts else 1.0
    array = jax.random.normal(own_key, extent, jnp.float32) * deviation * loudness
    return jnp.minimum(jnp.maximum(array, -reach), reach).astype(kind)


def setup_inputs(seed: int = 0) -> dict:
    arg_keys = jax.random.split(jax.random.key(seed), 21)
    big_crops = noise(arg_keys[0], (MICRO, BIG_MB, SB, SB, C), 1.0, 6.0, ((1, 8),))
    small_crops = noise(arg_keys[1], (MICRO, SMALL_MB, SS, SS, C), 1.0, 6.0, ((1, 8),))
    big_cot = noise(arg_keys[2], (MICRO, BIG_MB, SB // 2, SB // 2, C2), 1.0, 6.0, ((1, 8),))
    small_cot = noise(arg_keys[3], (MICRO, SMALL_MB, SS // 2, SS // 2, C2), 1.0, 6.0, ((1, 8),))
    drop_mask = set_ends((jax.random.randint(arg_keys[4], (MICRO, IMG_MB), 0, 10) < 9).astype(jnp.int32), jax.random.fold_in(arg_keys[4], 1), 0, 1)
    kernel_w = noise(arg_keys[5], (KS * KS, C), 1.0, 4.0, ((1, 8),), jnp.float32)
    kernel_mom = draw_kernel_mom(jax.random.fold_in(arg_keys[20], 71), 0)
    kernel_avg = noise(arg_keys[7], (KS * KS, C), 1.0, 4.0, ((1, 8),), jnp.float32)
    vector_w = draw_vector_w(jax.random.fold_in(arg_keys[20], 71), 0)
    vector_mom = draw_vector_mom(jax.random.fold_in(arg_keys[20], 71), 0)
    vector_avg = draw_vector_avg(jax.random.fold_in(arg_keys[20], 71), 0)
    up_w = noise(arg_keys[11], (C, FF), 1.0, 4.0, ((1, 8),), jnp.float32)
    up_mom = draw_up_mom(jax.random.fold_in(arg_keys[20], 71), 0)
    up_avg = noise(arg_keys[13], (C, FF), 1.0, 4.0, ((1, 8),), jnp.float32)
    down_w = noise(arg_keys[14], (FF, C), 1.0, 4.0, ((0, 8),), jnp.float32)
    down_mom = draw_down_mom(jax.random.fold_in(arg_keys[20], 71), 0)
    down_avg = noise(arg_keys[16], (FF, C), 1.0, 4.0, ((0, 8),), jnp.float32)
    strided_w = noise(arg_keys[17], (4 * C, C2), 1.0, 4.0, ((0, 8),), jnp.float32)
    strided_mom = draw_strided_mom(jax.random.fold_in(arg_keys[20], 71), 0)
    strided_avg = noise(arg_keys[19], (4 * C, C2), 1.0, 4.0, ((0, 8),), jnp.float32)
    return {"big_crops": big_crops, "small_crops": small_crops, "big_cot": big_cot, "small_cot": small_cot, "drop_mask": drop_mask, "kernel_w": kernel_w, "kernel_mom": kernel_mom, "kernel_avg": kernel_avg, "vector_w": vector_w, "vector_mom": vector_mom, "vector_avg": vector_avg, "up_w": up_w, "up_mom": up_mom, "up_avg": up_avg, "down_w": down_w, "down_mom": down_mom, "down_avg": down_avg, "strided_w": strided_w, "strided_mom": strided_mom, "strided_avg": strided_avg}


@jax.custom_vjp
def low(v):
    return lax.optimization_barrier(v.astype(jnp.bfloat16)).astype(jnp.float32)

@jax.custom_vjp
def low_back(v):
    return v

def low_keep(v):
    return (low(v), None)

def low_pass(kept, grad):
    return (grad,)

def back_keep(v):
    return (v, None)

def back_low(kept, grad):
    return (low(grad),)
low.defvjp(low_keep, low_pass)
low_back.defvjp(back_keep, back_low)
KEEP_RATE = 0.9
MOMENTUM = 0.5
AVERAGING = 0.5
EPSILON = 1e-06
RATES = (1.1, 0.4, 2.7, 1.3, 1.3)
HIGHEST = lax.Precision.HIGHEST

def layer_norm(values, gain_row, offset_row):
    average = lax.optimization_barrier(jnp.mean(values, axis=-1, keepdims=True))
    centered = values - average
    variance = lax.optimization_barrier(jnp.mean(centered * centered, axis=-1, keepdims=True))
    return centered * lax.rsqrt(variance + EPSILON) * gain_row + offset_row

def depthwise(crop_field, kernel):
    radius = KS // 2
    return lax.conv_general_dilated(crop_field, kernel.reshape(KS, KS, 1, C), (1, 1), ((radius, radius), (radius, radius)), dimension_numbers=('NHWC', 'HWIO', 'NHWC'), feature_group_count=C, precision=HIGHEST)

def unpack(vector):
    up_rows = FF // C
    return (vector[0], vector[1], vector[2], vector[3:3 + up_rows].reshape(FF), vector[3 + up_rows], vector[4 + up_rows], vector[5 + up_rows], vector[6 + up_rows], vector[7 + up_rows:].reshape(C2))

def to_blocks(crop_field):
    crop_count, crop_side = (crop_field.shape[0], crop_field.shape[1])
    half_side = crop_side // 2
    return crop_field.reshape(crop_count, half_side, 2, half_side, 2, C).transpose(0, 1, 3, 2, 4, 5).reshape(crop_count * half_side * half_side, 4 * C)

def group_forward(crop_field, keep_crop, weights):
    kernel, vector, up_w, down_w, strided_w = weights
    bias_dw, gain_one, offset_one, bias_up, bias_down, layer_scale, gain_two, offset_two, bias_out = unpack(vector)
    crop_count, crop_side = (crop_field.shape[0], crop_field.shape[1])
    conv_out = depthwise(crop_field, kernel) * (1.0 / KS) + bias_dw
    normed = low(low_back(layer_norm(conv_out, gain_one, offset_one)))
    flat_rows = normed.reshape(-1, C)
    pre_act = low_back(jnp.dot(flat_rows, up_w, precision=HIGHEST) * (1.0 / math.sqrt(C)) + bias_up)
    hidden = low(jax.nn.gelu(pre_act, approximate=False))
    branch = low_back(jnp.dot(hidden, down_w, precision=HIGHEST) * (1.0 / math.sqrt(FF)) + bias_down)
    mixed_sum = crop_field + (layer_scale * branch).reshape(crop_field.shape) * keep_crop[:, None, None, None]
    zeta_norm = low(low_back(layer_norm(mixed_sum, gain_two, offset_two)))
    result = jnp.dot(to_blocks(zeta_norm), strided_w, precision=HIGHEST) * (1.0 / math.sqrt(4 * C)) + bias_out
    half_side = crop_side // 2
    return result.reshape(crop_count, half_side, half_side, C2)

def reference(big_crops, small_crops, big_cot, small_cot, drop_mask, kernel_w, kernel_mom, kernel_avg, vector_w, vector_mom, vector_avg, up_w, up_mom, up_avg, down_w, down_mom, down_avg, strided_w, strided_mom, strided_avg):
    params = (kernel_w, vector_w, up_w, down_w, strided_w)
    keep_image = drop_mask.astype(jnp.float32) / KEEP_RATE
    keep_big = jnp.repeat(keep_image, BIG_IMG, axis=1)
    keep_small = jnp.repeat(keep_image, SMALL_IMG, axis=1)

    def one_micro(totals, pieces):
        field_big, field_small, cot_big, cot_small, factor_big, factor_small = pieces

        def forward(weights, crops_big, crops_small):
            lowered = tuple((low(weight) for weight in weights))
            return (group_forward(crops_big, factor_big, lowered), group_forward(crops_small, factor_small, lowered))
        outputs, pullback = jax.vjp(forward, params, field_big.astype(jnp.float32), field_small.astype(jnp.float32))
        gradients, grad_big, grad_small = pullback((cot_big.astype(jnp.float32), cot_small.astype(jnp.float32)))
        totals = tuple((running + addend for running, addend in zip(totals, gradients)))
        return (totals, (outputs[0], outputs[1], grad_big, grad_small))
    zero_totals = tuple((jnp.zeros_like(weight) for weight in params))
    totals, stacked = lax.scan(one_micro, zero_totals, (big_crops, small_crops, big_cot, small_cot, keep_big, keep_small))
    moments = (kernel_mom, vector_mom, up_mom, down_mom, strided_mom)
    averages = (kernel_avg, vector_avg, up_avg, down_avg, strided_avg)
    fans = (KS * KS, 1, C, FF, 4 * C)
    updates = []
    for position in range(5):
        step_rate = RATES[position] * math.sqrt(fans[position] / PIXELS)
        moment_next = MOMENTUM * moments[position] + totals[position]
        weight_next = params[position] - step_rate * (totals[position] + MOMENTUM * moment_next)
        average_next = AVERAGING * averages[position] + (1.0 - AVERAGING) * weight_next
        updates.append((weight_next, moment_next, average_next))
    return (stacked[0], stacked[1], stacked[2], stacked[3], updates[0][0], updates[0][1], updates[0][2], updates[1][0], updates[1][1], updates[1][2], updates[2][0], updates[2][1], updates[2][2], updates[3][0], updates[3][1], updates[3][2], updates[4][0], updates[4][1], updates[4][2])
```

```python
import math

import jax
import jax.numpy as jnp
from jax import lax
from jax.experimental import pallas as pl
from jax.experimental.pallas import tpu as pltpu
from jax.sharding import PartitionSpec as P

C = 384
FF = 1536
C2 = 768
KS = 7
BIG_IMG = 2
SMALL_IMG = 6

KEEP_RATE = 0.9
MOMENTUM = 0.5
AVERAGING = 0.5
EPSILON = 1e-06
RATES = (1.1, 0.4, 2.7, 1.3, 1.3)
FANS = (KS * KS, 1, C, FF, 4 * C)
UP_ROWS = FF // C


def layer_norm(values, gain_row, offset_row):
    average = jnp.mean(values, axis=-1, keepdims=True)
    centered = values - average
    variance = jnp.mean(centered * centered, axis=-1, keepdims=True)
    return centered * lax.rsqrt(variance + EPSILON) * gain_row + offset_row


def depthwise(field, kernel, precision):
    radius = KS // 2
    channels = field.shape[-1]
    return lax.conv_general_dilated(
        field,
        kernel.reshape(KS, KS, 1, channels),
        (1, 1),
        ((radius, radius), (radius, radius)),
        dimension_numbers=("NHWC", "HWIO", "NHWC"),
        feature_group_count=channels,
        precision=precision,
        preferred_element_type=jnp.float32,
    )


def to_blocks(field):
    count, side = field.shape[0], field.shape[1]
    half = side // 2
    return (
        field.reshape(count, half, 2, half, 2, C)
        .transpose(0, 1, 3, 2, 4, 5)
        .reshape(count * half * half, 4 * C)
    )


def from_blocks(flat, shape):
    count, half = shape[0], shape[1] // 2
    return flat.reshape(count, half, half, 2, 2, C).transpose(0, 1, 3, 2, 4, 5).reshape(shape)


def contract(left, right):
    return lax.dot_general(left, right, (((0,), (0,)), ((), ())), preferred_element_type=jnp.float32)


def dot_t(left, right):
    return lax.dot_general(left, right, (((1,), (1,)), ((), ())), preferred_element_type=jnp.float32)


def group_step(crops, cot, keep, kernel, values, up, down, strided):
    bias_dw, gain_one, offset_one = values[0], values[1], values[2]
    bias_up = values[3 : 3 + UP_ROWS].reshape(FF)
    bias_down, layer_scale = values[3 + UP_ROWS], values[4 + UP_ROWS]
    gain_two, offset_two = values[5 + UP_ROWS], values[6 + UP_ROWS]
    bias_out = values[7 + UP_ROWS :].reshape(C2)
    up_scale, down_scale, strided_scale = 1 / math.sqrt(C), 1 / math.sqrt(FF), 1 / math.sqrt(4 * C)
    side = crops.shape[1]
    factor = jnp.repeat(keep, side * side)[:, None]
    field = crops.astype(jnp.float32)

    def first(field_value, kernel_value, bias, gain, offset):
        conv_out = depthwise(field_value, kernel_value, None) * (1.0 / KS) + bias
        return layer_norm(conv_out, gain, offset)

    normed, first_pull = jax.vjp(first, field, kernel.astype(jnp.float32), bias_dw, gain_one, offset_one)
    rows = normed.astype(jnp.bfloat16).reshape(-1, C)
    pre_act = jnp.dot(rows, up, preferred_element_type=jnp.float32) * up_scale + bias_up
    phi_big = 0.5 * (1.0 + lax.erf(pre_act * math.sqrt(0.5)))
    density = jnp.exp(-0.5 * pre_act * pre_act) * (1.0 / math.sqrt(2.0 * math.pi))
    slope = phi_big + pre_act * density
    hidden = (pre_act * phi_big).astype(jnp.bfloat16)
    branch = jnp.dot(hidden, down, preferred_element_type=jnp.float32) * down_scale + bias_down
    mixed = field.reshape(-1, C) + layer_scale * branch * factor
    zeta, norm_pull = jax.vjp(layer_norm, mixed, gain_two, offset_two)
    blocks = to_blocks(zeta.astype(jnp.bfloat16).reshape(crops.shape))
    result = jnp.dot(blocks, strided, preferred_element_type=jnp.float32) * strided_scale + bias_out

    grad_out = cot.reshape(-1, C2)
    d_strided = contract(blocks, grad_out) * strided_scale
    d_bias_out = jnp.sum(grad_out.astype(jnp.float32), axis=0)
    d_blocks = dot_t(grad_out, strided) * strided_scale
    d_zeta = from_blocks(d_blocks.astype(jnp.bfloat16), crops.shape).reshape(-1, C)
    d_mixed, d_gain_two, d_offset_two = norm_pull(d_zeta.astype(jnp.float32))
    d_scale = jnp.sum(d_mixed * factor * branch, axis=0)
    d_branch = (d_mixed * factor * layer_scale).astype(jnp.bfloat16)
    d_bias_down = jnp.sum(d_branch.astype(jnp.float32), axis=0)
    d_down = contract(hidden, d_branch) * down_scale
    d_pre = (dot_t(d_branch, down) * down_scale * slope).astype(jnp.bfloat16)
    d_bias_up = jnp.sum(d_pre.astype(jnp.float32), axis=0)
    d_up = contract(rows, d_pre) * up_scale
    d_normed = (dot_t(d_pre, up) * up_scale).astype(jnp.bfloat16).reshape(crops.shape)
    d_field, d_kernel, d_bias_dw, d_gain_one, d_offset_one = first_pull(d_normed.astype(jnp.float32))
    d_vector = jnp.concatenate(
        [
            d_bias_dw[None],
            d_gain_one[None],
            d_offset_one[None],
            d_bias_up.reshape(UP_ROWS, C),
            d_bias_down[None],
            d_scale[None],
            d_gain_two[None],
            d_offset_two[None],
            d_bias_out.reshape(C2 // C, C),
        ]
    )
    half = side // 2
    return (
        result.reshape(-1, half, half, C2),
        d_field + d_mixed.reshape(crops.shape),
        (d_kernel, d_vector, d_up, d_down, d_strided),
    )


def plain_body(big_crops, small_crops, big_cot, small_cot, drop_mask, *state):
    masters, moments, averages = state[0::3], state[1::3], state[2::3]
    axes = (1, 1, 1, 0, 0)
    full = [
        lax.all_gather(weight.astype(jnp.bfloat16), "dp", axis=axis, tiled=True)
        for weight, axis in zip(masters, axes)
    ]
    kernel, vector, up, down, strided = full
    values = vector.astype(jnp.float32)
    sections, rank = lax.axis_size("section"), lax.axis_index("section")
    micro_count = big_crops.shape[0]
    own = micro_count // sections

    def take(array):
        return lax.dynamic_slice_in_dim(array, rank * own, own, 0)

    keep = take(drop_mask).astype(jnp.float32) / KEEP_RATE
    outputs, grads, totals = [], [], None
    for crops, cot, images in ((big_crops, big_cot, BIG_IMG), (small_crops, small_cot, SMALL_IMG)):
        mine, my_cot = take(crops), take(cot)
        result, grad, parts = group_step(
            mine.reshape(-1, *crops.shape[2:]),
            my_cot.reshape(-1, *cot.shape[2:]),
            jnp.repeat(keep, images, axis=1).reshape(-1),
            kernel,
            values,
            up,
            down,
            strided,
        )
        outputs.append(result.reshape(my_cot.shape))
        grads.append(grad.reshape(mine.shape))
        totals = parts if totals is None else [a + b for a, b in zip(totals, parts)]
    pixel_total = (
        lax.axis_size("dp")
        * micro_count
        * (math.prod(big_crops.shape[1:4]) + math.prod(small_crops.shape[1:4]))
    )
    updates = []
    for position in range(5):
        gradient = lax.psum_scatter(totals[position], "dp", scatter_dimension=axes[position], tiled=True)
        gradient = lax.psum(gradient, "section")
        step_rate = RATES[position] * math.sqrt(FANS[position] / pixel_total)
        moment_next = MOMENTUM * moments[position] + gradient
        weight_next = masters[position] - step_rate * (gradient + MOMENTUM * moment_next)
        average_next = AVERAGING * averages[position] + (1.0 - AVERAGING) * weight_next
        updates += [weight_next, moment_next, average_next]
    return (*outputs, *grads, *updates)


UNIT = 4
MESH = pl.DeviceIdType.MESH
F32, BF16 = jnp.float32, jnp.bfloat16
BIG_SIDE, SMALL_SIDE = 14, 6
BIG_HALF, SMALL_HALF = 7, 3
BIG_ROWS = BIG_HALF * BIG_SIDE * 8
SMALL_ROWS = SMALL_HALF * SMALL_SIDE * 8
UNITS = 3
ROWS = BIG_ROWS + UNITS * SMALL_ROWS
HALO_BIG = (BIG_HALF + 6) * BIG_SIDE * 8
HALO_SMALL = (SMALL_HALF + 6) * SMALL_SIDE * 8
BLOCK_BIG = 7 * 32
BLOCKS = BLOCK_BIG + UNITS * 3 * 16
TILE = 304
CHUNK = C
PIECE = 48
PLANES = 4
UP_SCALE, DOWN_SCALE, STRIDED_SCALE = 1 / math.sqrt(C), 1 / math.sqrt(FF), 1 / math.sqrt(4 * C)
TAPS = KS * KS
V_BIAS_DW, V_GAIN_ONE, V_OFFSET_ONE, V_BIAS_UP = 0, 1, 2, 3
V_BIAS_DOWN, V_SCALE, V_GAIN_TWO, V_OFFSET_TWO, V_BIAS_OUT = 7, 8, 9, 10, 11


def nn(a, b):
    return jnp.dot(a, b, preferred_element_type=F32)


def rows_at(start, size):
    return pl.ds(pl.multiple_of(start, 8), size)


def one_hot(shape, target, valid=None):
    row = lax.broadcasted_iota(jnp.int32, shape, 0)
    column = lax.broadcasted_iota(jnp.int32, shape, 1)
    hit = column == target(row)
    if valid is not None:
        hit = hit & valid(row)
    return jnp.where(hit, 1.0, 0.0).astype(BF16)


def flat(value):
    return value.reshape(-1, value.shape[-1])


def step_kernel(
    big_hbm, small_hbm, big_cot_hbm, small_cot_hbm, keep_ref, kernel_ref, vector_ref, up_shard, down_shard, strided_shard,
    out_big_ref, out_small_ref, grad_big_ref, grad_small_ref, kv_out, up_out, down_out, strided_out,
    xb_raw, xs_raw, gb_raw, gs_raw, halo_big, halo_small, taps, vec, conv, rstd_one, normed,
    hidden, slope, branch, xhat, rstd_two, zeta, blocks, g_wide, g_rows, d_zeta, d_mixed, d_branch, d_pre, d_normed,
    dhalo_big, dhalo_small, d_taps, d_vec, d_bias_up,
    kv_all, up_all, down_all, strided_all, d_up, d_down, d_strided,
    up_core, down_core, strided_core, up_plane, down_plane, strided_plane, up_line, down_line, strided_line,
    up_sum, down_sum, strided_sum, d_kv, kv_core, kv_plane, kv_line, kv_sum, kv_turn,
    sems, send_sems, recv_sems,
):
    pad_big = branch.at[0:896]
    rank, dp_rank = lax.axis_index("section"), lax.axis_index("dp")
    line, core = dp_rank // 2, lax.rem(dp_rank, 2)
    flanks = (rank + 1 - 2 * lax.rem(rank, 2), rank + 2 - 4 * (rank // 2), 3 - rank)
    twin = {"section": rank, "dp": dp_rank + 1 - 2 * core}

    def ahead(offset):
        return lax.rem(line + offset, PLANES)

    def on_line(offset):
        return {"section": rank, "dp": ahead(offset) * 2 + core}

    def on_plane(index):
        return {"section": flanks[index], "dp": dp_rank}

    barrier = pltpu.get_barrier_semaphore()
    for target in [twin] + [on_plane(index) for index in range(3)] + [on_line(offset) for offset in (1, 2, 3)]:
        pl.semaphore_signal(barrier, inc=1, device_id=target, device_id_type=MESH)

    pending = []

    def send(source, target_ref, target):
        index = len(pending)
        copy = pltpu.make_async_remote_copy(
            source, target_ref, send_sems.at[index], recv_sems.at[index], device_id=target, device_id_type=MESH
        )
        copy.start()
        pending.append(copy)
        return copy

    def arrived(copies):
        for copy in copies:
            copy.wait_recv()

    def piece(index):
        return pl.ds(pl.multiple_of(index * PIECE, 16), PIECE)

    def gather_line(ref, whole=False):
        part = ref.at[line, core] if whole else ref.at[line, core, piece(rank)]
        return [send(part, part, on_line(offset)) for offset in (1, 2, 3)]

    def gather_plane(ref, copies):
        result = []
        for offset, copy in zip((1, 2, 3), copies):
            copy.wait_recv()
            part = ref.at[ahead(PLANES - offset), core, piece(rank)]
            result += [send(part, part, on_plane(index)) for index in range(3)]
        return result

    def gather_core(ref, copies):
        arrived(copies)
        part = ref.at[:, core]
        return [send(part, part, twin)]

    def reduce_core(partial, landing):
        return [send(partial.at[:, 1 - core], landing, twin)]

    def reduce_plane(partial, landing, plane, copies):
        arrived(copies)
        for index in range(PLANES):
            landing[index] = (landing[index].astype(F32) + partial[index, core].astype(F32)).astype(BF16)
        return [
            send(landing.at[:, piece(flanks[index])], plane.at[index], on_plane(index)) for index in range(3)
        ]

    def reduce_line(landing, plane, ways, copies):
        arrived(copies)
        result = []
        for offset in (1, 2, 3, 0):
            index = ahead(offset)
            total = landing[index, piece(rank)].astype(F32)
            for source in range(3):
                total = total + plane[source, index].astype(F32)
            if offset:
                ways[offset - 1] = total.astype(BF16)
                result.append(send(ways.at[offset - 1], ways.at[2 + offset], on_line(offset)))
            else:
                ways[6] = total.astype(BF16)
        return result

    def reduce_back(ways, final, copies):
        arrived(copies)
        total = ways[6].astype(F32)
        for offset in (1, 2, 3):
            total = total + ways[2 + offset].astype(F32)
        final[piece(rank), :] = total.astype(BF16)
        part = final.at[piece(rank)]
        return [send(part, part, on_plane(index)) for index in range(3)]

    up_all[line, core] = up_shard[...].astype(BF16)
    down_all[line, core] = down_shard[...].astype(BF16)
    strided_all[line, core] = strided_shard[...].astype(BF16)
    put_taps = one_hot((TAPS, 128), lambda r: r)
    put_vector = one_hot((13, 128), lambda r: r + 64)
    kv_all[line, core] = (
        nn(kernel_ref[...].astype(BF16), put_taps)
        + lax.dot_general(
            vector_ref[...].astype(BF16), put_vector, (((0,), (0,)), ((), ())), preferred_element_type=F32
        )
    ).astype(BF16)
    pl.semaphore_wait(barrier, 7)
    kv_way = gather_line(kv_all, True)
    up_way = gather_line(up_all)
    down_way = gather_line(down_all)
    strided_way = gather_line(strided_all)

    own = pl.ds(rank * 2, 2)
    copies = [
        pltpu.make_async_copy(source, target, sems.at[index])
        for index, (source, target) in enumerate(
            (
                (big_hbm.at[own], xb_raw),
                (small_hbm, xs_raw),
                (big_cot_hbm.at[own], gb_raw),
                (small_cot_hbm, gs_raw),
            )
        )
    ]
    for copy in copies:
        copy.start()

    spread_big = one_hot((112, 128), lambda r: ((r >> 1) & 3) * 32 + (r >> 3) * 2 + (r & 1))
    spread_small = one_hot((48, 192), lambda r: ((r >> 1) & 3) * 48 + (r >> 3) * 8 + 2 * rank + (r & 1))
    gather_big = one_hot((128, 112), lambda r: ((r >> 1) & 15) * 8 + (r >> 5) * 2 + (r & 1))
    gather_small = one_hot((64, 48), lambda r: ((r >> 1) & 7) * 8 + (r >> 4) * 2 + (r & 1))
    block_big = one_hot(
        (128, 112), lambda r: (((r >> 1) & 7) * 2 + ((r >> 5) & 1)) * 8 + (r >> 6) * 4 + ((r >> 4) & 1) * 2 + (r & 1)
    )
    block_small = one_hot(
        (64, 48), lambda r: (((r >> 1) & 3) * 2 + ((r >> 4) & 1)) * 8 + (r >> 5) * 4 + ((r >> 3) & 1) * 2 + (r & 1)
    )
    pick_small = one_hot(
        (16, 48), lambda r: (r >> 3) * 24 + ((r >> 1) & 3) * 8 + 2 * rank + (r & 1), lambda r: (r & 7) < 6
    )
    sub = lax.broadcasted_iota(jnp.int32, (8, 128), 0)
    top = jnp.where(sub < 4, 1.0, 0.0).astype(F32)
    bottom = 1.0 - top

    def vector_row(index):
        return vec[index : index + 1, :]

    keep_zero = keep_ref[0, 0].astype(F32) / KEEP_RATE
    keep_one = keep_ref[1, 0].astype(F32) / KEEP_RATE
    lane_wide = lambda value: jnp.concatenate([value] * 3, axis=1)
    big_factor = lane_wide(jnp.where((sub & 2) == 0, keep_zero, keep_one))
    small_factor = lane_wide(jnp.where((sub & 1) == 0, keep_zero, keep_one))

    pad_big[...] = jnp.zeros_like(pad_big)
    g_wide[...] = jnp.zeros_like(g_wide)

    for copy in copies:
        copy.wait()

    for micro in range(2):
        def put_big(h, _):
            pad_big[rows_at((micro * 14 + h) * 32, 28), :] = xb_raw[micro, h].astype(F32).reshape(28, C)
            return 0

        lax.fori_loop(0, 14, put_big, 0)
        for p in range(7):
            start = p * 32 + micro * 16
            g_wide[start : start + 14, :] = gb_raw[micro, p].astype(F32).reshape(14, C2)
    for unit in range(UNITS):
        for p in range(3):
            source = jnp.concatenate(
                [gs_raw[2 * unit + crop, p].astype(F32).reshape(24, C2) for crop in range(2)], axis=0
            )
            start = BLOCK_BIG + (unit * 3 + p) * 16
            g_wide[start : start + 16, :] = nn(pick_small, source.astype(BF16))

    def spread_rows(hh, _):
        tiles = [pad_big[rows_at((micro * 14 + half * 7 + hh) * 32, 32), :] for half in range(2) for micro in range(2)]
        source = jnp.concatenate(tiles, axis=0).astype(BF16)
        halo_big[rows_at((hh + 3) * 112, 112), :] = nn(spread_big, source)
        return 0

    lax.fori_loop(0, BIG_HALF, spread_rows, 0)
    for unit in range(UNITS):
        def spread_unit(hh, _):
            tiles = [
                xs_raw[2 * unit + crop, half * 3 + hh].reshape(48, C) for half in range(2) for crop in range(2)
            ]
            source = jnp.concatenate(tiles, axis=0)
            halo_small[rows_at(unit * HALO_SMALL + (hh + 3) * 48, 48), :] = nn(spread_small, source)
            return 0

        lax.fori_loop(0, SMALL_HALF, spread_unit, 0)

    def halos(ref, base, half, side):
        def step(index, _):
            for lane in range(3):
                lanes = slice(lane * 128, lane * 128 + 128)
                low = ref[rows_at(base + (3 * side + index) * 8, 8), lanes]
                ref[rows_at(base + ((3 + half) * side + index) * 8, 8), lanes] = pltpu.roll(low, 4, 0) * top
                high = ref[rows_at(base + (half * side + index) * 8, 8), lanes]
                ref[rows_at(base + index * 8, 8), lanes] = pltpu.roll(high, 4, 0) * bottom
            return 0

        lax.fori_loop(0, 3 * side, step, 0)

    def all_halos(big, small):
        halos(big, 0, BIG_HALF, BIG_SIDE)
        for unit in range(UNITS):
            halos(small, unit * HALO_SMALL, SMALL_HALF, SMALL_SIDE)

    all_halos(halo_big, halo_small)

    kv_way = gather_core(kv_all, kv_way)
    arrived(kv_way)
    kv = jnp.transpose(flat(kv_all[...]).astype(F32))
    vec[...] = kv[64:80]
    for tap in range(TAPS):
        taps[tap] = jnp.broadcast_to(kv[tap : tap + 1] * (1.0 / KS), (8, C))

    def convolve(big, small, mirrored, finish, between):
        def tap_at(i, j, lanes):
            index = i * KS + j
            return taps[TAPS - 1 - index if mirrored else index, :, lanes]

        def row(step, _):
            h, lane = step // 3, lax.rem(step, 3)
            lanes = pl.ds(pl.multiple_of(lane * 128, 128), 128)
            sums = [None] * BIG_SIDE
            for i in range(KS):
                values = [big[rows_at(((h + i) * BIG_SIDE + w) * 8, 8), lanes] for w in range(BIG_SIDE)]
                for j in range(KS):
                    weight = tap_at(i, j, lanes)
                    for w in range(max(0, 3 - j), min(BIG_SIDE, BIG_SIDE + 3 - j)):
                        term = values[w + j - 3] * weight
                        sums[w] = term if sums[w] is None else sums[w] + term
            for w in range(BIG_SIDE):
                finish((h * BIG_SIDE + w) * 8, sums[w], lanes)
            return 0

        lax.fori_loop(0, BIG_HALF * 3, row, 0)
        between()

        def small_row(step, _):
            h, lane = step // 3, lax.rem(step, 3)
            lanes = pl.ds(pl.multiple_of(lane * 128, 128), 128)
            sums = [[None] * SMALL_SIDE for _ in range(UNITS)]
            for i in range(KS):
                values = [
                    [
                        small[rows_at(unit * HALO_SMALL + ((h + i) * SMALL_SIDE + w) * 8, 8), lanes]
                        for w in range(SMALL_SIDE)
                    ]
                    for unit in range(UNITS)
                ]
                for j in range(KS):
                    weight = tap_at(i, j, lanes)
                    for w in range(max(0, 3 - j), min(SMALL_SIDE, SMALL_SIDE + 3 - j)):
                        for unit in range(UNITS):
                            term = values[unit][w + j - 3] * weight
                            old = sums[unit][w]
                            sums[unit][w] = term if old is None else old + term
            for unit in range(UNITS):
                for w in range(SMALL_SIDE):
                    finish(BIG_ROWS + unit * SMALL_ROWS + (h * SMALL_SIDE + w) * 8, sums[unit][w], lanes)
            return 0

        lax.fori_loop(0, SMALL_HALF * 3, small_row, 0)

    def keep_conv(start, value, lanes):
        conv[rows_at(start, 8), lanes] = value

    ways = {}
    up_way = gather_plane(up_all, up_way)
    ways["down"] = down_way
    ways["strided"] = strided_way

    def weights_on():
        ways["down"] = gather_plane(down_all, ways["down"])
        ways["strided"] = gather_plane(strided_all, ways["strided"])
        ways["up"] = gather_core(up_all, up_way)

    convolve(halo_big, halo_small, False, keep_conv, weights_on)

    def for_tiles(run):
        def big_tile(index, _):
            run(index * 112, 112, big_factor, halo_big, dhalo_big, 336 + index * 112)
            return 0

        lax.fori_loop(0, BIG_HALF, big_tile, 0)

        def small_tile(index, _):
            run(BIG_ROWS + index * 144, 144, small_factor, halo_small, dhalo_small, index * HALO_SMALL + 144)
            return 0

        lax.fori_loop(0, UNITS, small_tile, 0)

    def fold(value):
        return jnp.sum(value.reshape(-1, 8, value.shape[-1]), axis=0)

    def mean_of(value):
        return jnp.sum(value, axis=-1, keepdims=True) * (1.0 / C)

    def wide(ref, rows):
        value = ref[rows, :]
        return jnp.concatenate([value, value, value], axis=1)

    def norm_one(start, size, *_):
        rows = rows_at(start, size)
        value = conv[rows, :] + vector_row(V_BIAS_DW)
        centered = value - mean_of(value)
        scale = lax.rsqrt(mean_of(centered * centered) + EPSILON)
        unit = centered * scale
        conv[rows, :] = unit
        rstd_one[rows, :] = jnp.broadcast_to(scale, (size, 128))
        normed[pl.ds(pl.multiple_of(start, 16), size), :] = (
            unit * vector_row(V_GAIN_ONE) + vector_row(V_OFFSET_ONE)
        ).astype(BF16)

    for_tiles(norm_one)

    def up_tile(index, _):
        rows = pl.ds(pl.multiple_of(index * TILE, 16), TILE)
        left = normed[rows, :]
        for chunk in range(FF // CHUNK):
            span = slice(chunk * CHUNK, (chunk + 1) * CHUNK)
            bias = vector_row(V_BIAS_UP + chunk)
            pre = (
                lax.dot_general(left, flat(up_all[chunk]), (((1,), (1,)), ((), ())), preferred_element_type=F32)
                * UP_SCALE
                + bias
            )
            whole = 0.5 + 0.5 * lax.erf(pre * math.sqrt(0.5))
            density = jnp.exp(pre * pre * -0.5) * (1.0 / math.sqrt(2.0 * math.pi))
            hidden[rows, span] = (pre * whole).astype(BF16)
            slope[rows, span] = whole + pre * density
        return 0

    arrived(ways["up"])
    lax.fori_loop(0, ROWS // TILE, up_tile, 0)
    ways["down"] = gather_core(down_all, ways["down"])
    arrived(ways["down"])

    def branch_tile(index, _):
        rows = pl.ds(pl.multiple_of(index * TILE, 16), TILE)
        branch[rows, :] = nn(hidden[rows, :], flat(down_all[...])) * DOWN_SCALE + vector_row(V_BIAS_DOWN)
        return 0

    lax.fori_loop(0, ROWS // TILE, branch_tile, 0)
    ways["strided"] = gather_core(strided_all, ways["strided"])

    def scaled(value, factor):
        return (value.reshape(-1, 8, C) * factor[None]).reshape(-1, C)

    def norm_two(start, size, factor, field, _, offset):
        rows = rows_at(start, size)
        value = field[rows_at(offset, size), :] + scaled(vector_row(V_SCALE) * branch[rows, :], factor)
        centered = value - mean_of(value)
        scale = lax.rsqrt(mean_of(centered * centered) + EPSILON)
        unit = centered * scale
        xhat[rows, :] = unit
        rstd_two[rows, :] = jnp.broadcast_to(scale, (size, 128))
        zeta[pl.ds(pl.multiple_of(start, 16), size), :] = (
            unit * vector_row(V_GAIN_TWO) + vector_row(V_OFFSET_TWO)
        ).astype(BF16)

    for_tiles(norm_two)

    def block_spans(base, count, hh, half_side):
        for half in range(2):
            h = half * half_side + hh
            p, a = h // 2, lax.rem(h, 2)
            for b in range(2):
                yield (
                    pl.ds(pl.multiple_of(base + p * count, 16), count),
                    pl.ds(pl.multiple_of((2 * a + b) * C, 128), C),
                )

    def block_rows(source, matrix, base, count, hh, half_side):
        picked = nn(matrix, source).astype(BF16)
        for index, span in enumerate(block_spans(base, count, hh, half_side)):
            blocks[span] = picked[index * count : (index + 1) * count]

    def big_blocks(hh, _):
        block_rows(zeta[pl.ds(pl.multiple_of(hh * 112, 16), 112), :], block_big, 0, 32, hh, 7)
        return 0

    lax.fori_loop(0, BIG_HALF, big_blocks, 0)
    for unit in range(UNITS):
        def small_blocks(hh, _):
            source = zeta[pl.ds(pl.multiple_of(BIG_ROWS + unit * SMALL_ROWS + hh * 48, 16), 48), :]
            block_rows(source, block_small, BLOCK_BIG + unit * 48, 16, hh, 3)
            return 0

        lax.fori_loop(0, SMALL_HALF, small_blocks, 0)

    g_rows[...] = g_wide[...].astype(BF16)
    bias_out_grad = jnp.sum(g_wide[...], axis=0, keepdims=True)
    d_vec[V_BIAS_OUT, 0:1, :] = bias_out_grad[:, :C]
    d_vec[V_BIAS_OUT + 1, 0:1, :] = bias_out_grad[:, C:]

    def strided_grad(index, _):
        span = pl.ds(pl.multiple_of(index * C, 128), C)
        d_strided[index] = (
            (
                lax.dot_general(blocks[:, span], g_rows[...], (((0,), (0,)), ((), ())), preferred_element_type=F32)
                * STRIDED_SCALE
            )
            .astype(BF16)
            .reshape(2, 192, C2)
        )
        return 0

    lax.fori_loop(0, 4, strided_grad, 0)
    ways["d_strided"] = reduce_core(d_strided, strided_core)
    arrived(ways["strided"])

    bias_out = jnp.concatenate([vector_row(V_BIAS_OUT), vector_row(V_BIAS_OUT + 1)], axis=1)

    for chunk in range(3):
        span = slice(chunk * 256, chunk * 256 + 256)
        g_wide[:, span] = nn(blocks[...], flat(strided_all[:, :, :, span])) * STRIDED_SCALE + bias_out[:, span]
    for micro in range(2):
        for p in range(7):
            start = p * 32 + micro * 16
            out_big_ref[micro, p] = g_wide[start : start + 14, :].reshape(7, 2, C2)
    for unit in range(UNITS):
        for p in range(3):
            for crop in range(2):
                start = BLOCK_BIG + (unit * 3 + p) * 16 + crop * 8
                out_small_ref[2 * unit + crop, p] = g_wide[start : start + 6, :].reshape(3, 2, C2)

    def block_grad(index, _):
        span = pl.ds(pl.multiple_of(index * 384, 128), 384)
        blocks[:, span] = (
            lax.dot_general(
                g_rows[...], flat(strided_all[index]), (((1,), (1,)), ((), ())), preferred_element_type=F32
            )
            * STRIDED_SCALE
        ).astype(BF16)
        return 0

    lax.fori_loop(0, 4, block_grad, 0)

    def unblock(matrix, base, count, hh, half_side):
        parts = jnp.concatenate([blocks[span] for span in block_spans(base, count, hh, half_side)], axis=0)
        return lax.dot_general(matrix, parts, (((0,), (0,)), ((), ())), preferred_element_type=F32)

    def big_unblock(hh, _):
        d_zeta[rows_at(hh * 112, 112), :] = unblock(block_big, 0, 32, hh, 7)
        return 0

    lax.fori_loop(0, BIG_HALF, big_unblock, 0)
    for unit in range(UNITS):
        def small_unblock(hh, _):
            d_zeta[rows_at(BIG_ROWS + unit * SMALL_ROWS + hh * 48, 48), :] = unblock(
                block_small, BLOCK_BIG + unit * 48, 16, hh, 3
            )
            return 0

        lax.fori_loop(0, SMALL_HALF, small_unblock, 0)

    ways["d_strided"] = reduce_plane(d_strided, strided_core, strided_plane, ways["d_strided"])

    for index in range(11):
        d_vec[index] = jnp.zeros((8, C), F32)

    def norm_two_back(start, size, factor, *_):
        rows = rows_at(start, size)
        unit = xhat[rows, :]
        grad = d_zeta[rows, :]
        d_vec[V_GAIN_TWO] += fold(grad * unit)
        d_vec[V_OFFSET_TWO] += fold(grad)
        inner = grad * vector_row(V_GAIN_TWO)
        mixed = (inner - mean_of(inner) - unit * mean_of(inner * unit)) * wide(rstd_two, rows)
        d_mixed[rows, :] = mixed
        kept = scaled(mixed, factor)
        d_vec[V_SCALE] += fold(kept * branch[rows, :])
        lowered = (kept * vector_row(V_SCALE)).astype(BF16)
        d_branch[pl.ds(pl.multiple_of(start, 16), size), :] = lowered
        d_vec[V_BIAS_DOWN] += fold(lowered.astype(F32))

    for_tiles(norm_two_back)

    d_bias_up[...] = jnp.zeros_like(d_bias_up)

    def down_tile(index, _):
        rows = pl.ds(pl.multiple_of(index * TILE, 16), TILE)
        left = d_branch[rows, :]
        for chunk in range(FF // CHUNK):
            span = slice(chunk * CHUNK, (chunk + 1) * CHUNK)
            d_hidden = (
                lax.dot_general(left, flat(down_all[chunk]), (((1,), (1,)), ((), ())), preferred_element_type=F32)
                * DOWN_SCALE
            )
            lowered = (d_hidden * slope[rows, span]).astype(BF16)
            d_pre[rows, span] = lowered
            d_bias_up[:, span] += fold(lowered.astype(F32))
        d_normed[rows, :] = (nn(d_pre[rows, :], flat(up_all[...])) * UP_SCALE).astype(BF16)
        return 0

    lax.fori_loop(0, ROWS // TILE, down_tile, 0)

    def outer(left, right, scale):
        product = lax.dot_general(left, right, (((0,), (0,)), ((), ())), preferred_element_type=F32)
        return (product * scale).astype(BF16).reshape(2, 192, C)

    def down_grad(index, _):
        span = pl.ds(pl.multiple_of(index * C, 128), C)
        d_down[index] = outer(hidden[:, span], d_branch[...], DOWN_SCALE)
        return 0

    def up_grad(index, _):
        span = pl.ds(pl.multiple_of(index * C, 128), C)
        d_up[index] = outer(d_pre[:, span], normed[...], UP_SCALE)
        return 0

    lax.fori_loop(0, 4, down_grad, 0)
    ways["d_down"] = reduce_core(d_down, down_core)
    lax.fori_loop(0, 4, up_grad, 0)
    ways["d_up"] = reduce_core(d_up, up_core)
    ways["d_down"] = reduce_plane(d_down, down_core, down_plane, ways["d_down"])

    def norm_one_back(start, size, _, __, target, offset):
        rows = rows_at(start, size)
        unit = conv[rows, :]
        grad = d_normed[pl.ds(pl.multiple_of(start, 16), size), :].astype(F32)
        d_vec[V_GAIN_ONE] += fold(grad * unit)
        d_vec[V_OFFSET_ONE] += fold(grad)
        inner = grad * vector_row(V_GAIN_ONE)
        result = (inner - mean_of(inner) - unit * mean_of(inner * unit)) * wide(rstd_one, rows)
        d_vec[V_BIAS_DW] += fold(result)
        target[rows_at(offset, size), :] = result

    for_tiles(norm_one_back)
    ways["d_up"] = reduce_plane(d_up, up_core, up_plane, ways["d_up"])
    ways["d_strided"] = reduce_line(strided_core, strided_plane, strided_line, ways["d_strided"])
    all_halos(dhalo_big, dhalo_small)

    def tap_grads(step, _):
        i, lane = step // 3, lax.rem(step, 3)
        lanes = pl.ds(pl.multiple_of(lane * 128, 128), 128)

        def image_row(side, field, grad, field_base, grad_base, sums):
            inputs = [field[rows_at(field_base + w * 8, 8), lanes] for w in range(side)]
            outer = [grad[rows_at(grad_base + w * 8, 8), lanes] for w in range(side)]
            result = []
            for j in range(KS):
                total = sums[j]
                for w in range(max(0, 3 - j), min(side, side + 3 - j)):
                    total = total + inputs[w + j - 3] * outer[w]
                result.append(total)
            return tuple(result)

        sums = tuple(jnp.zeros((8, 128), F32) for _ in range(KS))
        sums = lax.fori_loop(
            0,
            BIG_HALF,
            lambda h, carry: image_row(
                BIG_SIDE, halo_big, dhalo_big, (h + i) * 112, (h + 3) * 112, carry
            ),
            sums,
        )
        for unit in range(UNITS):
            sums = lax.fori_loop(
                0,
                SMALL_HALF,
                lambda h, carry, base=unit * HALO_SMALL: image_row(
                    SMALL_SIDE, halo_small, dhalo_small, base + (h + i) * 48, base + (h + 3) * 48, carry
                ),
                sums,
            )
        for j in range(KS):
            d_taps[i * KS + j, :, lanes] = sums[j]
        return 0

    lax.fori_loop(0, KS * 3, tap_grads, 0)

    d_kv[56:64, :] = jnp.zeros((8, C), F32)
    for tap in range(TAPS):
        d_kv[tap : tap + 1, :] = jnp.sum(d_taps[tap], axis=0, keepdims=True) * (1.0 / KS)
    for index in range(11):
        if V_BIAS_UP <= index < V_BIAS_UP + UP_ROWS:
            continue
        d_kv[TAPS + index : TAPS + index + 1, :] = jnp.sum(d_vec[index], axis=0, keepdims=True)
    d_kv[TAPS + V_BIAS_OUT : TAPS + V_BIAS_OUT + 1, :] = d_vec[V_BIAS_OUT, 0:1, :]
    d_kv[TAPS + V_BIAS_OUT + 1 : TAPS + V_BIAS_OUT + 2, :] = d_vec[V_BIAS_OUT + 1, 0:1, :]
    bias_up_grad = jnp.sum(d_bias_up[...], axis=0, keepdims=True)
    for index in range(UP_ROWS):
        d_kv[TAPS + V_BIAS_UP + index : TAPS + V_BIAS_UP + index + 1, :] = bias_up_grad[
            :, index * C : (index + 1) * C
        ]

    ways["d_kv"] = [send(d_kv, kv_core, twin)]

    def kv_rows(index):
        return pl.ds(pl.multiple_of(index * 16, 16), 16)

    def kv_reduce_plane(copies):
        arrived(copies)
        kv_core[...] += d_kv[...]
        return [send(kv_core.at[kv_rows(flanks[index])], kv_plane.at[index], on_plane(index)) for index in range(3)]

    def kv_reduce_line(copies):
        arrived(copies)
        kv_line[0] = kv_core[kv_rows(rank), :] + kv_plane[0] + kv_plane[1] + kv_plane[2]
        return [send(kv_line.at[0], kv_line.at[offset], on_line(offset)) for offset in (1, 2, 3)]

    def kv_reduce_back(copies):
        arrived(copies)
        total = jnp.zeros((16, C), F32)
        for index in range(PLANES):
            total = total + kv_line[lax.rem(line - index + PLANES, PLANES)]
        kv_sum[kv_rows(rank), :] = total
        part = kv_sum.at[kv_rows(rank)]
        return [send(part, part, on_plane(index)) for index in range(3)]

    def add_grad(start, value, lanes):
        d_mixed[rows_at(start, 8), lanes] += value

    def gradients_on():
        ways["d_kv"] = kv_reduce_plane(ways["d_kv"])
        ways["d_down"] = reduce_line(down_core, down_plane, down_line, ways["d_down"])
        ways["d_strided"] = reduce_back(strided_line, strided_sum, ways["d_strided"])

    convolve(dhalo_big, dhalo_small, True, add_grad, gradients_on)
    ways["d_kv"] = kv_reduce_line(ways["d_kv"])
    ways["d_up"] = reduce_line(up_core, up_plane, up_line, ways["d_up"])
    ways["d_down"] = reduce_back(down_line, down_sum, ways["d_down"])

    def restore(matrix, value):
        high = value.astype(BF16)
        low = (value - high.astype(F32)).astype(BF16)
        return nn(matrix, high) + nn(matrix, low)

    def grad_rows(hh, _):
        natural = restore(gather_big, d_mixed[rows_at(hh * 112, 112), :])
        for half in range(2):
            for micro in range(2):
                start = (half * 2 + micro) * 32
                grad_big_ref[micro, half * 7 + hh] = natural[start : start + 28].reshape(14, 2, C)
        return 0

    lax.fori_loop(0, BIG_HALF, grad_rows, 0)
    for unit in range(UNITS):
        def small_grad_rows(hh, _):
            natural = restore(gather_small, d_mixed[rows_at(BIG_ROWS + unit * SMALL_ROWS + hh * 48, 48), :])
            for half in range(2):
                for crop in range(2):
                    start = (half * 2 + crop) * 16
                    grad_small_ref[2 * unit + crop, half * 3 + hh] = natural[start : start + 12].reshape(6, 2, C)
            return 0

        lax.fori_loop(0, SMALL_HALF, small_grad_rows, 0)

    ways["d_kv"] = kv_reduce_back(ways["d_kv"])
    ways["d_up"] = reduce_back(up_line, up_sum, ways["d_up"])
    for name, final, target in (
        ("d_strided", strided_sum, strided_out),
        ("d_down", down_sum, down_out),
        ("d_up", up_sum, up_out),
    ):
        arrived(ways[name])
        target[...] = final[...]
    arrived(ways["d_kv"])
    kv_turn[...] = jnp.transpose(kv_sum[...])
    kv_out[...] = kv_turn[pl.ds(pl.multiple_of(dp_rank * PIECE, 16), PIECE), :]
    for copy in pending:
        copy.wait_send()


def fused_step(big_crops, small_crops, big_cot, small_cot, keep, kernel_t, vector, up_t, down, strided):
    any_spec = pl.BlockSpec(memory_space=pl.ANY)
    vmem = pl.BlockSpec(memory_space=pltpu.VMEM)
    shape = jax.ShapeDtypeStruct
    big_order, small_order = (0, 2, 3, 1, 4), (1, 2, 3, 0, 4)
    results = pl.pallas_call(
        step_kernel,
        out_shape=(
            shape((2, 7, 7, 2, C2), F32),
            shape((6, 3, 3, 2, C2), F32),
            shape((2, 14, 14, 2, C), F32),
            shape((6, 6, 6, 2, C), F32),
            shape((PIECE, 64), F32),
            shape((192, C), BF16),
            shape((192, C), BF16),
            shape((192, C2), BF16),
        ),
        in_specs=[any_spec] * 4 + [pl.BlockSpec(memory_space=pltpu.SMEM)] + [vmem] * 5,
        out_specs=[vmem] * 8,
        scratch_shapes=[
            pltpu.VMEM((2, 14, 14, 2, C), BF16),
            pltpu.VMEM((6, 6, 6, 8, C), BF16),
            pltpu.VMEM((2, 7, 7, 2, C2), BF16),
            pltpu.VMEM((6, 3, 3, 8, C2), BF16),
            pltpu.VMEM((HALO_BIG, C), F32),
            pltpu.VMEM((UNITS * HALO_SMALL, C), F32),
            pltpu.VMEM((TAPS, 8, C), F32),
            pltpu.VMEM((16, C), F32),
            pltpu.VMEM((ROWS, C), F32),
            pltpu.VMEM((ROWS, 128), F32),
            pltpu.VMEM((ROWS, C), BF16),
            pltpu.VMEM((ROWS, FF), BF16),
            pltpu.VMEM((ROWS, FF), F32),
            pltpu.VMEM((ROWS, C), F32),
            pltpu.VMEM((ROWS, C), F32),
            pltpu.VMEM((ROWS, 128), F32),
            pltpu.VMEM((ROWS, C), BF16),
            pltpu.VMEM((BLOCKS, 4 * C), BF16),
            pltpu.VMEM((BLOCKS, C2), F32),
            pltpu.VMEM((BLOCKS, C2), BF16),
            pltpu.VMEM((ROWS, C), F32),
            pltpu.VMEM((ROWS, C), F32),
            pltpu.VMEM((ROWS, C), BF16),
            pltpu.VMEM((ROWS, FF), BF16),
            pltpu.VMEM((ROWS, C), BF16),
            pltpu.VMEM((HALO_BIG, C), F32),
            pltpu.VMEM((UNITS * HALO_SMALL, C), F32),
            pltpu.VMEM((TAPS, 8, C), F32),
            pltpu.VMEM((13, 8, C), F32),
            pltpu.VMEM((8, FF), F32),
            pltpu.VMEM((4, 2, 48, 128), BF16),
            pltpu.VMEM((4, 2, 192, C), BF16),
            pltpu.VMEM((4, 2, 192, C), BF16),
            pltpu.VMEM((4, 2, 192, C2), BF16),
            pltpu.VMEM((4, 2, 192, C), BF16),
            pltpu.VMEM((4, 2, 192, C), BF16),
            pltpu.VMEM((4, 2, 192, C2), BF16),
            pltpu.VMEM((4, 192, C), BF16),
            pltpu.VMEM((4, 192, C), BF16),
            pltpu.VMEM((4, 192, C2), BF16),
            pltpu.VMEM((3, 4, PIECE, C), BF16),
            pltpu.VMEM((3, 4, PIECE, C), BF16),
            pltpu.VMEM((3, 4, PIECE, C2), BF16),
            pltpu.VMEM((7, PIECE, C), BF16),
            pltpu.VMEM((7, PIECE, C), BF16),
            pltpu.VMEM((7, PIECE, C2), BF16),
            pltpu.VMEM((192, C), BF16),
            pltpu.VMEM((192, C), BF16),
            pltpu.VMEM((192, C2), BF16),
            pltpu.VMEM((64, C), F32),
            pltpu.VMEM((64, C), F32),
            pltpu.VMEM((3, 16, C), F32),
            pltpu.VMEM((4, 16, C), F32),
            pltpu.VMEM((64, C), F32),
            pltpu.VMEM((C, 64), F32),
            pltpu.SemaphoreType.DMA((4,)),
            pltpu.SemaphoreType.DMA((83,)),
            pltpu.SemaphoreType.DMA((83,)),
        ],
        compiler_params=pltpu.CompilerParams(vmem_limit_bytes=(63 << 20) + (1 << 19), collective_id=0, has_side_effects=True),
    )(
        big_crops.transpose(big_order),
        small_crops.transpose(small_order),
        big_cot.transpose(big_order),
        small_cot.transpose(small_order),
        keep,
        kernel_t,
        vector,
        up_t,
        down,
        strided,
    )
    back_big, back_small = (0, 3, 1, 2, 4), (3, 0, 1, 2, 4)
    return (
        results[0].transpose(back_big),
        results[1].transpose(back_small),
        results[2].transpose(back_big),
        results[3].transpose(back_small),
        *results[4:],
    )


def body(big_crops, small_crops, big_cot, small_cot, drop_mask, *state):
    sections, rank = lax.axis_size("section"), lax.axis_index("section")
    micro_count = big_crops.shape[0]
    fits = (
        micro_count == 2 * sections
        and big_crops.shape[1:] == (BIG_IMG, BIG_SIDE, BIG_SIDE, C)
        and small_crops.shape[1:] == (SMALL_IMG, SMALL_SIDE, SMALL_SIDE, C)
        and drop_mask.shape[1] == 1
        and (sections, lax.axis_size("dp")) == (4, 8)
    )
    if not fits:
        return plain_body(big_crops, small_crops, big_cot, small_cot, drop_mask, *state)
    masters, moments, averages = state[0::3], state[1::3], state[2::3]
    turned = (True, False, True, False, False)
    masters, moments, averages = (
        [jnp.transpose(array) if turn else array for array, turn in zip(group, turned)]
        for group in (masters, moments, averages)
    )
    keep = lax.dynamic_slice_in_dim(drop_mask, rank * 2, 2, 0)
    out_big, out_small, grad_big, grad_small, d_kv, d_up, d_down, d_strided = fused_step(
        big_crops, small_crops, big_cot, small_cot, keep, *masters
    )
    gradients = (
        d_kv[:, :TAPS],
        jnp.transpose(d_kv[:, TAPS : TAPS + masters[1].shape[0]]),
        d_up.astype(F32),
        d_down.astype(F32),
        d_strided.astype(F32),
    )
    pixel_total = (
        lax.axis_size("dp")
        * micro_count
        * (math.prod(big_crops.shape[1:4]) + math.prod(small_crops.shape[1:4]))
    )
    updates = []
    for position in range(5):
        step_rate = RATES[position] * math.sqrt(FANS[position] / pixel_total)
        moment_next = MOMENTUM * moments[position] + gradients[position]
        weight_next = masters[position] - step_rate * (gradients[position] + MOMENTUM * moment_next)
        average_next = AVERAGING * averages[position] + (1.0 - AVERAGING) * weight_next
        new = (weight_next, moment_next, average_next)
        updates += [jnp.transpose(array) if turned[position] else array for array in new]
    return (out_big, out_small, grad_big, grad_small, *updates)


def solution(mesh):
    crops = P(None, "dp", None, None, None)
    owned = P("section", "dp", None, None, None)
    weights = (P(None, "dp"),) * 9 + (P("dp", None),) * 6
    return jax.shard_map(
        body,
        mesh=mesh,
        in_specs=(crops,) * 4 + (P(None, "dp"),) + weights,
        out_specs=(owned,) * 4 + weights,
        check_vma=False,
    )
```

```python
import functools
import math

import jax
import jax.numpy as jnp
from jax import lax
from jax.experimental import pallas as pl
from jax.experimental.pallas import tpu as pltpu
from jax.sharding import PartitionSpec as P

C = 384
FF = 1536
C2 = 768
KS = 7
BIG_IMG = 2
SMALL_IMG = 6

KEEP_RATE = 0.9
MOMENTUM = 0.5
AVERAGING = 0.5
EPSILON = 1e-06
RATES = (1.1, 0.4, 2.7, 1.3, 1.3)
FANS = (KS * KS, 1, C, FF, 4 * C)
UP_ROWS = FF // C


def layer_norm(values, gain_row, offset_row):
    average = jnp.mean(values, axis=-1, keepdims=True)
    centered = values - average
    variance = jnp.mean(centered * centered, axis=-1, keepdims=True)
    return centered * lax.rsqrt(variance + EPSILON) * gain_row + offset_row


def depthwise(field, kernel, precision):
    radius = KS // 2
    channels = field.shape[-1]
    return lax.conv_general_dilated(
        field,
        kernel.reshape(KS, KS, 1, channels),
        (1, 1),
        ((radius, radius), (radius, radius)),
        dimension_numbers=("NHWC", "HWIO", "NHWC"),
        feature_group_count=channels,
        precision=precision,
        preferred_element_type=jnp.float32,
    )


def to_blocks(field):
    count, side = field.shape[0], field.shape[1]
    half = side // 2
    return (
        field.reshape(count, half, 2, half, 2, C)
        .transpose(0, 1, 3, 2, 4, 5)
        .reshape(count * half * half, 4 * C)
    )


def from_blocks(flat, shape):
    count, half = shape[0], shape[1] // 2
    return flat.reshape(count, half, half, 2, 2, C).transpose(0, 1, 3, 2, 4, 5).reshape(shape)


def contract(left, right):
    return lax.dot_general(left, right, (((0,), (0,)), ((), ())), preferred_element_type=jnp.float32)


def dot_t(left, right):
    return lax.dot_general(left, right, (((1,), (1,)), ((), ())), preferred_element_type=jnp.float32)


def group_step(crops, cot, keep, kernel, values, up, down, strided):
    bias_dw, gain_one, offset_one = values[0], values[1], values[2]
    bias_up = values[3 : 3 + UP_ROWS].reshape(FF)
    bias_down, layer_scale = values[3 + UP_ROWS], values[4 + UP_ROWS]
    gain_two, offset_two = values[5 + UP_ROWS], values[6 + UP_ROWS]
    bias_out = values[7 + UP_ROWS :].reshape(C2)
    up_scale, down_scale, strided_scale = 1 / math.sqrt(C), 1 / math.sqrt(FF), 1 / math.sqrt(4 * C)
    side = crops.shape[1]
    factor = jnp.repeat(keep, side * side)[:, None]
    field = crops.astype(jnp.float32)

    def first(field_value, kernel_value, bias, gain, offset):
        conv_out = depthwise(field_value, kernel_value, None) * (1.0 / KS) + bias
        return layer_norm(conv_out, gain, offset)

    normed, first_pull = jax.vjp(first, field, kernel.astype(jnp.float32), bias_dw, gain_one, offset_one)
    rows = normed.astype(jnp.bfloat16).reshape(-1, C)
    pre_act = jnp.dot(rows, up, preferred_element_type=jnp.float32) * up_scale + bias_up
    phi_big = 0.5 * (1.0 + lax.erf(pre_act * math.sqrt(0.5)))
    density = jnp.exp(-0.5 * pre_act * pre_act) * (1.0 / math.sqrt(2.0 * math.pi))
    slope = phi_big + pre_act * density
    hidden = (pre_act * phi_big).astype(jnp.bfloat16)
    branch = jnp.dot(hidden, down, preferred_element_type=jnp.float32) * down_scale + bias_down
    mixed = field.reshape(-1, C) + layer_scale * branch * factor
    zeta, norm_pull = jax.vjp(layer_norm, mixed, gain_two, offset_two)
    blocks = to_blocks(zeta.astype(jnp.bfloat16).reshape(crops.shape))
    result = jnp.dot(blocks, strided, preferred_element_type=jnp.float32) * strided_scale + bias_out

    grad_out = cot.reshape(-1, C2)
    d_strided = contract(blocks, grad_out) * strided_scale
    d_bias_out = jnp.sum(grad_out.astype(jnp.float32), axis=0)
    d_blocks = dot_t(grad_out, strided) * strided_scale
    d_zeta = from_blocks(d_blocks.astype(jnp.bfloat16), crops.shape).reshape(-1, C)
    d_mixed, d_gain_two, d_offset_two = norm_pull(d_zeta.astype(jnp.float32))
    d_scale = jnp.sum(d_mixed * factor * branch, axis=0)
    d_branch = (d_mixed * factor * layer_scale).astype(jnp.bfloat16)
    d_bias_down = jnp.sum(d_branch.astype(jnp.float32), axis=0)
    d_down = contract(hidden, d_branch) * down_scale
    d_pre = (dot_t(d_branch, down) * down_scale * slope).astype(jnp.bfloat16)
    d_bias_up = jnp.sum(d_pre.astype(jnp.float32), axis=0)
    d_up = contract(rows, d_pre) * up_scale
    d_normed = (dot_t(d_pre, up) * up_scale).astype(jnp.bfloat16).reshape(crops.shape)
    d_field, d_kernel, d_bias_dw, d_gain_one, d_offset_one = first_pull(d_normed.astype(jnp.float32))
    d_vector = jnp.concatenate(
        [
            d_bias_dw[None],
            d_gain_one[None],
            d_offset_one[None],
            d_bias_up.reshape(UP_ROWS, C),
            d_bias_down[None],
            d_scale[None],
            d_gain_two[None],
            d_offset_two[None],
            d_bias_out.reshape(C2 // C, C),
        ]
    )
    half = side // 2
    return (
        result.reshape(-1, half, half, C2),
        d_field + d_mixed.reshape(crops.shape),
        (d_kernel, d_vector, d_up, d_down, d_strided),
    )


def plain_body(big_crops, small_crops, big_cot, small_cot, drop_mask, *state):
    masters, moments, averages = state[0::3], state[1::3], state[2::3]
    axes = (1, 1, 1, 0, 0)
    full = [
        lax.all_gather(weight.astype(jnp.bfloat16), "dp", axis=axis, tiled=True)
        for weight, axis in zip(masters, axes)
    ]
    kernel, vector, up, down, strided = full
    values = vector.astype(jnp.float32)
    sections, rank = lax.axis_size("section"), lax.axis_index("section")
    micro_count = big_crops.shape[0]
    own = micro_count // sections

    def take(array):
        return lax.dynamic_slice_in_dim(array, rank * own, own, 0)

    keep = take(drop_mask).astype(jnp.float32) / KEEP_RATE
    outputs, grads, totals = [], [], None
    for crops, cot, images in ((big_crops, big_cot, BIG_IMG), (small_crops, small_cot, SMALL_IMG)):
        mine, my_cot = take(crops), take(cot)
        result, grad, parts = group_step(
            mine.reshape(-1, *crops.shape[2:]),
            my_cot.reshape(-1, *cot.shape[2:]),
            jnp.repeat(keep, images, axis=1).reshape(-1),
            kernel,
            values,
            up,
            down,
            strided,
        )
        outputs.append(result.reshape(my_cot.shape))
        grads.append(grad.reshape(mine.shape))
        totals = parts if totals is None else [a + b for a, b in zip(totals, parts)]
    pixel_total = (
        lax.axis_size("dp")
        * micro_count
        * (math.prod(big_crops.shape[1:4]) + math.prod(small_crops.shape[1:4]))
    )
    updates = []
    for position in range(5):
        gradient = lax.psum_scatter(totals[position], "dp", scatter_dimension=axes[position], tiled=True)
        gradient = lax.psum(gradient, "section")
        step_rate = RATES[position] * math.sqrt(FANS[position] / pixel_total)
        moment_next = MOMENTUM * moments[position] + gradient
        weight_next = masters[position] - step_rate * (gradient + MOMENTUM * moment_next)
        average_next = AVERAGING * averages[position] + (1.0 - AVERAGING) * weight_next
        updates += [weight_next, moment_next, average_next]
    return (*outputs, *grads, *updates)


UNIT = 4
MESH = pl.DeviceIdType.MESH
F32, BF16 = jnp.float32, jnp.bfloat16
BIG_SIDE, SMALL_SIDE = 14, 6
BIG_HALF, SMALL_HALF = 7, 3
BIG_ROWS = BIG_HALF * BIG_SIDE * 8
SMALL_ROWS = SMALL_HALF * SMALL_SIDE * 8
UNITS = 3
ROWS = BIG_ROWS + UNITS * SMALL_ROWS
HALO_BIG = (BIG_HALF + 6) * BIG_SIDE * 8
HALO_SMALL = (SMALL_HALF + 6) * SMALL_SIDE * 8
BLOCK_BIG = 7 * 32
BLOCKS = BLOCK_BIG + UNITS * 3 * 16
TILE = 304
CHUNK = C
PIECE = 48
PLANES = 4
COPIES = 118
UP_SCALE, DOWN_SCALE, STRIDED_SCALE = 1 / math.sqrt(C), 1 / math.sqrt(FF), 1 / math.sqrt(4 * C)
TAPS = KS * KS
V_BIAS_DW, V_GAIN_ONE, V_OFFSET_ONE, V_BIAS_UP = 0, 1, 2, 3
V_BIAS_DOWN, V_SCALE, V_GAIN_TWO, V_OFFSET_TWO, V_BIAS_OUT = 7, 8, 9, 10, 11


def nn(a, b):
    return jnp.dot(a, b, preferred_element_type=F32)


def rows_at(start, size):
    return pl.ds(aligned(start, 8), size)


def aligned(value, factor):
    return value if isinstance(value, int) else pl.multiple_of(value, factor)


def unrolled(count, step):
    for index in range(count):
        step(index, 0)


def one_hot(shape, target, valid=None):
    row = lax.broadcasted_iota(jnp.int32, shape, 0)
    column = lax.broadcasted_iota(jnp.int32, shape, 1)
    hit = column == target(row)
    if valid is not None:
        hit = hit & valid(row)
    return jnp.where(hit, 1.0, 0.0).astype(BF16)


def flat(value):
    return value.reshape(-1, value.shape[-1])


def step_kernel(
    big_hbm, small_hbm, big_cot_hbm, small_cot_hbm, keep_ref, kernel_ref, vector_ref, up_shard, down_shard, strided_shard,
    out_big_ref, out_small_ref, grad_big_ref, grad_small_ref, kv_out, up_out, down_out, strided_out,
    xb_raw, xs_raw, gb_raw, gs_raw, halo_big, halo_small, taps, vec, conv, rstd_one, normed,
    hidden, slope, branch, xhat, rstd_two, zeta, blocks, d_blocks, g_wide, g_rows, d_branch, d_pre,
    dhalo_big, dhalo_small, d_taps, d_vec, d_bias_up,
    kv_all, w_all, d_all, landing, plane_in, totals, line_in, final,
    d_kv, kv_part, kv_in, kv_sum,
    sems, send_sems, recv_sems,
):
    pad_big, d_zeta, d_normed, d_mixed = branch.at[0:896], dhalo_big.at[0:ROWS], zeta, xhat
    rank, dp_rank = lax.axis_index("section"), lax.axis_index("dp")
    row, column = rank // 2, lax.rem(rank, 2)
    line, core = dp_rank // 2, lax.rem(dp_rank, 2)
    flanks = (rank + 1 - 2 * column, rank + 2 - 4 * row, 3 - rank)
    twin = {"section": rank, "dp": dp_rank + 1 - 2 * core}

    def ahead(offset):
        return lax.rem(line + offset, PLANES)

    def on_line(offset):
        return {"section": rank, "dp": ahead(offset) * 2 + core}

    def on_plane(index):
        return {"section": flanks[index], "dp": dp_rank}

    barrier = pltpu.get_barrier_semaphore()
    def on_group(offset):
        return {"section": rank, "dp": lax.rem(dp_rank + offset, 8)}

    for target in [on_plane(index) for index in range(3)] + [on_group(offset) for offset in range(1, 8)]:
        pl.semaphore_signal(barrier, inc=1, device_id=target, device_id_type=MESH)

    made = []

    def plan(source, target_ref, target):
        index = len(made)
        copy = pltpu.make_async_remote_copy(
            source, target_ref, send_sems.at[index], recv_sems.at[index], device_id=target, device_id_type=MESH
        )
        made.append(copy)
        return copy

    def same(ref, target):
        return plan(ref, ref, target)

    def go(copies):
        for copy in copies:
            copy.start()

    def arrived(copies):
        for copy in copies:
            copy.wait_recv()

    def piece(index):
        return pl.ds(aligned(index * PIECE, 16), PIECE)

    offsets = (1, 2, 3)

    kv_ways = [same(kv_all.at[line, core], on_line(offset)) for offset in offsets]
    kv_twin = [same(kv_all.at[:, core], twin)]
    along, across, twins = [], [], []
    for weight in range(4):
        def part(offset, quarter):
            return w_all.at[weight, ahead(PLANES - offset), core, piece(quarter)]

        along.append([same(w_all.at[weight, line, core, piece(rank)], on_line(offset)) for offset in offsets])
        across.append([[same(part(offset, rank), on_plane(index)) for offset in offsets] for index in range(3)])
        twins.append([same(w_all.at[weight, :, core, piece(quarter)], twin) for quarter in (rank,) + flanks])

    def pass_line(weight):
        arrived(along[weight])
        for copies in across[weight]:
            go(copies)
        go(twins[weight][:1])

    def pass_plane(weight):
        for index, copies in enumerate(across[weight]):
            arrived(copies)
            go(twins[weight][1 + index : 2 + index])

    def held(weight):
        arrived(twins[weight])

    red_core, red_plane, red_line, red_back = [], [], [], []
    corners = ((row, 1 - column), (1 - row, column), (1 - row, 1 - column))
    for weight in range(4):
        red_core.append([plan(d_all.at[weight, :, 1 - core], landing.at[weight], twin)])
        red_plane.append(
            [
                plan(landing.at[weight, :, at_row, at_column], plane_in.at[weight, index], on_plane(index))
                for index, (at_row, at_column) in enumerate(corners)
            ]
        )
        red_line.append(
            [plan(totals.at[weight, ahead(offset)], line_in.at[weight, offset - 1], on_line(offset)) for offset in offsets]
        )
        red_back.append([same(final.at[weight, rank], on_plane(index)) for index in range(3)])

    def sum_core(weight):
        arrived(red_core[weight])

        def step(index, _):
            landing[weight, index] = (
                landing[weight, index].astype(F32) + d_all[weight, index, core].astype(F32)
            ).astype(BF16)
            return 0

        lax.fori_loop(0, PLANES, step, 0)
        go(red_plane[weight])

    def sum_plane(weight):
        arrived(red_plane[weight])
        for index in range(PLANES):
            total = landing[weight, index, row, column].astype(F32)
            for source in range(3):
                total = total + plane_in[weight, source, index].astype(F32)
            totals[weight, index] = total.astype(BF16)
        go(red_line[weight])

    def sum_line(weight):
        arrived(red_line[weight])
        total = totals[weight, line].astype(F32)
        for offset in offsets:
            total = total + line_in[weight, offset - 1].astype(F32)
        final[weight, rank] = total.astype(BF16)
        go(red_back[weight])

    kv_across = [
        plan(kv_part.at[lax.rem(dp_rank + offset, 8)], kv_in.at[offset - 1], on_group(offset)) for offset in range(1, 8)
    ]
    kv_back = [same(kv_sum.at[rank], on_plane(index)) for index in range(3)]

    def kv_sum_group():
        arrived(kv_across)
        total = kv_part[dp_rank].astype(F32)
        for index in range(7):
            total = total + kv_in[index].astype(F32)
        kv_sum[rank] = total
        go(kv_back)

    w_all[0, line, core] = up_shard[...].astype(BF16)
    w_all[1, line, core] = down_shard[...].astype(BF16)
    w_all[2, line, core] = strided_shard[:, :C].astype(BF16)
    w_all[3, line, core] = strided_shard[:, C:].astype(BF16)
    put_taps = one_hot((TAPS, 128), lambda r: r)
    put_vector = one_hot((13, 128), lambda r: r + 64)
    kv_all[line, core] = (
        nn(kernel_ref[...].astype(BF16), put_taps)
        + lax.dot_general(
            vector_ref[...].astype(BF16), put_vector, (((0,), (0,)), ((), ())), preferred_element_type=F32
        )
    ).astype(BF16)
    pl.semaphore_wait(barrier, 10)
    go(kv_ways)
    for weight in range(4):
        go(along[weight])

    def at_step(step, hooks):
        for when, event in hooks:
            pl.when(step == when)(event)

    def events(*calls):
        def run():
            for call, *arguments in calls:
                call(*arguments)

        return run

    own = pl.ds(rank * 2, 2)
    copies = [
        pltpu.make_async_copy(source, target, sems.at[index])
        for index, (source, target) in enumerate(
            (
                (big_hbm.at[own], xb_raw),
                (small_hbm, xs_raw),
                (big_cot_hbm.at[own], gb_raw),
                (small_cot_hbm, gs_raw),
            )
        )
    ]
    for copy in copies:
        copy.start()

    spread_big = one_hot((112, 128), lambda r: ((r >> 1) & 3) * 32 + (r >> 3) * 2 + (r & 1))
    spread_small = one_hot((48, 192), lambda r: ((r >> 1) & 3) * 48 + (r >> 3) * 8 + 2 * rank + (r & 1))
    gather_big = one_hot((128, 112), lambda r: ((r >> 1) & 15) * 8 + (r >> 5) * 2 + (r & 1))
    gather_small = one_hot((64, 48), lambda r: ((r >> 1) & 7) * 8 + (r >> 4) * 2 + (r & 1))
    block_big = one_hot(
        (128, 112), lambda r: (((r >> 1) & 7) * 2 + ((r >> 5) & 1)) * 8 + (r >> 6) * 4 + ((r >> 4) & 1) * 2 + (r & 1)
    )
    block_small = one_hot(
        (64, 48), lambda r: (((r >> 1) & 3) * 2 + ((r >> 4) & 1)) * 8 + (r >> 5) * 4 + ((r >> 3) & 1) * 2 + (r & 1)
    )
    pick_small = one_hot(
        (16, 48), lambda r: (r >> 3) * 24 + ((r >> 1) & 3) * 8 + 2 * rank + (r & 1), lambda r: (r & 7) < 6
    )
    sub = lax.broadcasted_iota(jnp.int32, (8, 128), 0)
    top = jnp.where(sub < 4, 1.0, 0.0).astype(F32)
    bottom = 1.0 - top

    def vector_row(index):
        return vec[index : index + 1, :]

    keep_zero = keep_ref[0, 2 * rank].astype(F32) / KEEP_RATE
    keep_one = keep_ref[0, 2 * rank + 1].astype(F32) / KEEP_RATE
    lane_wide = lambda value: jnp.concatenate([value] * 3, axis=1)
    big_factor = lane_wide(jnp.where((sub & 2) == 0, keep_zero, keep_one))
    small_factor = lane_wide(jnp.where((sub & 1) == 0, keep_zero, keep_one))

    pad_big[...] = jnp.zeros_like(pad_big)
    g_wide[...] = jnp.zeros_like(g_wide)

    for copy in copies:
        copy.wait()

    for micro in range(2):
        def put_big(h, _):
            pad_big[rows_at((micro * 14 + h) * 32, 28), :] = xb_raw[micro, h].astype(F32).reshape(28, C)
            return 0

        unrolled(14, put_big)
        for p in range(7):
            start = p * 32 + micro * 16
            g_wide[start : start + 14, :] = gb_raw[micro, p].astype(F32).reshape(14, C2)
    for unit in range(UNITS):
        for p in range(3):
            source = jnp.concatenate(
                [gs_raw[2 * unit + crop, p].astype(F32).reshape(24, C2) for crop in range(2)], axis=0
            )
            start = BLOCK_BIG + (unit * 3 + p) * 16
            g_wide[start : start + 16, :] = nn(pick_small, source.astype(BF16))

    arrived(kv_ways)
    go(kv_twin)

    def spread_rows(hh, _):
        tiles = [pad_big[rows_at((micro * 14 + half * 7 + hh) * 32, 32), :] for half in range(2) for micro in range(2)]
        source = jnp.concatenate(tiles, axis=0).astype(BF16)
        halo_big[rows_at((hh + 3) * 112, 112), :] = nn(spread_big, source)
        return 0

    unrolled(BIG_HALF, spread_rows)
    for unit in range(UNITS):
        def spread_unit(hh, _):
            tiles = [
                xs_raw[2 * unit + crop, half * 3 + hh].reshape(48, C) for half in range(2) for crop in range(2)
            ]
            source = jnp.concatenate(tiles, axis=0)
            halo_small[rows_at(unit * HALO_SMALL + (hh + 3) * 48, 48), :] = nn(spread_small, source)
            return 0

        unrolled(SMALL_HALF, spread_unit)

    def halos(ref, base, half, side):
        def step(index, _):
            for lane in range(3):
                lanes = slice(lane * 128, lane * 128 + 128)
                low = ref[rows_at(base + (3 * side + index) * 8, 8), lanes]
                ref[rows_at(base + ((3 + half) * side + index) * 8, 8), lanes] = pltpu.roll(low, 4, 0) * top
                high = ref[rows_at(base + (half * side + index) * 8, 8), lanes]
                ref[rows_at(base + index * 8, 8), lanes] = pltpu.roll(high, 4, 0) * bottom
            return 0

        unrolled(3 * side, step)

    def all_halos(big, small):
        halos(big, 0, BIG_HALF, BIG_SIDE)
        for unit in range(UNITS):
            halos(small, unit * HALO_SMALL, SMALL_HALF, SMALL_SIDE)

    all_halos(halo_big, halo_small)

    arrived(kv_twin)
    kv = jnp.transpose(flat(kv_all[...]).astype(F32))
    vec[...] = kv[64:80]
    for tap in range(TAPS):
        taps[tap] = jnp.broadcast_to(kv[tap : tap + 1] * (1.0 / KS), (8, C))

    def convolve(big, small, mirrored, finish, hooks):
        def tap_at(i, j, lanes):
            index = i * KS + j
            return taps[TAPS - 1 - index if mirrored else index, :, lanes]

        def image_row(step, _):
            h, lane = step // 3, lax.rem(step, 3)
            lanes = pl.ds(aligned(lane * 128, 128), 128)
            sums = [None] * BIG_SIDE
            for i in range(KS):
                values = [big[rows_at(((h + i) * BIG_SIDE + w) * 8, 8), lanes] for w in range(BIG_SIDE)]
                for j in range(KS):
                    weight = tap_at(i, j, lanes)
                    for w in range(max(0, 3 - j), min(BIG_SIDE, BIG_SIDE + 3 - j)):
                        term = values[w + j - 3] * weight
                        sums[w] = term if sums[w] is None else sums[w] + term
            for w in range(BIG_SIDE):
                finish((h * BIG_SIDE + w) * 8, sums[w], lanes)
            at_step(step, hooks)
            return 0

        lax.fori_loop(0, BIG_HALF * 3, image_row, 0)

        def small_row(step, _):
            h, lane = step // 3, lax.rem(step, 3)
            lanes = pl.ds(aligned(lane * 128, 128), 128)
            sums = [[None] * SMALL_SIDE for _ in range(UNITS)]
            for i in range(KS):
                values = [
                    [
                        small[rows_at(unit * HALO_SMALL + ((h + i) * SMALL_SIDE + w) * 8, 8), lanes]
                        for w in range(SMALL_SIDE)
                    ]
                    for unit in range(UNITS)
                ]
                for j in range(KS):
                    weight = tap_at(i, j, lanes)
                    for w in range(max(0, 3 - j), min(SMALL_SIDE, SMALL_SIDE + 3 - j)):
                        for unit in range(UNITS):
                            term = values[unit][w + j - 3] * weight
                            old = sums[unit][w]
                            sums[unit][w] = term if old is None else old + term
            for unit in range(UNITS):
                for w in range(SMALL_SIDE):
                    finish(BIG_ROWS + unit * SMALL_ROWS + (h * SMALL_SIDE + w) * 8, sums[unit][w], lanes)
            return 0

        lax.fori_loop(0, SMALL_HALF * 3, small_row, 0)

    def keep_conv(start, value, lanes):
        conv[rows_at(start, 8), lanes] = value

    convolve(halo_big, halo_small, False, keep_conv, [(3, events((pass_line, 0))), (20, events((pass_line, 1)))])
    pass_plane(0)

    def for_tiles(run):
        def big_tile(index, _):
            run(index * 112, 112, big_factor, halo_big, dhalo_big, 336 + index * 112)
            return 0

        unrolled(BIG_HALF, big_tile)

        def small_tile(index, _):
            run(BIG_ROWS + index * 144, 144, small_factor, halo_small, dhalo_small, index * HALO_SMALL + 144)
            return 0

        unrolled(UNITS, small_tile)

    def fold(value):
        return jnp.sum(value.reshape(-1, 8, value.shape[-1]), axis=0)

    def mean_of(value):
        return jnp.sum(value, axis=-1, keepdims=True) * (1.0 / C)

    def wide(ref, rows):
        value = ref[rows, :]
        return jnp.concatenate([value, value, value], axis=1)

    def norm_one(start, size, *_):
        rows = rows_at(start, size)
        value = conv[rows, :] + vector_row(V_BIAS_DW)
        centered = value - mean_of(value)
        scale = lax.rsqrt(mean_of(centered * centered) + EPSILON)
        unit = centered * scale
        conv[rows, :] = unit
        rstd_one[rows, :] = jnp.broadcast_to(scale, (size, 128))
        normed[pl.ds(aligned(start, 16), size), :] = (
            unit * vector_row(V_GAIN_ONE) + vector_row(V_OFFSET_ONE)
        ).astype(BF16)

    for_tiles(norm_one)
    pass_line(2)

    def up_tile(index, _):
        rows = pl.ds(aligned(index * TILE, 16), TILE)
        left = normed[rows, :]
        for chunk in range(FF // CHUNK):
            span = slice(chunk * CHUNK, (chunk + 1) * CHUNK)
            bias = vector_row(V_BIAS_UP + chunk)
            pre = (
                lax.dot_general(left, flat(w_all[0, chunk]), (((1,), (1,)), ((), ())), preferred_element_type=F32)
                * UP_SCALE
                + bias
            )
            scaled_pre = pre * math.sqrt(0.5)
            whole = 0.5 + 0.5 * lax.erf(scaled_pre)
            density = jnp.exp2(scaled_pre * scaled_pre * -math.log2(math.e))
            hidden[rows, span] = (pre * whole).astype(BF16)
            slope[rows, span] = whole + pre * density * (1.0 / math.sqrt(2.0 * math.pi))
        at_step(index, [(0, events((pass_line, 3))), (2, events((pass_plane, 1)))])
        return 0

    held(0)
    lax.fori_loop(0, ROWS // TILE, up_tile, 0)
    held(1)

    def branch_tile(index, _):
        rows = pl.ds(aligned(index * TILE, 16), TILE)
        branch[rows, :] = nn(hidden[rows, :], flat(w_all[1])) * DOWN_SCALE + vector_row(V_BIAS_DOWN)
        return 0

    lax.fori_loop(0, ROWS // TILE, branch_tile, 0)

    def scaled(value, factor):
        return (value.reshape(-1, 8, C) * factor[None]).reshape(-1, C)

    def norm_two(start, size, factor, field, _, offset):
        rows = rows_at(start, size)
        value = field[rows_at(offset, size), :] + scaled(vector_row(V_SCALE) * branch[rows, :], factor)
        centered = value - mean_of(value)
        scale = lax.rsqrt(mean_of(centered * centered) + EPSILON)
        unit = centered * scale
        xhat[rows, :] = unit
        rstd_two[rows, :] = jnp.broadcast_to(scale, (size, 128))
        zeta[pl.ds(aligned(start, 16), size), :] = (
            unit * vector_row(V_GAIN_TWO) + vector_row(V_OFFSET_TWO)
        ).astype(BF16)

    for_tiles(norm_two)

    def block_spans(base, count, hh, half_side):
        for half in range(2):
            h = half * half_side + hh
            p, a = h // 2, h % 2
            for b in range(2):
                yield (
                    pl.ds(aligned(base + p * count, 16), count),
                    pl.ds(aligned((2 * a + b) * C, 128), C),
                )

    def block_rows(source, matrix, base, count, hh, half_side):
        picked = nn(matrix, source).astype(BF16)
        for index, span in enumerate(block_spans(base, count, hh, half_side)):
            blocks[span] = picked[index * count : (index + 1) * count]

    def big_blocks(hh, _):
        block_rows(zeta[pl.ds(aligned(hh * 112, 16), 112), :], block_big, 0, 32, hh, 7)
        return 0

    unrolled(BIG_HALF, big_blocks)
    for unit in range(UNITS):
        def small_blocks(hh, _):
            source = zeta[pl.ds(aligned(BIG_ROWS + unit * SMALL_ROWS + hh * 48, 16), 48), :]
            block_rows(source, block_small, BLOCK_BIG + unit * 48, 16, hh, 3)
            return 0

        unrolled(SMALL_HALF, small_blocks)

    g_rows[...] = g_wide[...].astype(BF16)
    bias_out_grad = jnp.sum(g_wide[...], axis=0, keepdims=True)
    d_vec[V_BIAS_OUT, 0:1, :] = bias_out_grad[:, :C]
    d_vec[V_BIAS_OUT + 1, 0:1, :] = bias_out_grad[:, C:]

    def outer(left, right, scale):
        product = lax.dot_general(left, right, (((0,), (0,)), ((), ())), preferred_element_type=F32)
        return (product * scale).astype(BF16).reshape(2, 2, 2, PIECE, C)

    for half in range(2):
        def strided_grad(index, _):
            span = pl.ds(aligned(index * C, 128), C)
            d_all[2 + half, index] = outer(blocks[:, span], g_rows[:, half * C : half * C + C], STRIDED_SCALE)
            return 0

        lax.fori_loop(0, 4, strided_grad, 0)
        go(red_core[2 + half])
        if half == 0:
            pass_plane(2)

    bias_out = jnp.concatenate([vector_row(V_BIAS_OUT), vector_row(V_BIAS_OUT + 1)], axis=1)

    def out_half(half):
        span = slice(half * C, half * C + C)
        g_wide[:, span] = nn(blocks[...], flat(w_all[2 + half])) * STRIDED_SCALE + bias_out[:, span]

    held(2)
    out_half(0)
    pass_plane(3)
    held(3)

    def block_grad(index, _):
        span = pl.ds(aligned(index * 384, 128), 384)
        total = None
        for half in range(2):
            term = lax.dot_general(
                g_rows[:, half * C : half * C + C],
                flat(w_all[2 + half, index]),
                (((1,), (1,)), ((), ())),
                preferred_element_type=F32,
            )
            total = term if total is None else total + term
        d_blocks[:, span] = (total * STRIDED_SCALE).astype(BF16)
        return 0

    lax.fori_loop(0, 4, block_grad, 0)

    def unblock(matrix, base, count, hh, half_side):
        parts = jnp.concatenate([d_blocks[span] for span in block_spans(base, count, hh, half_side)], axis=0)
        return lax.dot_general(matrix, parts, (((0,), (0,)), ((), ())), preferred_element_type=F32)

    def big_unblock(hh, _):
        d_zeta[rows_at(hh * 112, 112), :] = unblock(block_big, 0, 32, hh, 7)
        return 0

    unrolled(BIG_HALF, big_unblock)
    for unit in range(UNITS):
        def small_unblock(hh, _):
            d_zeta[rows_at(BIG_ROWS + unit * SMALL_ROWS + hh * 48, 48), :] = unblock(
                block_small, BLOCK_BIG + unit * 48, 16, hh, 3
            )
            return 0

        unrolled(SMALL_HALF, small_unblock)

    sum_core(2)

    for index in range(11):
        d_vec[index] = jnp.zeros((8, C), F32)

    def norm_two_back(start, size, factor, *_):
        rows = rows_at(start, size)
        unit = xhat[rows, :]
        grad = d_zeta[rows, :]
        d_vec[V_GAIN_TWO] += fold(grad * unit)
        d_vec[V_OFFSET_TWO] += fold(grad)
        inner = grad * vector_row(V_GAIN_TWO)
        mixed = (inner - mean_of(inner) - unit * mean_of(inner * unit)) * wide(rstd_two, rows)
        d_mixed[rows, :] = mixed
        kept = scaled(mixed, factor)
        d_vec[V_SCALE] += fold(kept * branch[rows, :])
        lowered = (kept * vector_row(V_SCALE)).astype(BF16)
        d_branch[pl.ds(aligned(start, 16), size), :] = lowered
        d_vec[V_BIAS_DOWN] += fold(lowered.astype(F32))

    for_tiles(norm_two_back)
    sum_core(3)

    def down_grad(index, _):
        span = pl.ds(aligned(index * C, 128), C)
        d_all[1, index] = outer(hidden[:, span], d_branch[...], DOWN_SCALE)
        return 0

    lax.fori_loop(0, 4, down_grad, 0)
    go(red_core[1])

    d_bias_up[...] = jnp.zeros_like(d_bias_up)

    def down_tile(index, _):
        rows = pl.ds(aligned(index * TILE, 16), TILE)
        left = d_branch[rows, :]
        for chunk in range(FF // CHUNK):
            span = slice(chunk * CHUNK, (chunk + 1) * CHUNK)
            d_hidden = (
                lax.dot_general(left, flat(w_all[1, chunk]), (((1,), (1,)), ((), ())), preferred_element_type=F32)
                * DOWN_SCALE
            )
            lowered = (d_hidden * slope[rows, span]).astype(BF16)
            d_pre[rows, span] = lowered
            d_bias_up[:, span] += fold(lowered.astype(F32))
        d_normed[rows, :] = (nn(d_pre[rows, :], flat(w_all[0])) * UP_SCALE).astype(BF16)
        at_step(index, [(2, events((sum_core, 1))), (3, events((sum_plane, 2)))])
        return 0

    lax.fori_loop(0, ROWS // TILE, down_tile, 0)

    def up_grad(index, _):
        span = pl.ds(aligned(index * C, 128), C)
        d_all[0, index] = outer(d_pre[:, span], normed[...], UP_SCALE)
        return 0

    lax.fori_loop(0, 4, up_grad, 0)
    go(red_core[0])

    def norm_one_back(start, size, _, __, target, offset):
        rows = rows_at(start, size)
        unit = conv[rows, :]
        grad = d_normed[pl.ds(aligned(start, 16), size), :].astype(F32)
        d_vec[V_GAIN_ONE] += fold(grad * unit)
        d_vec[V_OFFSET_ONE] += fold(grad)
        inner = grad * vector_row(V_GAIN_ONE)
        result = (inner - mean_of(inner) - unit * mean_of(inner * unit)) * wide(rstd_one, rows)
        d_vec[V_BIAS_DW] += fold(result)
        target[rows_at(offset, size), :] = result

    for_tiles(norm_one_back)
    all_halos(dhalo_big, dhalo_small)

    def tap_grads(step, _):
        i, lane = step // 3, lax.rem(step, 3)
        lanes = pl.ds(aligned(lane * 128, 128), 128)

        sums = [[None, None] for _ in range(KS)]

        def image_row(side, field, grad, field_base, grad_base, turn):
            inputs = [field[rows_at(field_base + w * 8, 8), lanes] for w in range(side)]
            outer = [grad[rows_at(grad_base + w * 8, 8), lanes] for w in range(side)]
            for w in range(side):
                for j in range(max(0, 3 - w), min(KS, side + 3 - w)):
                    term = inputs[w + j - 3] * outer[w]
                    slot = (w + turn) % 2
                    old = sums[j][slot]
                    sums[j][slot] = term if old is None else old + term

        for h in range(BIG_HALF):
            image_row(BIG_SIDE, halo_big, dhalo_big, (h + i) * 112, (h + 3) * 112, h)
        for h in range(SMALL_HALF):
            for unit in range(UNITS):
                base = unit * HALO_SMALL
                image_row(SMALL_SIDE, halo_small, dhalo_small, base + (h + i) * 48, base + (h + 3) * 48, h)
        for j in range(KS):
            d_taps[i * KS + j, :, lanes] = sums[j][0] + sums[j][1]
        at_step(
            step,
            [
                (3, events((sum_plane, 3))),
                (5, events((sum_core, 0))),
                (7, events((sum_line, 2))),
                (16, events((sum_line, 3))),
                (19, events((sum_plane, 1))),
            ],
        )
        return 0

    lax.fori_loop(0, KS * 3, tap_grads, 0)

    d_kv[56:128, :] = jnp.zeros((72, C), F32)
    for tap in range(TAPS):
        d_kv[tap : tap + 1, :] = jnp.sum(d_taps[tap], axis=0, keepdims=True) * (1.0 / KS)
    for index in range(11):
        if V_BIAS_UP <= index < V_BIAS_UP + UP_ROWS:
            continue
        d_kv[TAPS + index : TAPS + index + 1, :] = jnp.sum(d_vec[index], axis=0, keepdims=True)
    d_kv[TAPS + V_BIAS_OUT : TAPS + V_BIAS_OUT + 1, :] = d_vec[V_BIAS_OUT, 0:1, :]
    d_kv[TAPS + V_BIAS_OUT + 1 : TAPS + V_BIAS_OUT + 2, :] = d_vec[V_BIAS_OUT + 1, 0:1, :]
    bias_up_grad = jnp.sum(d_bias_up[...], axis=0, keepdims=True)
    for index in range(UP_ROWS):
        d_kv[TAPS + V_BIAS_UP + index : TAPS + V_BIAS_UP + index + 1, :] = bias_up_grad[
            :, index * C : (index + 1) * C
        ]

    kv_part[...] = jnp.transpose(d_kv[...]).astype(BF16).reshape(8, PIECE, 128)
    go(kv_across)

    def add_grad(start, value, lanes):
        d_mixed[rows_at(start, 8), lanes] += value

    convolve(
        dhalo_big,
        dhalo_small,
        True,
        add_grad,
        [
            (14, events((sum_line, 1), (kv_sum_group,))),
            (18, events((sum_plane, 0))),
        ],
    )
    out_half(1)
    for micro in range(2):
        for p in range(7):
            start = p * 32 + micro * 16
            out_big_ref[micro, p] = g_wide[start : start + 14, :].reshape(7, 2, C2)
    for unit in range(UNITS):
        for p in range(3):
            for crop in range(2):
                start = BLOCK_BIG + (unit * 3 + p) * 16 + crop * 8
                out_small_ref[2 * unit + crop, p] = g_wide[start : start + 6, :].reshape(3, 2, C2)


    sum_line(0)

    def restore(matrix, value):
        high = value.astype(BF16)
        low = (value - high.astype(F32)).astype(BF16)
        return nn(matrix, high) + nn(matrix, low)

    def grad_rows(hh, _):
        natural = restore(gather_big, d_mixed[rows_at(hh * 112, 112), :])
        for half in range(2):
            for micro in range(2):
                start = (half * 2 + micro) * 32
                grad_big_ref[micro, half * 7 + hh] = natural[start : start + 28].reshape(14, 2, C)
        return 0

    unrolled(BIG_HALF, grad_rows)
    for unit in range(UNITS):
        def small_grad_rows(hh, _):
            natural = restore(gather_small, d_mixed[rows_at(BIG_ROWS + unit * SMALL_ROWS + hh * 48, 48), :])
            for half in range(2):
                for crop in range(2):
                    start = (half * 2 + crop) * 16
                    grad_small_ref[2 * unit + crop, half * 3 + hh] = natural[start : start + 12].reshape(6, 2, C)
            return 0

        unrolled(SMALL_HALF, small_grad_rows)

    for weight in range(4):
        arrived(red_back[weight])
    up_out[...] = flat(final[0])
    down_out[...] = flat(final[1])
    strided_out[:, :C] = flat(final[2])
    strided_out[:, C:] = flat(final[3])
    arrived(kv_back)
    kv_out[...] = kv_sum[0] + kv_sum[1] + kv_sum[2] + kv_sum[3]
    for copy in made:
        copy.wait_send()


def finish_kernel(rates, *refs):
    d_kv, d_up, d_down, d_strided = refs[:4]
    state, images, outs = refs[4:19], refs[19:23], refs[23:42]
    held, sems = refs[42:46], refs[46]
    inward = [pltpu.make_async_copy(images[index], held[index], sems.at[index]) for index in range(4)]
    outward = [pltpu.make_async_copy(held[index], outs[index], sems.at[4 + index]) for index in range(4)]
    for copy in inward:
        copy.start()
    for copy, onward in zip(inward, outward):
        copy.wait()
        onward.start()
    packed = d_kv[...]
    gradients = (
        packed[:, :TAPS],
        jnp.transpose(packed)[TAPS : TAPS + 13],
        d_up[...].astype(F32),
        d_down[...].astype(F32),
        d_strided[...].astype(F32),
    )
    for position in range(5):
        weight, moment, average = state[3 * position : 3 * position + 3]
        new_weight, new_moment, new_average = outs[4 + 3 * position : 7 + 3 * position]
        gradient = gradients[position]
        moment_next = MOMENTUM * moment[...] + gradient
        weight_next = weight[...] - rates[position] * (gradient + MOMENTUM * moment_next)
        new_moment[...] = moment_next
        new_weight[...] = weight_next
        new_average[...] = AVERAGING * average[...] + (1.0 - AVERAGING) * weight_next
    for copy in outward:
        copy.wait()


def finish(rates, grads, state, images):
    any_spec = pl.BlockSpec(memory_space=pl.ANY)
    vmem = pl.BlockSpec(memory_space=pltpu.VMEM)
    return pl.pallas_call(
        functools.partial(finish_kernel, rates),
        out_shape=[jax.ShapeDtypeStruct(array.shape, F32) for array in (*images, *state)],
        in_specs=[vmem] * 19 + [any_spec] * 4,
        out_specs=[any_spec] * 4 + [vmem] * 15,
        scratch_shapes=[pltpu.VMEM(array.shape, F32) for array in images] + [pltpu.SemaphoreType.DMA((8,))],
        compiler_params=pltpu.CompilerParams(vmem_limit_bytes=(63 << 20) + (1 << 19)),
    )(*grads, *state, *images)


def fused_step(big_crops, small_crops, big_cot, small_cot, keep, kernel_t, vector, up_t, down, strided):
    any_spec = pl.BlockSpec(memory_space=pl.ANY)
    vmem = pl.BlockSpec(memory_space=pltpu.VMEM)
    shape = jax.ShapeDtypeStruct
    big_order, small_order = (0, 2, 3, 1, 4), (1, 2, 3, 0, 4)
    results = pl.pallas_call(
        step_kernel,
        out_shape=(
            shape((2, 7, 7, 2, C2), F32),
            shape((6, 3, 3, 2, C2), F32),
            shape((2, 14, 14, 2, C), F32),
            shape((6, 6, 6, 2, C), F32),
            shape((PIECE, 128), F32),
            shape((192, C), BF16),
            shape((192, C), BF16),
            shape((192, C2), BF16),
        ),
        in_specs=[any_spec] * 4 + [pl.BlockSpec(memory_space=pltpu.SMEM)] + [vmem] * 5,
        out_specs=[vmem] * 8,
        scratch_shapes=[
            pltpu.VMEM((2, 14, 14, 2, C), BF16),
            pltpu.VMEM((6, 6, 6, 8, C), BF16),
            pltpu.VMEM((2, 7, 7, 2, C2), BF16),
            pltpu.VMEM((6, 3, 3, 8, C2), BF16),
            pltpu.VMEM((HALO_BIG, C), F32),
            pltpu.VMEM((UNITS * HALO_SMALL, C), F32),
            pltpu.VMEM((TAPS, 8, C), F32),
            pltpu.VMEM((16, C), F32),
            pltpu.VMEM((ROWS, C), F32),
            pltpu.VMEM((ROWS, 128), F32),
            pltpu.VMEM((ROWS, C), BF16),
            pltpu.VMEM((ROWS, FF), BF16),
            pltpu.VMEM((ROWS, FF), F32),
            pltpu.VMEM((ROWS, C), F32),
            pltpu.VMEM((ROWS, C), F32),
            pltpu.VMEM((ROWS, 128), F32),
            pltpu.VMEM((ROWS, C), BF16),
            pltpu.VMEM((BLOCKS, 4 * C), BF16),
            pltpu.VMEM((BLOCKS, 4 * C), BF16),
            pltpu.VMEM((BLOCKS, C2), F32),
            pltpu.VMEM((BLOCKS, C2), BF16),
            pltpu.VMEM((ROWS, C), BF16),
            pltpu.VMEM((ROWS, FF), BF16),
            pltpu.VMEM((HALO_BIG, C), F32),
            pltpu.VMEM((UNITS * HALO_SMALL, C), F32),
            pltpu.VMEM((TAPS, 8, C), F32),
            pltpu.VMEM((13, 8, C), F32),
            pltpu.VMEM((8, FF), F32),
            pltpu.VMEM((4, 2, 48, 128), BF16),
            pltpu.VMEM((4, 4, 2, 192, C), BF16),
            pltpu.VMEM((4, 4, 2, 2, 2, PIECE, C), BF16),
            pltpu.VMEM((4, 4, 2, 2, PIECE, C), BF16),
            pltpu.VMEM((4, 3, 4, PIECE, C), BF16),
            pltpu.VMEM((4, 4, PIECE, C), BF16),
            pltpu.VMEM((4, 3, PIECE, C), BF16),
            pltpu.VMEM((4, 4, PIECE, C), BF16),
            pltpu.VMEM((128, C), F32),
            pltpu.VMEM((8, PIECE, 128), BF16),
            pltpu.VMEM((7, PIECE, 128), BF16),
            pltpu.VMEM((4, PIECE, 128), F32),
            pltpu.SemaphoreType.DMA((4,)),
            pltpu.SemaphoreType.DMA((COPIES,)),
            pltpu.SemaphoreType.DMA((COPIES,)),
        ],
        compiler_params=pltpu.CompilerParams(vmem_limit_bytes=(63 << 20) + (1 << 19), collective_id=0, has_side_effects=True),
    )(
        big_crops.transpose(big_order),
        small_crops.transpose(small_order),
        big_cot.transpose(big_order),
        small_cot.transpose(small_order),
        keep,
        kernel_t,
        vector,
        up_t,
        down,
        strided,
    )
    return results[4:], results[:4]


def body(big_crops, small_crops, big_cot, small_cot, drop_mask, *state):
    sections, rank = lax.axis_size("section"), lax.axis_index("section")
    micro_count = big_crops.shape[0]
    fits = (
        micro_count == 2 * sections
        and big_crops.shape[1:] == (BIG_IMG, BIG_SIDE, BIG_SIDE, C)
        and small_crops.shape[1:] == (SMALL_IMG, SMALL_SIDE, SMALL_SIDE, C)
        and drop_mask.shape[1] == 1
        and (sections, lax.axis_size("dp")) == (4, 8)
    )
    if not fits:
        return plain_body(big_crops, small_crops, big_cot, small_cot, drop_mask, *state)
    masters, moments, averages = state[0::3], state[1::3], state[2::3]
    turned = (True, False, True, False, False)
    masters, moments, averages = (
        [jnp.transpose(array) if turn else array for array, turn in zip(group, turned)]
        for group in (masters, moments, averages)
    )
    grads, images = fused_step(big_crops, small_crops, big_cot, small_cot, drop_mask.T, *masters)
    pixel_total = (
        lax.axis_size("dp")
        * micro_count
        * (math.prod(big_crops.shape[1:4]) + math.prod(small_crops.shape[1:4]))
    )
    rates = tuple(rate * math.sqrt(fan / pixel_total) for rate, fan in zip(RATES, FANS))
    state = [array for group in zip(masters, moments, averages) for array in group]
    results = finish(rates, grads, state, images)
    order_big, order_small = (0, 3, 1, 2, 4), (3, 0, 1, 2, 4)
    return (
        results[0].transpose(order_big),
        results[1].transpose(order_small),
        results[2].transpose(order_big),
        results[3].transpose(order_small),
        *(array.T if turned[index // 3] else array for index, array in enumerate(results[4:])),
    )


def solution(mesh):
    crops = P(None, "dp", None, None, None)
    owned = P("section", "dp", None, None, None)
    weights = (P(None, "dp"),) * 9 + (P("dp", None),) * 6
    return jax.shard_map(
        body,
        mesh=mesh,
        in_specs=(crops,) * 4 + (P(None, "dp"),) + weights,
        out_specs=(owned,) * 4 + weights,
        check_vma=False,
    )
```

```python
import functools
import math

import jax
import jax.numpy as jnp
from jax import lax
from jax.experimental import pallas as pl
from jax.experimental.pallas import tpu as pltpu
from jax.sharding import PartitionSpec as P

C = 384
FF = 1536
C2 = 768
KS = 7
BIG_IMG = 2
SMALL_IMG = 6

KEEP_RATE = 0.9
MOMENTUM = 0.5
AVERAGING = 0.5
EPSILON = 1e-06
RATES = (1.1, 0.4, 2.7, 1.3, 1.3)
FANS = (KS * KS, 1, C, FF, 4 * C)
UP_ROWS = FF // C


def layer_norm(values, gain_row, offset_row):
    average = jnp.mean(values, axis=-1, keepdims=True)
    centered = values - average
    variance = jnp.mean(centered * centered, axis=-1, keepdims=True)
    return centered * lax.rsqrt(variance + EPSILON) * gain_row + offset_row


def depthwise(field, kernel, precision):
    radius = KS // 2
    channels = field.shape[-1]
    return lax.conv_general_dilated(
        field,
        kernel.reshape(KS, KS, 1, channels),
        (1, 1),
        ((radius, radius), (radius, radius)),
        dimension_numbers=("NHWC", "HWIO", "NHWC"),
        feature_group_count=channels,
        precision=precision,
        preferred_element_type=jnp.float32,
    )


def to_blocks(field):
    count, side = field.shape[0], field.shape[1]
    half = side // 2
    return (
        field.reshape(count, half, 2, half, 2, C)
        .transpose(0, 1, 3, 2, 4, 5)
        .reshape(count * half * half, 4 * C)
    )


def from_blocks(flat, shape):
    count, half = shape[0], shape[1] // 2
    return flat.reshape(count, half, half, 2, 2, C).transpose(0, 1, 3, 2, 4, 5).reshape(shape)


def contract(left, right):
    return lax.dot_general(left, right, (((0,), (0,)), ((), ())), preferred_element_type=jnp.float32)


def dot_t(left, right):
    return lax.dot_general(left, right, (((1,), (1,)), ((), ())), preferred_element_type=jnp.float32)


def group_step(crops, cot, keep, kernel, values, up, down, strided):
    bias_dw, gain_one, offset_one = values[0], values[1], values[2]
    bias_up = values[3 : 3 + UP_ROWS].reshape(FF)
    bias_down, layer_scale = values[3 + UP_ROWS], values[4 + UP_ROWS]
    gain_two, offset_two = values[5 + UP_ROWS], values[6 + UP_ROWS]
    bias_out = values[7 + UP_ROWS :].reshape(C2)
    up_scale, down_scale, strided_scale = 1 / math.sqrt(C), 1 / math.sqrt(FF), 1 / math.sqrt(4 * C)
    side = crops.shape[1]
    factor = jnp.repeat(keep, side * side)[:, None]
    field = crops.astype(jnp.float32)

    def first(field_value, kernel_value, bias, gain, offset):
        conv_out = depthwise(field_value, kernel_value, None) * (1.0 / KS) + bias
        return layer_norm(conv_out, gain, offset)

    normed, first_pull = jax.vjp(first, field, kernel.astype(jnp.float32), bias_dw, gain_one, offset_one)
    rows = normed.astype(jnp.bfloat16).reshape(-1, C)
    pre_act = jnp.dot(rows, up, preferred_element_type=jnp.float32) * up_scale + bias_up
    phi_big = 0.5 * (1.0 + lax.erf(pre_act * math.sqrt(0.5)))
    density = jnp.exp(-0.5 * pre_act * pre_act) * (1.0 / math.sqrt(2.0 * math.pi))
    slope = phi_big + pre_act * density
    hidden = (pre_act * phi_big).astype(jnp.bfloat16)
    branch = jnp.dot(hidden, down, preferred_element_type=jnp.float32) * down_scale + bias_down
    mixed = field.reshape(-1, C) + layer_scale * branch * factor
    zeta, norm_pull = jax.vjp(layer_norm, mixed, gain_two, offset_two)
    blocks = to_blocks(zeta.astype(jnp.bfloat16).reshape(crops.shape))
    result = jnp.dot(blocks, strided, preferred_element_type=jnp.float32) * strided_scale + bias_out

    grad_out = cot.reshape(-1, C2)
    d_strided = contract(blocks, grad_out) * strided_scale
    d_bias_out = jnp.sum(grad_out.astype(jnp.float32), axis=0)
    d_blocks = dot_t(grad_out, strided) * strided_scale
    d_zeta = from_blocks(d_blocks.astype(jnp.bfloat16), crops.shape).reshape(-1, C)
    d_mixed, d_gain_two, d_offset_two = norm_pull(d_zeta.astype(jnp.float32))
    d_scale = jnp.sum(d_mixed * factor * branch, axis=0)
    d_branch = (d_mixed * factor * layer_scale).astype(jnp.bfloat16)
    d_bias_down = jnp.sum(d_branch.astype(jnp.float32), axis=0)
    d_down = contract(hidden, d_branch) * down_scale
    d_pre = (dot_t(d_branch, down) * down_scale * slope).astype(jnp.bfloat16)
    d_bias_up = jnp.sum(d_pre.astype(jnp.float32), axis=0)
    d_up = contract(rows, d_pre) * up_scale
    d_normed = (dot_t(d_pre, up) * up_scale).astype(jnp.bfloat16).reshape(crops.shape)
    d_field, d_kernel, d_bias_dw, d_gain_one, d_offset_one = first_pull(d_normed.astype(jnp.float32))
    d_vector = jnp.concatenate(
        [
            d_bias_dw[None],
            d_gain_one[None],
            d_offset_one[None],
            d_bias_up.reshape(UP_ROWS, C),
            d_bias_down[None],
            d_scale[None],
            d_gain_two[None],
            d_offset_two[None],
            d_bias_out.reshape(C2 // C, C),
        ]
    )
    half = side // 2
    return (
        result.reshape(-1, half, half, C2),
        d_field + d_mixed.reshape(crops.shape),
        (d_kernel, d_vector, d_up, d_down, d_strided),
    )


def plain_body(big_crops, small_crops, big_cot, small_cot, drop_mask, *state):
    masters, moments, averages = state[0::3], state[1::3], state[2::3]
    axes = (1, 1, 1, 0, 0)
    full = [
        lax.all_gather(weight.astype(jnp.bfloat16), "dp", axis=axis, tiled=True)
        for weight, axis in zip(masters, axes)
    ]
    kernel, vector, up, down, strided = full
    values = vector.astype(jnp.float32)
    sections, rank = lax.axis_size("section"), lax.axis_index("section")
    micro_count = big_crops.shape[0]
    own = micro_count // sections

    def take(array):
        return lax.dynamic_slice_in_dim(array, rank * own, own, 0)

    keep = take(drop_mask).astype(jnp.float32) / KEEP_RATE
    outputs, grads, totals = [], [], None
    for crops, cot, images in ((big_crops, big_cot, BIG_IMG), (small_crops, small_cot, SMALL_IMG)):
        mine, my_cot = take(crops), take(cot)
        result, grad, parts = group_step(
            mine.reshape(-1, *crops.shape[2:]),
            my_cot.reshape(-1, *cot.shape[2:]),
            jnp.repeat(keep, images, axis=1).reshape(-1),
            kernel,
            values,
            up,
            down,
            strided,
        )
        outputs.append(result.reshape(my_cot.shape))
        grads.append(grad.reshape(mine.shape))
        totals = parts if totals is None else [a + b for a, b in zip(totals, parts)]
    pixel_total = (
        lax.axis_size("dp")
        * micro_count
        * (math.prod(big_crops.shape[1:4]) + math.prod(small_crops.shape[1:4]))
    )
    updates = []
    for position in range(5):
        gradient = lax.psum_scatter(totals[position], "dp", scatter_dimension=axes[position], tiled=True)
        gradient = lax.psum(gradient, "section")
        step_rate = RATES[position] * math.sqrt(FANS[position] / pixel_total)
        moment_next = MOMENTUM * moments[position] + gradient
        weight_next = masters[position] - step_rate * (gradient + MOMENTUM * moment_next)
        average_next = AVERAGING * averages[position] + (1.0 - AVERAGING) * weight_next
        updates += [weight_next, moment_next, average_next]
    return (*outputs, *grads, *updates)


UNIT = 4
MESH = pl.DeviceIdType.MESH
F32, BF16 = jnp.float32, jnp.bfloat16
BIG_SIDE, SMALL_SIDE = 14, 6
BIG_HALF, SMALL_HALF = 7, 3
BIG_ROWS = BIG_HALF * BIG_SIDE * 8
SMALL_ROWS = SMALL_HALF * SMALL_SIDE * 8
UNITS = 3
ROWS = BIG_ROWS + UNITS * SMALL_ROWS
HALO_BIG = (BIG_HALF + 6) * BIG_SIDE * 8
HALO_SMALL = (SMALL_HALF + 6) * SMALL_SIDE * 8
BLOCK_BIG = 7 * 32
BLOCKS = BLOCK_BIG + UNITS * 3 * 16
TILE = 304
CHUNK = C
PIECE = 48
PLANES = 4
COPIES = 118
UP_SCALE, DOWN_SCALE, STRIDED_SCALE = 1 / math.sqrt(C), 1 / math.sqrt(FF), 1 / math.sqrt(4 * C)
TAPS = KS * KS
V_BIAS_DW, V_GAIN_ONE, V_OFFSET_ONE, V_BIAS_UP = 0, 1, 2, 3
V_BIAS_DOWN, V_SCALE, V_GAIN_TWO, V_OFFSET_TWO, V_BIAS_OUT = 7, 8, 9, 10, 11


def nn(a, b):
    return jnp.dot(a, b, preferred_element_type=F32)


def rows_at(start, size):
    return pl.ds(aligned(start, 8), size)


def aligned(value, factor):
    return value if isinstance(value, int) else pl.multiple_of(value, factor)


def unrolled(count, step):
    for index in range(count):
        step(index, 0)


def one_hot(shape, target, valid=None):
    row = lax.broadcasted_iota(jnp.int32, shape, 0)
    column = lax.broadcasted_iota(jnp.int32, shape, 1)
    hit = column == target(row)
    if valid is not None:
        hit = hit & valid(row)
    return jnp.where(hit, 1.0, 0.0).astype(BF16)


def flat(value):
    return value.reshape(-1, value.shape[-1])


def step_kernel(
    big_hbm, small_hbm, big_cot_hbm, small_cot_hbm, keep_ref, kernel_ref, vector_ref, up_shard, down_shard, strided_shard,
    out_big_hbm, out_small_hbm, grad_big_hbm, grad_small_hbm, kv_out, up_out, down_out, strided_out,
    out_big_ref, out_small_ref, grad_big_ref, grad_small_ref,
    xb_raw, xs_raw, gb_raw, gs_raw, halo_big, halo_small, taps, vec, conv, rstd_one, normed,
    hidden, slope, branch, xhat, rstd_two, zeta, blocks, d_blocks, g_wide, g_rows, d_branch, d_pre,
    dhalo_big, dhalo_small, d_taps, d_vec, d_bias_up,
    kv_all, w_all, d_all, landing, plane_in, totals, line_in, final,
    d_kv, kv_part, kv_in, kv_sum,
    sems, send_sems, recv_sems,
):
    pad_big, d_zeta, d_normed, d_mixed = branch.at[0:896], dhalo_big.at[0:ROWS], zeta, xhat
    rank, dp_rank = lax.axis_index("section"), lax.axis_index("dp")
    row, column = rank // 2, lax.rem(rank, 2)
    line, core = dp_rank // 2, lax.rem(dp_rank, 2)
    flanks = (rank + 1 - 2 * column, rank + 2 - 4 * row, 3 - rank)
    twin = {"section": rank, "dp": dp_rank + 1 - 2 * core}

    def ahead(offset):
        return lax.rem(line + offset, PLANES)

    def on_line(offset):
        return {"section": rank, "dp": ahead(offset) * 2 + core}

    def on_plane(index):
        return {"section": flanks[index], "dp": dp_rank}

    barrier = pltpu.get_barrier_semaphore()
    def on_group(offset):
        return {"section": rank, "dp": lax.rem(dp_rank + offset, 8)}

    for target in [on_plane(index) for index in range(3)] + [on_group(offset) for offset in range(1, 8)]:
        pl.semaphore_signal(barrier, inc=1, device_id=target, device_id_type=MESH)

    made = []

    def plan(source, target_ref, target):
        index = len(made)
        copy = pltpu.make_async_remote_copy(
            source, target_ref, send_sems.at[index], recv_sems.at[index], device_id=target, device_id_type=MESH
        )
        made.append(copy)
        return copy

    def same(ref, target):
        return plan(ref, ref, target)

    def go(copies):
        for copy in copies:
            copy.start()

    def arrived(copies):
        for copy in copies:
            copy.wait_recv()

    def piece(index):
        return pl.ds(aligned(index * PIECE, 16), PIECE)

    offsets = (1, 2, 3)

    kv_ways = [same(kv_all.at[line, core], on_line(offset)) for offset in offsets]
    kv_twin = [same(kv_all.at[:, core], twin)]
    along, across, twins = [], [], []
    for weight in range(4):
        def part(offset, quarter):
            return w_all.at[weight, ahead(PLANES - offset), core, piece(quarter)]

        along.append([same(w_all.at[weight, line, core, piece(rank)], on_line(offset)) for offset in offsets])
        across.append([[same(part(offset, rank), on_plane(index)) for offset in offsets] for index in range(3)])
        twins.append([same(w_all.at[weight, :, core, piece(quarter)], twin) for quarter in (rank,) + flanks])

    def pass_line(weight):
        arrived(along[weight])
        for copies in across[weight]:
            go(copies)
        go(twins[weight][:1])

    def pass_plane(weight):
        for index, copies in enumerate(across[weight]):
            arrived(copies)
            go(twins[weight][1 + index : 2 + index])

    def held(weight):
        arrived(twins[weight])

    red_core, red_plane, red_line, red_back = [], [], [], []
    corners = ((row, 1 - column), (1 - row, column), (1 - row, 1 - column))
    for weight in range(4):
        red_core.append([plan(d_all.at[weight, :, 1 - core], landing.at[weight], twin)])
        red_plane.append(
            [
                plan(landing.at[weight, :, at_row, at_column], plane_in.at[weight, index], on_plane(index))
                for index, (at_row, at_column) in enumerate(corners)
            ]
        )
        red_line.append(
            [plan(totals.at[weight, ahead(offset)], line_in.at[weight, offset - 1], on_line(offset)) for offset in offsets]
        )
        red_back.append([same(final.at[weight, rank], on_plane(index)) for index in range(3)])

    def sum_core(weight):
        arrived(red_core[weight])

        def step(index, _):
            landing[weight, index] = (
                landing[weight, index].astype(F32) + d_all[weight, index, core].astype(F32)
            ).astype(BF16)
            return 0

        lax.fori_loop(0, PLANES, step, 0)
        go(red_plane[weight])

    def sum_plane(weight):
        arrived(red_plane[weight])
        for index in range(PLANES):
            total = landing[weight, index, row, column].astype(F32)
            for source in range(3):
                total = total + plane_in[weight, source, index].astype(F32)
            totals[weight, index] = total.astype(BF16)
        go(red_line[weight])

    def sum_line(weight):
        arrived(red_line[weight])
        total = totals[weight, line].astype(F32)
        for offset in offsets:
            total = total + line_in[weight, offset - 1].astype(F32)
        final[weight, rank] = total.astype(BF16)
        go(red_back[weight])

    kv_across = [
        plan(kv_part.at[lax.rem(dp_rank + offset, 8)], kv_in.at[offset - 1], on_group(offset)) for offset in range(1, 8)
    ]
    kv_back = [same(kv_sum.at[rank], on_plane(index)) for index in range(3)]

    def kv_sum_group():
        arrived(kv_across)
        total = kv_part[dp_rank].astype(F32)
        for index in range(7):
            total = total + kv_in[index].astype(F32)
        kv_sum[rank] = total
        go(kv_back)

    w_all[0, line, core] = up_shard[...].astype(BF16)
    w_all[1, line, core] = down_shard[...].astype(BF16)
    w_all[2, line, core] = strided_shard[:, :C].astype(BF16)
    w_all[3, line, core] = strided_shard[:, C:].astype(BF16)
    put_taps = one_hot((TAPS, 128), lambda r: r)
    put_vector = one_hot((13, 128), lambda r: r + 64)
    kv_all[line, core] = (
        nn(kernel_ref[...].astype(BF16), put_taps)
        + lax.dot_general(
            vector_ref[...].astype(BF16), put_vector, (((0,), (0,)), ((), ())), preferred_element_type=F32
        )
    ).astype(BF16)
    pl.semaphore_wait(barrier, 10)
    go(kv_ways)
    for weight in range(4):
        go(along[weight])

    def at_step(step, hooks):
        for when, event in hooks:
            pl.when(step == when)(event)

    def events(*calls):
        def run():
            for call, *arguments in calls:
                call(*arguments)

        return run

    own = pl.ds(rank * 2, 2)
    copies = [
        pltpu.make_async_copy(source, target, sems.at[index])
        for index, (source, target) in enumerate(
            (
                (big_hbm.at[own], xb_raw),
                (small_hbm, xs_raw),
                (big_cot_hbm.at[own], gb_raw),
                (small_cot_hbm, gs_raw),
            )
        )
    ]
    for copy in copies:
        copy.start()

    spread_big = one_hot((112, 128), lambda r: ((r >> 1) & 3) * 32 + (r >> 3) * 2 + (r & 1))
    spread_small = one_hot((48, 192), lambda r: ((r >> 1) & 3) * 48 + (r >> 3) * 8 + 2 * rank + (r & 1))
    gather_big = one_hot((128, 112), lambda r: ((r >> 1) & 15) * 8 + (r >> 5) * 2 + (r & 1))
    gather_small = one_hot((64, 48), lambda r: ((r >> 1) & 7) * 8 + (r >> 4) * 2 + (r & 1))
    block_big = one_hot(
        (128, 112), lambda r: (((r >> 1) & 7) * 2 + ((r >> 5) & 1)) * 8 + (r >> 6) * 4 + ((r >> 4) & 1) * 2 + (r & 1)
    )
    block_small = one_hot(
        (64, 48), lambda r: (((r >> 1) & 3) * 2 + ((r >> 4) & 1)) * 8 + (r >> 5) * 4 + ((r >> 3) & 1) * 2 + (r & 1)
    )
    pick_small = one_hot(
        (16, 48), lambda r: (r >> 3) * 24 + ((r >> 1) & 3) * 8 + 2 * rank + (r & 1), lambda r: (r & 7) < 6
    )
    sub = lax.broadcasted_iota(jnp.int32, (8, 128), 0)
    top = jnp.where(sub < 4, 1.0, 0.0).astype(F32)
    bottom = 1.0 - top

    def vector_row(index):
        return vec[index : index + 1, :]

    keep_zero = keep_ref[0, 2 * rank].astype(F32) / KEEP_RATE
    keep_one = keep_ref[0, 2 * rank + 1].astype(F32) / KEEP_RATE
    lane_wide = lambda value: jnp.concatenate([value] * 3, axis=1)
    big_factor = lane_wide(jnp.where((sub & 2) == 0, keep_zero, keep_one))
    small_factor = lane_wide(jnp.where((sub & 1) == 0, keep_zero, keep_one))

    pad_big[...] = jnp.zeros_like(pad_big)
    g_wide[...] = jnp.zeros_like(g_wide)

    for copy in copies:
        copy.wait()

    for micro in range(2):
        def put_big(h, _):
            pad_big[rows_at((micro * 14 + h) * 32, 28), :] = xb_raw[micro, h].astype(F32).reshape(28, C)
            return 0

        unrolled(14, put_big)
        for p in range(7):
            start = p * 32 + micro * 16
            g_wide[start : start + 14, :] = gb_raw[micro, p].astype(F32).reshape(14, C2)
    for unit in range(UNITS):
        for p in range(3):
            source = jnp.concatenate(
                [gs_raw[2 * unit + crop, p].astype(F32).reshape(24, C2) for crop in range(2)], axis=0
            )
            start = BLOCK_BIG + (unit * 3 + p) * 16
            g_wide[start : start + 16, :] = nn(pick_small, source.astype(BF16))

    arrived(kv_ways)
    go(kv_twin)

    def spread_rows(hh, _):
        tiles = [pad_big[rows_at((micro * 14 + half * 7 + hh) * 32, 32), :] for half in range(2) for micro in range(2)]
        source = jnp.concatenate(tiles, axis=0).astype(BF16)
        halo_big[rows_at((hh + 3) * 112, 112), :] = nn(spread_big, source)
        return 0

    unrolled(BIG_HALF, spread_rows)
    for unit in range(UNITS):
        def spread_unit(hh, _):
            tiles = [
                xs_raw[2 * unit + crop, half * 3 + hh].reshape(48, C) for half in range(2) for crop in range(2)
            ]
            source = jnp.concatenate(tiles, axis=0)
            halo_small[rows_at(unit * HALO_SMALL + (hh + 3) * 48, 48), :] = nn(spread_small, source)
            return 0

        unrolled(SMALL_HALF, spread_unit)

    def halos(ref, base, half, side):
        def step(index, _):
            for lane in range(3):
                lanes = slice(lane * 128, lane * 128 + 128)
                low = ref[rows_at(base + (3 * side + index) * 8, 8), lanes]
                ref[rows_at(base + ((3 + half) * side + index) * 8, 8), lanes] = pltpu.roll(low, 4, 0) * top
                high = ref[rows_at(base + (half * side + index) * 8, 8), lanes]
                ref[rows_at(base + index * 8, 8), lanes] = pltpu.roll(high, 4, 0) * bottom
            return 0

        unrolled(3 * side, step)

    def all_halos(big, small):
        halos(big, 0, BIG_HALF, BIG_SIDE)
        for unit in range(UNITS):
            halos(small, unit * HALO_SMALL, SMALL_HALF, SMALL_SIDE)

    all_halos(halo_big, halo_small)

    arrived(kv_twin)
    kv = jnp.transpose(flat(kv_all[...]).astype(F32))
    vec[...] = kv[64:80]
    for tap in range(TAPS):
        taps[tap] = jnp.broadcast_to(kv[tap : tap + 1] * (1.0 / KS), (8, C))

    def convolve(big, small, mirrored, finish, hooks):
        def tap_at(i, j, lanes):
            index = i * KS + j
            return taps[TAPS - 1 - index if mirrored else index, :, lanes]

        def image_row(step, _):
            h, lane = step // 3, lax.rem(step, 3)
            lanes = pl.ds(aligned(lane * 128, 128), 128)
            sums = [None] * BIG_SIDE
            for i in range(KS):
                values = [big[rows_at(((h + i) * BIG_SIDE + w) * 8, 8), lanes] for w in range(BIG_SIDE)]
                for j in range(KS):
                    weight = tap_at(i, j, lanes)
                    for w in range(max(0, 3 - j), min(BIG_SIDE, BIG_SIDE + 3 - j)):
                        term = values[w + j - 3] * weight
                        sums[w] = term if sums[w] is None else sums[w] + term
            for w in range(BIG_SIDE):
                finish((h * BIG_SIDE + w) * 8, sums[w], lanes)
            at_step(step, hooks)
            return 0

        lax.fori_loop(0, BIG_HALF * 3, image_row, 0)

        def small_row(step, _):
            h, lane = step // 3, lax.rem(step, 3)
            lanes = pl.ds(aligned(lane * 128, 128), 128)
            sums = [[None] * SMALL_SIDE for _ in range(UNITS)]
            for i in range(KS):
                values = [
                    [
                        small[rows_at(unit * HALO_SMALL + ((h + i) * SMALL_SIDE + w) * 8, 8), lanes]
                        for w in range(SMALL_SIDE)
                    ]
                    for unit in range(UNITS)
                ]
                for j in range(KS):
                    weight = tap_at(i, j, lanes)
                    for w in range(max(0, 3 - j), min(SMALL_SIDE, SMALL_SIDE + 3 - j)):
                        for unit in range(UNITS):
                            term = values[unit][w + j - 3] * weight
                            old = sums[unit][w]
                            sums[unit][w] = term if old is None else old + term
            for unit in range(UNITS):
                for w in range(SMALL_SIDE):
                    finish(BIG_ROWS + unit * SMALL_ROWS + (h * SMALL_SIDE + w) * 8, sums[unit][w], lanes)
            return 0

        lax.fori_loop(0, SMALL_HALF * 3, small_row, 0)

    def keep_conv(start, value, lanes):
        conv[rows_at(start, 8), lanes] = value

    convolve(halo_big, halo_small, False, keep_conv, [(3, events((pass_line, 0))), (20, events((pass_line, 1)))])
    pass_plane(0)

    def for_tiles(run):
        def big_tile(index, _):
            run(index * 112, 112, big_factor, halo_big, dhalo_big, 336 + index * 112)
            return 0

        unrolled(BIG_HALF, big_tile)

        def small_tile(index, _):
            run(BIG_ROWS + index * 144, 144, small_factor, halo_small, dhalo_small, index * HALO_SMALL + 144)
            return 0

        unrolled(UNITS, small_tile)

    def fold(value):
        return jnp.sum(value.reshape(-1, 8, value.shape[-1]), axis=0)

    def mean_of(value):
        return jnp.sum(value, axis=-1, keepdims=True) * (1.0 / C)

    def wide(ref, rows):
        value = ref[rows, :]
        return jnp.concatenate([value, value, value], axis=1)

    def norm_one(start, size, *_):
        rows = rows_at(start, size)
        value = conv[rows, :] + vector_row(V_BIAS_DW)
        centered = value - mean_of(value)
        scale = lax.rsqrt(mean_of(centered * centered) + EPSILON)
        unit = centered * scale
        conv[rows, :] = unit
        rstd_one[rows, :] = jnp.broadcast_to(scale, (size, 128))
        normed[pl.ds(aligned(start, 16), size), :] = (
            unit * vector_row(V_GAIN_ONE) + vector_row(V_OFFSET_ONE)
        ).astype(BF16)

    for_tiles(norm_one)
    pass_line(2)

    def up_tile(index, _):
        rows = pl.ds(aligned(index * TILE, 16), TILE)
        left = normed[rows, :]
        for chunk in range(FF // CHUNK):
            span = slice(chunk * CHUNK, (chunk + 1) * CHUNK)
            bias = vector_row(V_BIAS_UP + chunk)
            pre = (
                lax.dot_general(left, flat(w_all[0, chunk]), (((1,), (1,)), ((), ())), preferred_element_type=F32)
                * UP_SCALE
                + bias
            )
            scaled_pre = pre * math.sqrt(0.5)
            whole = 0.5 + 0.5 * lax.erf(scaled_pre)
            density = jnp.exp2(scaled_pre * scaled_pre * -math.log2(math.e))
            hidden[rows, span] = (pre * whole).astype(BF16)
            slope[rows, span] = whole + pre * density * (1.0 / math.sqrt(2.0 * math.pi))
        at_step(index, [(0, events((pass_line, 3))), (2, events((pass_plane, 1)))])
        return 0

    held(0)
    lax.fori_loop(0, ROWS // TILE, up_tile, 0)
    held(1)

    def branch_tile(index, _):
        rows = pl.ds(aligned(index * TILE, 16), TILE)
        branch[rows, :] = nn(hidden[rows, :], flat(w_all[1])) * DOWN_SCALE + vector_row(V_BIAS_DOWN)
        return 0

    lax.fori_loop(0, ROWS // TILE, branch_tile, 0)

    def scaled(value, factor):
        return (value.reshape(-1, 8, C) * factor[None]).reshape(-1, C)

    def norm_two(start, size, factor, field, _, offset):
        rows = rows_at(start, size)
        value = field[rows_at(offset, size), :] + scaled(vector_row(V_SCALE) * branch[rows, :], factor)
        centered = value - mean_of(value)
        scale = lax.rsqrt(mean_of(centered * centered) + EPSILON)
        unit = centered * scale
        xhat[rows, :] = unit
        rstd_two[rows, :] = jnp.broadcast_to(scale, (size, 128))
        zeta[pl.ds(aligned(start, 16), size), :] = (
            unit * vector_row(V_GAIN_TWO) + vector_row(V_OFFSET_TWO)
        ).astype(BF16)

    for_tiles(norm_two)

    def block_spans(base, count, hh, half_side):
        for half in range(2):
            h = half * half_side + hh
            p, a = h // 2, h % 2
            for b in range(2):
                yield (
                    pl.ds(aligned(base + p * count, 16), count),
                    pl.ds(aligned((2 * a + b) * C, 128), C),
                )

    def block_rows(source, matrix, base, count, hh, half_side):
        picked = nn(matrix, source).astype(BF16)
        for index, span in enumerate(block_spans(base, count, hh, half_side)):
            blocks[span] = picked[index * count : (index + 1) * count]

    def big_blocks(hh, _):
        block_rows(zeta[pl.ds(aligned(hh * 112, 16), 112), :], block_big, 0, 32, hh, 7)
        return 0

    unrolled(BIG_HALF, big_blocks)
    for unit in range(UNITS):
        def small_blocks(hh, _):
            source = zeta[pl.ds(aligned(BIG_ROWS + unit * SMALL_ROWS + hh * 48, 16), 48), :]
            block_rows(source, block_small, BLOCK_BIG + unit * 48, 16, hh, 3)
            return 0

        unrolled(SMALL_HALF, small_blocks)

    g_rows[...] = g_wide[...].astype(BF16)
    bias_out_grad = jnp.sum(g_wide[...], axis=0, keepdims=True)
    d_vec[V_BIAS_OUT, 0:1, :] = bias_out_grad[:, :C]
    d_vec[V_BIAS_OUT + 1, 0:1, :] = bias_out_grad[:, C:]

    def outer(left, right, scale):
        product = lax.dot_general(left, right, (((0,), (0,)), ((), ())), preferred_element_type=F32)
        return (product * scale).astype(BF16).reshape(2, 2, 2, PIECE, C)

    for half in range(2):
        def strided_grad(index, _):
            span = pl.ds(aligned(index * C, 128), C)
            d_all[2 + half, index] = outer(blocks[:, span], g_rows[:, half * C : half * C + C], STRIDED_SCALE)
            return 0

        unrolled(4, strided_grad)
        go(red_core[2 + half])
        if half == 0:
            pass_plane(2)

    bias_out = jnp.concatenate([vector_row(V_BIAS_OUT), vector_row(V_BIAS_OUT + 1)], axis=1)

    def out_half(half):
        span = slice(half * C, half * C + C)
        g_wide[:, span] = nn(blocks[...], flat(w_all[2 + half])) * STRIDED_SCALE + bias_out[:, span]

    held(2)
    out_half(0)
    pass_plane(3)
    held(3)

    def block_grad(index, _):
        span = pl.ds(aligned(index * 384, 128), 384)
        total = None
        for half in range(2):
            term = lax.dot_general(
                g_rows[:, half * C : half * C + C],
                flat(w_all[2 + half, index]),
                (((1,), (1,)), ((), ())),
                preferred_element_type=F32,
            )
            total = term if total is None else total + term
        d_blocks[:, span] = (total * STRIDED_SCALE).astype(BF16)
        return 0

    unrolled(4, block_grad)

    def unblock(matrix, base, count, hh, half_side):
        parts = jnp.concatenate([d_blocks[span] for span in block_spans(base, count, hh, half_side)], axis=0)
        return lax.dot_general(matrix, parts, (((0,), (0,)), ((), ())), preferred_element_type=F32)

    def big_unblock(hh, _):
        d_zeta[rows_at(hh * 112, 112), :] = unblock(block_big, 0, 32, hh, 7)
        return 0

    unrolled(BIG_HALF, big_unblock)
    for unit in range(UNITS):
        def small_unblock(hh, _):
            d_zeta[rows_at(BIG_ROWS + unit * SMALL_ROWS + hh * 48, 48), :] = unblock(
                block_small, BLOCK_BIG + unit * 48, 16, hh, 3
            )
            return 0

        unrolled(SMALL_HALF, small_unblock)

    sum_core(2)

    for index in range(11):
        d_vec[index] = jnp.zeros((8, C), F32)

    def norm_two_back(start, size, factor, *_):
        rows = rows_at(start, size)
        unit = xhat[rows, :]
        grad = d_zeta[rows, :]
        d_vec[V_GAIN_TWO] += fold(grad * unit)
        d_vec[V_OFFSET_TWO] += fold(grad)
        inner = grad * vector_row(V_GAIN_TWO)
        mixed = (inner - mean_of(inner) - unit * mean_of(inner * unit)) * wide(rstd_two, rows)
        d_mixed[rows, :] = mixed
        kept = scaled(mixed, factor)
        d_vec[V_SCALE] += fold(kept * branch[rows, :])
        lowered = (kept * vector_row(V_SCALE)).astype(BF16)
        d_branch[pl.ds(aligned(start, 16), size), :] = lowered
        d_vec[V_BIAS_DOWN] += fold(lowered.astype(F32))

    for_tiles(norm_two_back)
    sum_core(3)

    def down_grad(index, _):
        span = pl.ds(aligned(index * C, 128), C)
        d_all[1, index] = outer(hidden[:, span], d_branch[...], DOWN_SCALE)
        return 0

    unrolled(4, down_grad)
    go(red_core[1])

    d_bias_up[...] = jnp.zeros_like(d_bias_up)

    def down_tile(index, _):
        rows = pl.ds(aligned(index * TILE, 16), TILE)
        left = d_branch[rows, :]
        for chunk in range(FF // CHUNK):
            span = slice(chunk * CHUNK, (chunk + 1) * CHUNK)
            d_hidden = (
                lax.dot_general(left, flat(w_all[1, chunk]), (((1,), (1,)), ((), ())), preferred_element_type=F32)
                * DOWN_SCALE
            )
            lowered = (d_hidden * slope[rows, span]).astype(BF16)
            d_pre[rows, span] = lowered
            d_bias_up[:, span] += fold(lowered.astype(F32))
        d_normed[rows, :] = (nn(d_pre[rows, :], flat(w_all[0])) * UP_SCALE).astype(BF16)
        at_step(index, [(2, events((sum_core, 1))), (3, events((sum_plane, 2)))])
        return 0

    lax.fori_loop(0, ROWS // TILE, down_tile, 0)

    def up_grad(index, _):
        span = pl.ds(aligned(index * C, 128), C)
        d_all[0, index] = outer(d_pre[:, span], normed[...], UP_SCALE)
        return 0

    unrolled(4, up_grad)
    go(red_core[0])

    def norm_one_back(start, size, _, __, target, offset):
        rows = rows_at(start, size)
        unit = conv[rows, :]
        grad = d_normed[pl.ds(aligned(start, 16), size), :].astype(F32)
        d_vec[V_GAIN_ONE] += fold(grad * unit)
        d_vec[V_OFFSET_ONE] += fold(grad)
        inner = grad * vector_row(V_GAIN_ONE)
        result = (inner - mean_of(inner) - unit * mean_of(inner * unit)) * wide(rstd_one, rows)
        d_vec[V_BIAS_DW] += fold(result)
        target[rows_at(offset, size), :] = result

    for_tiles(norm_one_back)
    all_halos(dhalo_big, dhalo_small)

    def tap_grads(step, _):
        i, lane = step // 3, lax.rem(step, 3)
        lanes = pl.ds(aligned(lane * 128, 128), 128)

        sums = [[None, None] for _ in range(KS)]

        def image_row(side, field, grad, field_base, grad_base, turn):
            inputs = [field[rows_at(field_base + w * 8, 8), lanes] for w in range(side)]
            outer = [grad[rows_at(grad_base + w * 8, 8), lanes] for w in range(side)]
            for w in range(side):
                for j in range(max(0, 3 - w), min(KS, side + 3 - w)):
                    term = inputs[w + j - 3] * outer[w]
                    slot = (w + turn) % 2
                    old = sums[j][slot]
                    sums[j][slot] = term if old is None else old + term

        for h in range(BIG_HALF):
            image_row(BIG_SIDE, halo_big, dhalo_big, (h + i) * 112, (h + 3) * 112, h)
        for h in range(SMALL_HALF):
            for unit in range(UNITS):
                base = unit * HALO_SMALL
                image_row(SMALL_SIDE, halo_small, dhalo_small, base + (h + i) * 48, base + (h + 3) * 48, h)
        for j in range(KS):
            d_taps[i * KS + j, :, lanes] = sums[j][0] + sums[j][1]
        at_step(
            step,
            [
                (3, events((sum_plane, 3))),
                (5, events((sum_core, 0))),
                (7, events((sum_line, 2))),
                (16, events((sum_line, 3))),
                (19, events((sum_plane, 1))),
            ],
        )
        return 0

    lax.fori_loop(0, KS * 3, tap_grads, 0)

    d_kv[56:128, :] = jnp.zeros((72, C), F32)
    for tap in range(TAPS):
        d_kv[tap : tap + 1, :] = jnp.sum(d_taps[tap], axis=0, keepdims=True) * (1.0 / KS)
    for index in range(11):
        if V_BIAS_UP <= index < V_BIAS_UP + UP_ROWS:
            continue
        d_kv[TAPS + index : TAPS + index + 1, :] = jnp.sum(d_vec[index], axis=0, keepdims=True)
    d_kv[TAPS + V_BIAS_OUT : TAPS + V_BIAS_OUT + 1, :] = d_vec[V_BIAS_OUT, 0:1, :]
    d_kv[TAPS + V_BIAS_OUT + 1 : TAPS + V_BIAS_OUT + 2, :] = d_vec[V_BIAS_OUT + 1, 0:1, :]
    bias_up_grad = jnp.sum(d_bias_up[...], axis=0, keepdims=True)
    for index in range(UP_ROWS):
        d_kv[TAPS + V_BIAS_UP + index : TAPS + V_BIAS_UP + index + 1, :] = bias_up_grad[
            :, index * C : (index + 1) * C
        ]

    kv_part[...] = jnp.transpose(d_kv[...]).astype(BF16).reshape(8, PIECE, 128)
    go(kv_across)

    def add_grad(start, value, lanes):
        d_mixed[rows_at(start, 8), lanes] += value

    convolve(
        dhalo_big,
        dhalo_small,
        True,
        add_grad,
        [
            (14, events((sum_line, 1), (kv_sum_group,))),
            (18, events((sum_plane, 0))),
        ],
    )
    out_half(1)
    for micro in range(2):
        for p in range(7):
            start = p * 32 + micro * 16
            out_big_ref[micro, p] = g_wide[start : start + 14, :].reshape(7, 2, C2)
    for unit in range(UNITS):
        for p in range(3):
            for crop in range(2):
                start = BLOCK_BIG + (unit * 3 + p) * 16 + crop * 8
                out_small_ref[2 * unit + crop, p] = g_wide[start : start + 6, :].reshape(3, 2, C2)


    sum_line(0)

    def restore(matrix, value):
        high = value.astype(BF16)
        low = (value - high.astype(F32)).astype(BF16)
        return nn(matrix, high) + nn(matrix, low)

    def grad_rows(hh, _):
        natural = restore(gather_big, d_mixed[rows_at(hh * 112, 112), :])
        for half in range(2):
            for micro in range(2):
                start = (half * 2 + micro) * 32
                grad_big_ref[micro, half * 7 + hh] = natural[start : start + 28].reshape(14, 2, C)
        return 0

    unrolled(BIG_HALF, grad_rows)
    for unit in range(UNITS):
        def small_grad_rows(hh, _):
            natural = restore(gather_small, d_mixed[rows_at(BIG_ROWS + unit * SMALL_ROWS + hh * 48, 48), :])
            for half in range(2):
                for crop in range(2):
                    start = (half * 2 + crop) * 16
                    grad_small_ref[2 * unit + crop, half * 3 + hh] = natural[start : start + 12].reshape(6, 2, C)
            return 0

        unrolled(SMALL_HALF, small_grad_rows)

    leaving = [
        pltpu.make_async_copy(source, target, sems.at[4 + index])
        for index, (source, target) in enumerate(
            (
                (out_big_ref, out_big_hbm),
                (out_small_ref, out_small_hbm),
                (grad_big_ref, grad_big_hbm),
                (grad_small_ref, grad_small_hbm),
            )
        )
    ]
    for copy in leaving:
        copy.start()
    for weight in range(4):
        arrived(red_back[weight])
    up_out[...] = flat(final[0])
    down_out[...] = flat(final[1])
    strided_out[:, :C] = flat(final[2])
    strided_out[:, C:] = flat(final[3])
    arrived(kv_back)
    kv_out[...] = kv_sum[0] + kv_sum[1] + kv_sum[2] + kv_sum[3]
    for copy in made:
        copy.wait_send()
    for copy in leaving:
        copy.wait()


def finish_kernel(rates, *refs):
    sources, outs, held, fresh, sems = refs[:23], refs[23:42], refs[42:65], refs[65:80], refs[80]
    inward = [pltpu.make_async_copy(source, target, sems.at[index]) for index, (source, target) in enumerate(zip(sources, held))]
    outward = [
        pltpu.make_async_copy(source, target, sems.at[23 + index])
        for index, (source, target) in enumerate(zip((*held[19:], *fresh), outs))
    ]
    order = (4, 3, 2, 1, 0)
    for index in (19, 21):
        inward[index].start()
    for position in order:
        if position:
            inward[position - 1].start()
        for index in range(4 + 3 * position, 7 + 3 * position):
            inward[index].start()
    for index in (20, 22):
        inward[index].start()
    for index in (19, 21):
        inward[index].wait()
        outward[index - 19].start()
    for position in order:
        state = range(4 + 3 * position, 7 + 3 * position)
        for index in state:
            inward[index].wait()
        if position >= 2:
            inward[position - 1].wait()
            gradient = held[position - 1][...].astype(F32)
        elif position == 1:
            inward[0].wait()
            gradient = jnp.transpose(held[0][...])[TAPS : TAPS + 13]
        else:
            gradient = held[0][:, :TAPS]
        weight, moment, average = (held[index][...] for index in state)
        moment_next = MOMENTUM * moment + gradient
        weight_next = weight - rates[position] * (gradient + MOMENTUM * moment_next)
        results = (weight_next, moment_next, AVERAGING * average + (1.0 - AVERAGING) * weight_next)
        for index, value in enumerate(results):
            fresh[3 * position + index][...] = value
            outward[4 + 3 * position + index].start()
    for index in (20, 22):
        inward[index].wait()
        outward[index - 19].start()
    for copy in outward:
        copy.wait()


def finish(rates, grads, state, images):
    any_spec = pl.BlockSpec(memory_space=pl.ANY)
    inputs = (*grads, *state, *images)
    return pl.pallas_call(
        functools.partial(finish_kernel, rates),
        out_shape=[jax.ShapeDtypeStruct(array.shape, F32) for array in (*images, *state)],
        in_specs=[any_spec] * 23,
        out_specs=[any_spec] * 19,
        scratch_shapes=[pltpu.VMEM(array.shape, array.dtype) for array in inputs]
        + [pltpu.VMEM(array.shape, F32) for array in state]
        + [pltpu.SemaphoreType.DMA((42,))],
        compiler_params=pltpu.CompilerParams(vmem_limit_bytes=(63 << 20) + (1 << 19)),
    )(*inputs)


def fused_step(big_crops, small_crops, big_cot, small_cot, keep, kernel_t, vector, up_t, down, strided):
    any_spec = pl.BlockSpec(memory_space=pl.ANY)
    vmem = pl.BlockSpec(memory_space=pltpu.VMEM)
    shape = jax.ShapeDtypeStruct
    big_order, small_order = (0, 2, 3, 1, 4), (1, 2, 3, 0, 4)
    results = pl.pallas_call(
        step_kernel,
        out_shape=(
            shape((2, 7, 7, 2, C2), F32),
            shape((6, 3, 3, 2, C2), F32),
            shape((2, 14, 14, 2, C), F32),
            shape((6, 6, 6, 2, C), F32),
            shape((PIECE, 128), F32),
            shape((192, C), BF16),
            shape((192, C), BF16),
            shape((192, C2), BF16),
        ),
        in_specs=[any_spec] * 4 + [pl.BlockSpec(memory_space=pltpu.SMEM)] + [vmem] * 5,
        out_specs=[any_spec] * 4 + [vmem] * 4,
        scratch_shapes=[
            pltpu.VMEM((2, 7, 7, 2, C2), F32),
            pltpu.VMEM((6, 3, 3, 2, C2), F32),
            pltpu.VMEM((2, 14, 14, 2, C), F32),
            pltpu.VMEM((6, 6, 6, 2, C), F32),
            pltpu.VMEM((2, 14, 14, 2, C), BF16),
            pltpu.VMEM((6, 6, 6, 8, C), BF16),
            pltpu.VMEM((2, 7, 7, 2, C2), BF16),
            pltpu.VMEM((6, 3, 3, 8, C2), BF16),
            pltpu.VMEM((HALO_BIG, C), F32),
            pltpu.VMEM((UNITS * HALO_SMALL, C), F32),
            pltpu.VMEM((TAPS, 8, C), F32),
            pltpu.VMEM((16, C), F32),
            pltpu.VMEM((ROWS, C), F32),
            pltpu.VMEM((ROWS, 128), F32),
            pltpu.VMEM((ROWS, C), BF16),
            pltpu.VMEM((ROWS, FF), BF16),
            pltpu.VMEM((ROWS, FF), F32),
            pltpu.VMEM((ROWS, C), F32),
            pltpu.VMEM((ROWS, C), F32),
            pltpu.VMEM((ROWS, 128), F32),
            pltpu.VMEM((ROWS, C), BF16),
            pltpu.VMEM((BLOCKS, 4 * C), BF16),
            pltpu.VMEM((BLOCKS, 4 * C), BF16),
            pltpu.VMEM((BLOCKS, C2), F32),
            pltpu.VMEM((BLOCKS, C2), BF16),
            pltpu.VMEM((ROWS, C), BF16),
            pltpu.VMEM((ROWS, FF), BF16),
            pltpu.VMEM((HALO_BIG, C), F32),
            pltpu.VMEM((UNITS * HALO_SMALL, C), F32),
            pltpu.VMEM((TAPS, 8, C), F32),
            pltpu.VMEM((13, 8, C), F32),
            pltpu.VMEM((8, FF), F32),
            pltpu.VMEM((4, 2, 48, 128), BF16),
            pltpu.VMEM((4, 4, 2, 192, C), BF16),
            pltpu.VMEM((4, 4, 2, 2, 2, PIECE, C), BF16),
            pltpu.VMEM((4, 4, 2, 2, PIECE, C), BF16),
            pltpu.VMEM((4, 3, 4, PIECE, C), BF16),
            pltpu.VMEM((4, 4, PIECE, C), BF16),
            pltpu.VMEM((4, 3, PIECE, C), BF16),
            pltpu.VMEM((4, 4, PIECE, C), BF16),
            pltpu.VMEM((128, C), F32),
            pltpu.VMEM((8, PIECE, 128), BF16),
            pltpu.VMEM((7, PIECE, 128), BF16),
            pltpu.VMEM((4, PIECE, 128), F32),
            pltpu.SemaphoreType.DMA((8,)),
            pltpu.SemaphoreType.DMA((COPIES,)),
            pltpu.SemaphoreType.DMA((COPIES,)),
        ],
        compiler_params=pltpu.CompilerParams(vmem_limit_bytes=(63 << 20) + (1 << 19), collective_id=0, has_side_effects=True),
    )(
        big_crops.transpose(big_order),
        small_crops.transpose(small_order),
        big_cot.transpose(big_order),
        small_cot.transpose(small_order),
        keep,
        kernel_t,
        vector,
        up_t,
        down,
        strided,
    )
    return results[4:], results[:4]


def body(big_crops, small_crops, big_cot, small_cot, drop_mask, *state):
    sections, rank = lax.axis_size("section"), lax.axis_index("section")
    micro_count = big_crops.shape[0]
    fits = (
        micro_count == 2 * sections
        and big_crops.shape[1:] == (BIG_IMG, BIG_SIDE, BIG_SIDE, C)
        and small_crops.shape[1:] == (SMALL_IMG, SMALL_SIDE, SMALL_SIDE, C)
        and drop_mask.shape[1] == 1
        and (sections, lax.axis_size("dp")) == (4, 8)
    )
    if not fits:
        return plain_body(big_crops, small_crops, big_cot, small_cot, drop_mask, *state)
    masters, moments, averages = state[0::3], state[1::3], state[2::3]
    turned = (True, False, True, False, False)
    masters, moments, averages = (
        [jnp.transpose(array) if turn else array for array, turn in zip(group, turned)]
        for group in (masters, moments, averages)
    )
    grads, images = fused_step(big_crops, small_crops, big_cot, small_cot, drop_mask.T, *masters)
    pixel_total = (
        lax.axis_size("dp")
        * micro_count
        * (math.prod(big_crops.shape[1:4]) + math.prod(small_crops.shape[1:4]))
    )
    rates = tuple(rate * math.sqrt(fan / pixel_total) for rate, fan in zip(RATES, FANS))
    state = [array for group in zip(masters, moments, averages) for array in group]
    results = finish(rates, grads, state, images)
    order_big, order_small = (0, 3, 1, 2, 4), (3, 0, 1, 2, 4)
    return (
        results[0].transpose(order_big),
        results[1].transpose(order_small),
        results[2].transpose(order_big),
        results[3].transpose(order_small),
        *(array.T if turned[index // 3] else array for index, array in enumerate(results[4:])),
    )


def solution(mesh):
    crops = P(None, "dp", None, None, None)
    owned = P("section", "dp", None, None, None)
    weights = (P(None, "dp"),) * 9 + (P("dp", None),) * 6
    return jax.shard_map(
        body,
        mesh=mesh,
        in_specs=(crops,) * 4 + (P(None, "dp"),) + weights,
        out_specs=(owned,) * 4 + weights,
        check_vma=False,
    )
```

```python
import functools
import math

import jax
import jax.numpy as jnp
from jax import lax
from jax.experimental import pallas as pl
from jax.experimental.pallas import tpu as pltpu
from jax.sharding import PartitionSpec as P

C = 384
FF = 1536
C2 = 768
KS = 7
BIG_IMG = 2
SMALL_IMG = 6

KEEP_RATE = 0.9
MOMENTUM = 0.5
AVERAGING = 0.5
EPSILON = 1e-06
RATES = (1.1, 0.4, 2.7, 1.3, 1.3)
FANS = (KS * KS, 1, C, FF, 4 * C)
UP_ROWS = FF // C


def layer_norm(values, gain_row, offset_row):
    average = jnp.mean(values, axis=-1, keepdims=True)
    centered = values - average
    variance = jnp.mean(centered * centered, axis=-1, keepdims=True)
    return centered * lax.rsqrt(variance + EPSILON) * gain_row + offset_row


def depthwise(field, kernel, precision):
    radius = KS // 2
    channels = field.shape[-1]
    return lax.conv_general_dilated(
        field,
        kernel.reshape(KS, KS, 1, channels),
        (1, 1),
        ((radius, radius), (radius, radius)),
        dimension_numbers=("NHWC", "HWIO", "NHWC"),
        feature_group_count=channels,
        precision=precision,
        preferred_element_type=jnp.float32,
    )


def to_blocks(field):
    count, side = field.shape[0], field.shape[1]
    half = side // 2
    return (
        field.reshape(count, half, 2, half, 2, C)
        .transpose(0, 1, 3, 2, 4, 5)
        .reshape(count * half * half, 4 * C)
    )


def from_blocks(flat, shape):
    count, half = shape[0], shape[1] // 2
    return flat.reshape(count, half, half, 2, 2, C).transpose(0, 1, 3, 2, 4, 5).reshape(shape)


def contract(left, right):
    return lax.dot_general(left, right, (((0,), (0,)), ((), ())), preferred_element_type=jnp.float32)


def dot_t(left, right):
    return lax.dot_general(left, right, (((1,), (1,)), ((), ())), preferred_element_type=jnp.float32)


def group_step(crops, cot, keep, kernel, values, up, down, strided):
    bias_dw, gain_one, offset_one = values[0], values[1], values[2]
    bias_up = values[3 : 3 + UP_ROWS].reshape(FF)
    bias_down, layer_scale = values[3 + UP_ROWS], values[4 + UP_ROWS]
    gain_two, offset_two = values[5 + UP_ROWS], values[6 + UP_ROWS]
    bias_out = values[7 + UP_ROWS :].reshape(C2)
    up_scale, down_scale, strided_scale = 1 / math.sqrt(C), 1 / math.sqrt(FF), 1 / math.sqrt(4 * C)
    side = crops.shape[1]
    factor = jnp.repeat(keep, side * side)[:, None]
    field = crops.astype(jnp.float32)

    def first(field_value, kernel_value, bias, gain, offset):
        conv_out = depthwise(field_value, kernel_value, None) * (1.0 / KS) + bias
        return layer_norm(conv_out, gain, offset)

    normed, first_pull = jax.vjp(first, field, kernel.astype(jnp.float32), bias_dw, gain_one, offset_one)
    rows = normed.astype(jnp.bfloat16).reshape(-1, C)
    pre_act = jnp.dot(rows, up, preferred_element_type=jnp.float32) * up_scale + bias_up
    phi_big = 0.5 * (1.0 + lax.erf(pre_act * math.sqrt(0.5)))
    density = jnp.exp(-0.5 * pre_act * pre_act) * (1.0 / math.sqrt(2.0 * math.pi))
    slope = phi_big + pre_act * density
    hidden = (pre_act * phi_big).astype(jnp.bfloat16)
    branch = jnp.dot(hidden, down, preferred_element_type=jnp.float32) * down_scale + bias_down
    mixed = field.reshape(-1, C) + layer_scale * branch * factor
    zeta, norm_pull = jax.vjp(layer_norm, mixed, gain_two, offset_two)
    blocks = to_blocks(zeta.astype(jnp.bfloat16).reshape(crops.shape))
    result = jnp.dot(blocks, strided, preferred_element_type=jnp.float32) * strided_scale + bias_out

    grad_out = cot.reshape(-1, C2)
    d_strided = contract(blocks, grad_out) * strided_scale
    d_bias_out = jnp.sum(grad_out.astype(jnp.float32), axis=0)
    d_blocks = dot_t(grad_out, strided) * strided_scale
    d_zeta = from_blocks(d_blocks.astype(jnp.bfloat16), crops.shape).reshape(-1, C)
    d_mixed, d_gain_two, d_offset_two = norm_pull(d_zeta.astype(jnp.float32))
    d_scale = jnp.sum(d_mixed * factor * branch, axis=0)
    d_branch = (d_mixed * factor * layer_scale).astype(jnp.bfloat16)
    d_bias_down = jnp.sum(d_branch.astype(jnp.float32), axis=0)
    d_down = contract(hidden, d_branch) * down_scale
    d_pre = (dot_t(d_branch, down) * down_scale * slope).astype(jnp.bfloat16)
    d_bias_up = jnp.sum(d_pre.astype(jnp.float32), axis=0)
    d_up = contract(rows, d_pre) * up_scale
    d_normed = (dot_t(d_pre, up) * up_scale).astype(jnp.bfloat16).reshape(crops.shape)
    d_field, d_kernel, d_bias_dw, d_gain_one, d_offset_one = first_pull(d_normed.astype(jnp.float32))
    d_vector = jnp.concatenate(
        [
            d_bias_dw[None],
            d_gain_one[None],
            d_offset_one[None],
            d_bias_up.reshape(UP_ROWS, C),
            d_bias_down[None],
            d_scale[None],
            d_gain_two[None],
            d_offset_two[None],
            d_bias_out.reshape(C2 // C, C),
        ]
    )
    half = side // 2
    return (
        result.reshape(-1, half, half, C2),
        d_field + d_mixed.reshape(crops.shape),
        (d_kernel, d_vector, d_up, d_down, d_strided),
    )


def plain_body(big_crops, small_crops, big_cot, small_cot, drop_mask, *state):
    masters, moments, averages = state[0::3], state[1::3], state[2::3]
    axes = (1, 1, 1, 0, 0)
    full = [
        lax.all_gather(weight.astype(jnp.bfloat16), "dp", axis=axis, tiled=True)
        for weight, axis in zip(masters, axes)
    ]
    kernel, vector, up, down, strided = full
    values = vector.astype(jnp.float32)
    sections, rank = lax.axis_size("section"), lax.axis_index("section")
    micro_count = big_crops.shape[0]
    own = micro_count // sections

    def take(array):
        return lax.dynamic_slice_in_dim(array, rank * own, own, 0)

    keep = take(drop_mask).astype(jnp.float32) / KEEP_RATE
    outputs, grads, totals = [], [], None
    for crops, cot, images in ((big_crops, big_cot, BIG_IMG), (small_crops, small_cot, SMALL_IMG)):
        mine, my_cot = take(crops), take(cot)
        result, grad, parts = group_step(
            mine.reshape(-1, *crops.shape[2:]),
            my_cot.reshape(-1, *cot.shape[2:]),
            jnp.repeat(keep, images, axis=1).reshape(-1),
            kernel,
            values,
            up,
            down,
            strided,
        )
        outputs.append(result.reshape(my_cot.shape))
        grads.append(grad.reshape(mine.shape))
        totals = parts if totals is None else [a + b for a, b in zip(totals, parts)]
    pixel_total = (
        lax.axis_size("dp")
        * micro_count
        * (math.prod(big_crops.shape[1:4]) + math.prod(small_crops.shape[1:4]))
    )
    updates = []
    for position in range(5):
        gradient = lax.psum_scatter(totals[position], "dp", scatter_dimension=axes[position], tiled=True)
        gradient = lax.psum(gradient, "section")
        step_rate = RATES[position] * math.sqrt(FANS[position] / pixel_total)
        moment_next = MOMENTUM * moments[position] + gradient
        weight_next = masters[position] - step_rate * (gradient + MOMENTUM * moment_next)
        average_next = AVERAGING * averages[position] + (1.0 - AVERAGING) * weight_next
        updates += [weight_next, moment_next, average_next]
    return (*outputs, *grads, *updates)


UNIT = 4
MESH = pl.DeviceIdType.MESH
F32, BF16 = jnp.float32, jnp.bfloat16
BIG_SIDE, SMALL_SIDE = 14, 6
BIG_HALF, SMALL_HALF = 7, 3
BIG_ROWS = BIG_HALF * BIG_SIDE * 8
SMALL_ROWS = SMALL_HALF * SMALL_SIDE * 8
UNITS = 3
ROWS = BIG_ROWS + UNITS * SMALL_ROWS
HALO_BIG = (BIG_HALF + 6) * BIG_SIDE * 8
HALO_SMALL = (SMALL_HALF + 6) * SMALL_SIDE * 8
BLOCK_BIG = 7 * 32
BLOCKS = BLOCK_BIG + UNITS * 3 * 16
TILE = 304
CHUNK = C
PIECE = 48
PLANES = 4
COPIES = 118
UP_SCALE, DOWN_SCALE, STRIDED_SCALE = 1 / math.sqrt(C), 1 / math.sqrt(FF), 1 / math.sqrt(4 * C)
TAPS = KS * KS
V_BIAS_DW, V_GAIN_ONE, V_OFFSET_ONE, V_BIAS_UP = 0, 1, 2, 3
V_BIAS_DOWN, V_SCALE, V_GAIN_TWO, V_OFFSET_TWO, V_BIAS_OUT = 7, 8, 9, 10, 11


def nn(a, b):
    return jnp.dot(a, b, preferred_element_type=F32)


def rows_at(start, size):
    return pl.ds(aligned(start, 8), size)


def aligned(value, factor):
    return value if isinstance(value, int) else pl.multiple_of(value, factor)


def unrolled(count, step):
    for index in range(count):
        step(index, 0)


def one_hot(shape, target, valid=None):
    row = lax.broadcasted_iota(jnp.int32, shape, 0)
    column = lax.broadcasted_iota(jnp.int32, shape, 1)
    hit = column == target(row)
    if valid is not None:
        hit = hit & valid(row)
    return jnp.where(hit, 1.0, 0.0).astype(BF16)


def flat(value):
    return value.reshape(-1, value.shape[-1])


def step_kernel(
    big_hbm, small_hbm, big_cot_hbm, small_cot_hbm, keep_ref, kernel_ref, vector_ref, up_shard, down_shard, strided_shard,
    out_big_hbm, out_small_hbm, grad_big_hbm, grad_small_hbm, kv_out, up_out, down_out, strided_out,
    out_big_ref, out_small_ref, grad_big_ref, grad_small_ref,
    xb_raw, xs_raw, gb_raw, gs_raw, halo_big, halo_small, taps, vec, conv, rstd_one, normed,
    hidden, slope, branch, xhat, rstd_two, zeta, blocks, d_blocks, g_wide, g_rows, d_branch, d_pre,
    dhalo_big, dhalo_small, d_taps, d_vec, d_bias_up,
    kv_all, w_all, d_all, landing, plane_in, totals, line_in, final,
    d_kv, kv_part, kv_in, kv_sum,
    sems, send_sems, recv_sems,
):
    pad_big, d_zeta, d_normed, d_mixed = branch.at[0:896], dhalo_big.at[0:ROWS], zeta, xhat
    rank, dp_rank = lax.axis_index("section"), lax.axis_index("dp")
    row, column = rank // 2, lax.rem(rank, 2)
    line, core = dp_rank // 2, lax.rem(dp_rank, 2)
    flanks = (rank + 1 - 2 * column, rank + 2 - 4 * row, 3 - rank)
    twin = {"section": rank, "dp": dp_rank + 1 - 2 * core}

    def ahead(offset):
        return lax.rem(line + offset, PLANES)

    def on_line(offset):
        return {"section": rank, "dp": ahead(offset) * 2 + core}

    def on_plane(index):
        return {"section": flanks[index], "dp": dp_rank}

    barrier = pltpu.get_barrier_semaphore()
    def on_group(offset):
        return {"section": rank, "dp": lax.rem(dp_rank + offset, 8)}

    for target in [on_plane(index) for index in range(3)] + [on_group(offset) for offset in range(1, 8)]:
        pl.semaphore_signal(barrier, inc=1, device_id=target, device_id_type=MESH)

    made = []

    def plan(source, target_ref, target):
        index = len(made)
        copy = pltpu.make_async_remote_copy(
            source, target_ref, send_sems.at[index], recv_sems.at[index], device_id=target, device_id_type=MESH
        )
        made.append(copy)
        return copy

    def same(ref, target):
        return plan(ref, ref, target)

    def go(copies):
        for copy in copies:
            copy.start()

    def arrived(copies):
        for copy in copies:
            copy.wait_recv()

    def piece(index):
        return pl.ds(aligned(index * PIECE, 16), PIECE)

    offsets = (1, 2, 3)

    kv_ways = [same(kv_all.at[line, core], on_line(offset)) for offset in offsets]
    kv_twin = [same(kv_all.at[:, core], twin)]
    along, across, twins = [], [], []
    for weight in range(4):
        def part(offset, quarter):
            return w_all.at[weight, ahead(PLANES - offset), core, piece(quarter)]

        along.append([same(w_all.at[weight, line, core, piece(rank)], on_line(offset)) for offset in offsets])
        across.append([[same(part(offset, rank), on_plane(index)) for offset in offsets] for index in range(3)])
        twins.append([same(w_all.at[weight, :, core, piece(quarter)], twin) for quarter in (rank,) + flanks])

    def pass_line(weight):
        arrived(along[weight])
        for copies in across[weight]:
            go(copies)
        go(twins[weight][:1])

    def pass_plane(weight):
        for index, copies in enumerate(across[weight]):
            arrived(copies)
            go(twins[weight][1 + index : 2 + index])

    def held(weight):
        arrived(twins[weight])

    red_core, red_plane, red_line, red_back = [], [], [], []
    corners = ((row, 1 - column), (1 - row, column), (1 - row, 1 - column))
    for weight in range(4):
        red_core.append([plan(d_all.at[weight, :, 1 - core], landing.at[weight], twin)])
        red_plane.append(
            [
                plan(landing.at[weight, :, at_row, at_column], plane_in.at[weight, index], on_plane(index))
                for index, (at_row, at_column) in enumerate(corners)
            ]
        )
        red_line.append(
            [plan(totals.at[weight, ahead(offset)], line_in.at[weight, offset - 1], on_line(offset)) for offset in offsets]
        )
        red_back.append([same(final.at[weight, rank], on_plane(index)) for index in range(3)])

    def sum_core(weight):
        arrived(red_core[weight])

        def step(index, _):
            landing[weight, index] = (
                landing[weight, index].astype(F32) + d_all[weight, index, core].astype(F32)
            ).astype(BF16)
            return 0

        lax.fori_loop(0, PLANES, step, 0)
        go(red_plane[weight])

    def sum_plane(weight):
        arrived(red_plane[weight])
        for index in range(PLANES):
            total = landing[weight, index, row, column].astype(F32)
            for source in range(3):
                total = total + plane_in[weight, source, index].astype(F32)
            totals[weight, index] = total.astype(BF16)
        go(red_line[weight])

    def sum_line(weight):
        arrived(red_line[weight])
        total = totals[weight, line].astype(F32)
        for offset in offsets:
            total = total + line_in[weight, offset - 1].astype(F32)
        final[weight, rank] = total.astype(BF16)
        go(red_back[weight])

    kv_across = [
        plan(kv_part.at[lax.rem(dp_rank + offset, 8)], kv_in.at[offset - 1], on_group(offset)) for offset in range(1, 8)
    ]
    kv_back = [same(kv_sum.at[rank], on_plane(index)) for index in range(3)]

    def kv_sum_group():
        arrived(kv_across)
        total = kv_part[dp_rank].astype(F32)
        for index in range(7):
            total = total + kv_in[index].astype(F32)
        kv_sum[rank] = total
        go(kv_back)

    w_all[0, line, core] = up_shard[...].astype(BF16)
    w_all[1, line, core] = down_shard[...].astype(BF16)
    w_all[2, line, core] = strided_shard[:, :C].astype(BF16)
    w_all[3, line, core] = strided_shard[:, C:].astype(BF16)
    put_taps = one_hot((TAPS, 128), lambda r: r)
    put_vector = one_hot((13, 128), lambda r: r + 64)
    kv_all[line, core] = (
        nn(kernel_ref[...].astype(BF16), put_taps)
        + lax.dot_general(
            vector_ref[...].astype(BF16), put_vector, (((0,), (0,)), ((), ())), preferred_element_type=F32
        )
    ).astype(BF16)
    pl.semaphore_wait(barrier, 10)
    go(kv_ways)
    for weight in range(4):
        go(along[weight])

    def at_step(step, hooks):
        for when, event in hooks:
            pl.when(step == when)(event)

    def events(*calls):
        def run():
            for call, *arguments in calls:
                call(*arguments)

        return run

    own = pl.ds(rank * 2, 2)
    copies = [
        pltpu.make_async_copy(source, target, sems.at[index])
        for index, (source, target) in enumerate(
            (
                (big_hbm.at[own], xb_raw),
                (small_hbm, xs_raw),
                (big_cot_hbm.at[own], gb_raw),
                (small_cot_hbm, gs_raw),
            )
        )
    ]
    for copy in copies:
        copy.start()

    spread_big = one_hot((112, 128), lambda r: ((r >> 1) & 3) * 32 + (r >> 3) * 2 + (r & 1))
    spread_small = one_hot((48, 192), lambda r: ((r >> 1) & 3) * 48 + (r >> 3) * 8 + 2 * rank + (r & 1))
    gather_big = one_hot((128, 112), lambda r: ((r >> 1) & 15) * 8 + (r >> 5) * 2 + (r & 1))
    gather_small = one_hot((64, 48), lambda r: ((r >> 1) & 7) * 8 + (r >> 4) * 2 + (r & 1))
    block_big = one_hot(
        (128, 112), lambda r: (((r >> 1) & 7) * 2 + ((r >> 5) & 1)) * 8 + (r >> 6) * 4 + ((r >> 4) & 1) * 2 + (r & 1)
    )
    block_small = one_hot(
        (64, 48), lambda r: (((r >> 1) & 3) * 2 + ((r >> 4) & 1)) * 8 + (r >> 5) * 4 + ((r >> 3) & 1) * 2 + (r & 1)
    )
    pick_small = one_hot(
        (16, 48), lambda r: (r >> 3) * 24 + ((r >> 1) & 3) * 8 + 2 * rank + (r & 1), lambda r: (r & 7) < 6
    )
    sub = lax.broadcasted_iota(jnp.int32, (8, 128), 0)
    top = jnp.where(sub < 4, 1.0, 0.0).astype(F32)
    bottom = 1.0 - top

    def vector_row(index):
        return vec[index : index + 1, :]

    keep_zero = keep_ref[0, 2 * rank].astype(F32) / KEEP_RATE
    keep_one = keep_ref[0, 2 * rank + 1].astype(F32) / KEEP_RATE
    lane_wide = lambda value: jnp.concatenate([value] * 3, axis=1)
    big_factor = lane_wide(jnp.where((sub & 2) == 0, keep_zero, keep_one))
    small_factor = lane_wide(jnp.where((sub & 1) == 0, keep_zero, keep_one))

    pad_big[...] = jnp.zeros_like(pad_big)
    g_wide[...] = jnp.zeros_like(g_wide)

    for copy in copies:
        copy.wait()

    for micro in range(2):
        def put_big(h, _):
            pad_big[rows_at((micro * 14 + h) * 32, 28), :] = xb_raw[micro, h].astype(F32).reshape(28, C)
            return 0

        unrolled(14, put_big)
        for p in range(7):
            start = p * 32 + micro * 16
            g_wide[start : start + 14, :] = gb_raw[micro, p].astype(F32).reshape(14, C2)
    for unit in range(UNITS):
        for p in range(3):
            source = jnp.concatenate(
                [gs_raw[2 * unit + crop, p].astype(F32).reshape(24, C2) for crop in range(2)], axis=0
            )
            start = BLOCK_BIG + (unit * 3 + p) * 16
            g_wide[start : start + 16, :] = nn(pick_small, source.astype(BF16))

    arrived(kv_ways)
    go(kv_twin)

    def spread_rows(hh, _):
        tiles = [pad_big[rows_at((micro * 14 + half * 7 + hh) * 32, 32), :] for half in range(2) for micro in range(2)]
        source = jnp.concatenate(tiles, axis=0).astype(BF16)
        halo_big[rows_at((hh + 3) * 112, 112), :] = nn(spread_big, source)
        return 0

    unrolled(BIG_HALF, spread_rows)
    for unit in range(UNITS):
        def spread_unit(hh, _):
            tiles = [
                xs_raw[2 * unit + crop, half * 3 + hh].reshape(48, C) for half in range(2) for crop in range(2)
            ]
            source = jnp.concatenate(tiles, axis=0)
            halo_small[rows_at(unit * HALO_SMALL + (hh + 3) * 48, 48), :] = nn(spread_small, source)
            return 0

        unrolled(SMALL_HALF, spread_unit)

    def halos(ref, base, half, side):
        def step(index, _):
            for lane in range(3):
                lanes = slice(lane * 128, lane * 128 + 128)
                low = ref[rows_at(base + (3 * side + index) * 8, 8), lanes]
                ref[rows_at(base + ((3 + half) * side + index) * 8, 8), lanes] = pltpu.roll(low, 4, 0) * top
                high = ref[rows_at(base + (half * side + index) * 8, 8), lanes]
                ref[rows_at(base + index * 8, 8), lanes] = pltpu.roll(high, 4, 0) * bottom
            return 0

        unrolled(3 * side, step)

    def all_halos(big, small):
        halos(big, 0, BIG_HALF, BIG_SIDE)
        for unit in range(UNITS):
            halos(small, unit * HALO_SMALL, SMALL_HALF, SMALL_SIDE)

    all_halos(halo_big, halo_small)

    arrived(kv_twin)
    kv = jnp.transpose(flat(kv_all[...]).astype(F32))
    vec[...] = kv[64:80]
    for tap in range(TAPS):
        taps[tap] = jnp.broadcast_to(kv[tap : tap + 1] * (1.0 / KS), (8, C))

    def convolve(big, small, mirrored, finish, hooks):
        def tap_at(i, j, lanes):
            index = i * KS + j
            return taps[TAPS - 1 - index if mirrored else index, :, lanes]

        def image_row(step, _):
            h, lane = step // 3, lax.rem(step, 3)
            lanes = pl.ds(aligned(lane * 128, 128), 128)
            sums = [None] * BIG_SIDE
            for i in range(KS):
                values = [big[rows_at(((h + i) * BIG_SIDE + w) * 8, 8), lanes] for w in range(BIG_SIDE)]
                for j in range(KS):
                    weight = tap_at(i, j, lanes)
                    for w in range(max(0, 3 - j), min(BIG_SIDE, BIG_SIDE + 3 - j)):
                        term = values[w + j - 3] * weight
                        sums[w] = term if sums[w] is None else sums[w] + term
            for w in range(BIG_SIDE):
                finish((h * BIG_SIDE + w) * 8, sums[w], lanes)
            at_step(step, hooks)
            return 0

        lax.fori_loop(0, BIG_HALF * 3, image_row, 0)

        def small_row(step, _):
            h, lane = step // 3, lax.rem(step, 3)
            lanes = pl.ds(aligned(lane * 128, 128), 128)
            sums = [[None] * SMALL_SIDE for _ in range(UNITS)]
            for i in range(KS):
                values = [
                    [
                        small[rows_at(unit * HALO_SMALL + ((h + i) * SMALL_SIDE + w) * 8, 8), lanes]
                        for w in range(SMALL_SIDE)
                    ]
                    for unit in range(UNITS)
                ]
                for j in range(KS):
                    weight = tap_at(i, j, lanes)
                    for w in range(max(0, 3 - j), min(SMALL_SIDE, SMALL_SIDE + 3 - j)):
                        for unit in range(UNITS):
                            term = values[unit][w + j - 3] * weight
                            old = sums[unit][w]
                            sums[unit][w] = term if old is None else old + term
            for unit in range(UNITS):
                for w in range(SMALL_SIDE):
                    finish(BIG_ROWS + unit * SMALL_ROWS + (h * SMALL_SIDE + w) * 8, sums[unit][w], lanes)
            return 0

        lax.fori_loop(0, SMALL_HALF * 3, small_row, 0)

    def keep_conv(start, value, lanes):
        conv[rows_at(start, 8), lanes] = value

    convolve(halo_big, halo_small, False, keep_conv, [(3, events((pass_line, 0))), (20, events((pass_line, 1)))])
    pass_plane(0)

    def for_tiles(run):
        def big_tile(index, _):
            run(index * 112, 112, big_factor, halo_big, dhalo_big, 336 + index * 112)
            return 0

        unrolled(BIG_HALF, big_tile)

        def small_tile(index, _):
            run(BIG_ROWS + index * 144, 144, small_factor, halo_small, dhalo_small, index * HALO_SMALL + 144)
            return 0

        unrolled(UNITS, small_tile)

    def fold(value):
        return jnp.sum(value.reshape(-1, 8, value.shape[-1]), axis=0)

    def mean_of(value):
        return jnp.sum(value, axis=-1, keepdims=True) * (1.0 / C)

    def wide(ref, rows):
        value = ref[rows, :]
        return jnp.concatenate([value, value, value], axis=1)

    def norm_one(start, size, *_):
        rows = rows_at(start, size)
        value = conv[rows, :] + vector_row(V_BIAS_DW)
        centered = value - mean_of(value)
        scale = lax.rsqrt(mean_of(centered * centered) + EPSILON)
        unit = centered * scale
        conv[rows, :] = unit
        rstd_one[rows, :] = jnp.broadcast_to(scale, (size, 128))
        normed[pl.ds(aligned(start, 16), size), :] = (
            unit * vector_row(V_GAIN_ONE) + vector_row(V_OFFSET_ONE)
        ).astype(BF16)

    for_tiles(norm_one)
    pass_line(2)

    def up_tile(index, _):
        rows = pl.ds(aligned(index * TILE, 16), TILE)
        left = normed[rows, :]
        for chunk in range(FF // CHUNK):
            span = slice(chunk * CHUNK, (chunk + 1) * CHUNK)
            bias = vector_row(V_BIAS_UP + chunk)
            pre = (
                lax.dot_general(left, flat(w_all[0, chunk]), (((1,), (1,)), ((), ())), preferred_element_type=F32)
                * UP_SCALE
                + bias
            )
            scaled_pre = pre * math.sqrt(0.5)
            whole = 0.5 + 0.5 * lax.erf(scaled_pre)
            density = jnp.exp2(scaled_pre * scaled_pre * -math.log2(math.e))
            hidden[rows, span] = (pre * whole).astype(BF16)
            slope[rows, span] = whole + pre * density * (1.0 / math.sqrt(2.0 * math.pi))
        at_step(index, [(0, events((pass_line, 3))), (2, events((pass_plane, 1)))])
        return 0

    held(0)
    unrolled(ROWS // TILE, up_tile)
    held(1)

    def branch_tile(index, _):
        rows = pl.ds(aligned(index * TILE, 16), TILE)
        branch[rows, :] = nn(hidden[rows, :], flat(w_all[1])) * DOWN_SCALE + vector_row(V_BIAS_DOWN)
        return 0

    unrolled(ROWS // TILE, branch_tile)

    def scaled(value, factor):
        return (value.reshape(-1, 8, C) * factor[None]).reshape(-1, C)

    def norm_two(start, size, factor, field, _, offset):
        rows = rows_at(start, size)
        value = field[rows_at(offset, size), :] + scaled(vector_row(V_SCALE) * branch[rows, :], factor)
        centered = value - mean_of(value)
        scale = lax.rsqrt(mean_of(centered * centered) + EPSILON)
        unit = centered * scale
        xhat[rows, :] = unit
        rstd_two[rows, :] = jnp.broadcast_to(scale, (size, 128))
        zeta[pl.ds(aligned(start, 16), size), :] = (
            unit * vector_row(V_GAIN_TWO) + vector_row(V_OFFSET_TWO)
        ).astype(BF16)

    for_tiles(norm_two)

    def block_spans(base, count, hh, half_side):
        for half in range(2):
            h = half * half_side + hh
            p, a = h // 2, h % 2
            for b in range(2):
                yield (
                    pl.ds(aligned(base + p * count, 16), count),
                    pl.ds(aligned((2 * a + b) * C, 128), C),
                )

    def block_rows(source, matrix, base, count, hh, half_side):
        picked = nn(matrix, source).astype(BF16)
        for index, span in enumerate(block_spans(base, count, hh, half_side)):
            blocks[span] = picked[index * count : (index + 1) * count]

    def big_blocks(hh, _):
        block_rows(zeta[pl.ds(aligned(hh * 112, 16), 112), :], block_big, 0, 32, hh, 7)
        return 0

    unrolled(BIG_HALF, big_blocks)
    for unit in range(UNITS):
        def small_blocks(hh, _):
            source = zeta[pl.ds(aligned(BIG_ROWS + unit * SMALL_ROWS + hh * 48, 16), 48), :]
            block_rows(source, block_small, BLOCK_BIG + unit * 48, 16, hh, 3)
            return 0

        unrolled(SMALL_HALF, small_blocks)

    g_rows[...] = g_wide[...].astype(BF16)
    bias_out_grad = jnp.sum(g_wide[...], axis=0, keepdims=True)
    d_vec[V_BIAS_OUT, 0:1, :] = bias_out_grad[:, :C]
    d_vec[V_BIAS_OUT + 1, 0:1, :] = bias_out_grad[:, C:]

    def outer(left, right, scale):
        product = lax.dot_general(left, right, (((0,), (0,)), ((), ())), preferred_element_type=F32)
        return (product * scale).astype(BF16).reshape(2, 2, 2, PIECE, C)

    for half in range(2):
        def strided_grad(index, _):
            span = pl.ds(aligned(index * C, 128), C)
            d_all[2 + half, index] = outer(blocks[:, span], g_rows[:, half * C : half * C + C], STRIDED_SCALE)
            return 0

        unrolled(4, strided_grad)
        go(red_core[2 + half])
        if half == 0:
            pass_plane(2)

    bias_out = jnp.concatenate([vector_row(V_BIAS_OUT), vector_row(V_BIAS_OUT + 1)], axis=1)

    def out_half(half):
        span = slice(half * C, half * C + C)
        g_wide[:, span] = nn(blocks[...], flat(w_all[2 + half])) * STRIDED_SCALE + bias_out[:, span]

    held(2)
    out_half(0)
    pass_plane(3)
    held(3)

    def block_grad(index, _):
        span = pl.ds(aligned(index * 384, 128), 384)
        total = None
        for half in range(2):
            term = lax.dot_general(
                g_rows[:, half * C : half * C + C],
                flat(w_all[2 + half, index]),
                (((1,), (1,)), ((), ())),
                preferred_element_type=F32,
            )
            total = term if total is None else total + term
        d_blocks[:, span] = (total * STRIDED_SCALE).astype(BF16)
        return 0

    unrolled(4, block_grad)

    def unblock(matrix, base, count, hh, half_side):
        parts = jnp.concatenate([d_blocks[span] for span in block_spans(base, count, hh, half_side)], axis=0)
        return lax.dot_general(matrix, parts, (((0,), (0,)), ((), ())), preferred_element_type=F32)

    def big_unblock(hh, _):
        d_zeta[rows_at(hh * 112, 112), :] = unblock(block_big, 0, 32, hh, 7)
        return 0

    unrolled(BIG_HALF, big_unblock)
    for unit in range(UNITS):
        def small_unblock(hh, _):
            d_zeta[rows_at(BIG_ROWS + unit * SMALL_ROWS + hh * 48, 48), :] = unblock(
                block_small, BLOCK_BIG + unit * 48, 16, hh, 3
            )
            return 0

        unrolled(SMALL_HALF, small_unblock)

    sum_core(2)

    for index in range(11):
        d_vec[index] = jnp.zeros((8, C), F32)

    def norm_two_back(start, size, factor, *_):
        rows = rows_at(start, size)
        unit = xhat[rows, :]
        grad = d_zeta[rows, :]
        d_vec[V_GAIN_TWO] += fold(grad * unit)
        d_vec[V_OFFSET_TWO] += fold(grad)
        inner = grad * vector_row(V_GAIN_TWO)
        mixed = (inner - mean_of(inner) - unit * mean_of(inner * unit)) * wide(rstd_two, rows)
        d_mixed[rows, :] = mixed
        kept = scaled(mixed, factor)
        d_vec[V_SCALE] += fold(kept * branch[rows, :])
        lowered = (kept * vector_row(V_SCALE)).astype(BF16)
        d_branch[pl.ds(aligned(start, 16), size), :] = lowered
        d_vec[V_BIAS_DOWN] += fold(lowered.astype(F32))

    for_tiles(norm_two_back)
    sum_core(3)

    def down_grad(index, _):
        span = pl.ds(aligned(index * C, 128), C)
        d_all[1, index] = outer(hidden[:, span], d_branch[...], DOWN_SCALE)
        return 0

    unrolled(4, down_grad)
    go(red_core[1])

    d_bias_up[...] = jnp.zeros_like(d_bias_up)

    def down_tile(index, _):
        rows = pl.ds(aligned(index * TILE, 16), TILE)
        left = d_branch[rows, :]
        for chunk in range(FF // CHUNK):
            span = slice(chunk * CHUNK, (chunk + 1) * CHUNK)
            d_hidden = (
                lax.dot_general(left, flat(w_all[1, chunk]), (((1,), (1,)), ((), ())), preferred_element_type=F32)
                * DOWN_SCALE
            )
            lowered = (d_hidden * slope[rows, span]).astype(BF16)
            d_pre[rows, span] = lowered
            d_bias_up[:, span] += fold(lowered.astype(F32))
        d_normed[rows, :] = (nn(d_pre[rows, :], flat(w_all[0])) * UP_SCALE).astype(BF16)
        at_step(index, [(2, events((sum_core, 1))), (3, events((sum_plane, 2)))])
        return 0

    unrolled(ROWS // TILE, down_tile)

    def up_grad(index, _):
        span = pl.ds(aligned(index * C, 128), C)
        d_all[0, index] = outer(d_pre[:, span], normed[...], UP_SCALE)
        return 0

    unrolled(4, up_grad)
    go(red_core[0])

    def norm_one_back(start, size, _, __, target, offset):
        rows = rows_at(start, size)
        unit = conv[rows, :]
        grad = d_normed[pl.ds(aligned(start, 16), size), :].astype(F32)
        d_vec[V_GAIN_ONE] += fold(grad * unit)
        d_vec[V_OFFSET_ONE] += fold(grad)
        inner = grad * vector_row(V_GAIN_ONE)
        result = (inner - mean_of(inner) - unit * mean_of(inner * unit)) * wide(rstd_one, rows)
        d_vec[V_BIAS_DW] += fold(result)
        target[rows_at(offset, size), :] = result

    for_tiles(norm_one_back)
    all_halos(dhalo_big, dhalo_small)

    def tap_grads(step, _):
        i, lane = step // 3, lax.rem(step, 3)
        lanes = pl.ds(aligned(lane * 128, 128), 128)

        sums = [[None, None] for _ in range(KS)]

        def image_row(side, field, grad, field_base, grad_base, turn):
            inputs = [field[rows_at(field_base + w * 8, 8), lanes] for w in range(side)]
            outer = [grad[rows_at(grad_base + w * 8, 8), lanes] for w in range(side)]
            for w in range(side):
                for j in range(max(0, 3 - w), min(KS, side + 3 - w)):
                    term = inputs[w + j - 3] * outer[w]
                    slot = (w + turn) % 2
                    old = sums[j][slot]
                    sums[j][slot] = term if old is None else old + term

        for h in range(BIG_HALF):
            image_row(BIG_SIDE, halo_big, dhalo_big, (h + i) * 112, (h + 3) * 112, h)
        for h in range(SMALL_HALF):
            for unit in range(UNITS):
                base = unit * HALO_SMALL
                image_row(SMALL_SIDE, halo_small, dhalo_small, base + (h + i) * 48, base + (h + 3) * 48, h)
        for j in range(KS):
            d_taps[i * KS + j, :, lanes] = sums[j][0] + sums[j][1]
        at_step(
            step,
            [
                (3, events((sum_plane, 3))),
                (5, events((sum_core, 0))),
                (7, events((sum_line, 2))),
                (16, events((sum_line, 3))),
                (19, events((sum_plane, 1))),
            ],
        )
        return 0

    lax.fori_loop(0, KS * 3, tap_grads, 0)

    d_kv[56:128, :] = jnp.zeros((72, C), F32)
    for tap in range(TAPS):
        d_kv[tap : tap + 1, :] = jnp.sum(d_taps[tap], axis=0, keepdims=True) * (1.0 / KS)
    for index in range(11):
        if V_BIAS_UP <= index < V_BIAS_UP + UP_ROWS:
            continue
        d_kv[TAPS + index : TAPS + index + 1, :] = jnp.sum(d_vec[index], axis=0, keepdims=True)
    d_kv[TAPS + V_BIAS_OUT : TAPS + V_BIAS_OUT + 1, :] = d_vec[V_BIAS_OUT, 0:1, :]
    d_kv[TAPS + V_BIAS_OUT + 1 : TAPS + V_BIAS_OUT + 2, :] = d_vec[V_BIAS_OUT + 1, 0:1, :]
    bias_up_grad = jnp.sum(d_bias_up[...], axis=0, keepdims=True)
    for index in range(UP_ROWS):
        d_kv[TAPS + V_BIAS_UP + index : TAPS + V_BIAS_UP + index + 1, :] = bias_up_grad[
            :, index * C : (index + 1) * C
        ]

    kv_part[...] = jnp.transpose(d_kv[...]).astype(BF16).reshape(8, PIECE, 128)
    go(kv_across)

    def add_grad(start, value, lanes):
        d_mixed[rows_at(start, 8), lanes] += value

    convolve(
        dhalo_big,
        dhalo_small,
        True,
        add_grad,
        [
            (14, events((sum_line, 1), (kv_sum_group,))),
            (18, events((sum_plane, 0))),
        ],
    )
    out_half(1)
    for micro in range(2):
        for p in range(7):
            start = p * 32 + micro * 16
            out_big_ref[micro, p] = g_wide[start : start + 14, :].reshape(7, 2, C2)
    for unit in range(UNITS):
        for p in range(3):
            for crop in range(2):
                start = BLOCK_BIG + (unit * 3 + p) * 16 + crop * 8
                out_small_ref[2 * unit + crop, p] = g_wide[start : start + 6, :].reshape(3, 2, C2)


    sum_line(0)

    def restore(matrix, value):
        high = value.astype(BF16)
        low = (value - high.astype(F32)).astype(BF16)
        return nn(matrix, high) + nn(matrix, low)

    def grad_rows(hh, _):
        natural = restore(gather_big, d_mixed[rows_at(hh * 112, 112), :])
        for half in range(2):
            for micro in range(2):
                start = (half * 2 + micro) * 32
                grad_big_ref[micro, half * 7 + hh] = natural[start : start + 28].reshape(14, 2, C)
        return 0

    unrolled(BIG_HALF, grad_rows)
    for unit in range(UNITS):
        def small_grad_rows(hh, _):
            natural = restore(gather_small, d_mixed[rows_at(BIG_ROWS + unit * SMALL_ROWS + hh * 48, 48), :])
            for half in range(2):
                for crop in range(2):
                    start = (half * 2 + crop) * 16
                    grad_small_ref[2 * unit + crop, half * 3 + hh] = natural[start : start + 12].reshape(6, 2, C)
            return 0

        unrolled(SMALL_HALF, small_grad_rows)

    leaving = [
        pltpu.make_async_copy(source, target, sems.at[4 + index])
        for index, (source, target) in enumerate(
            (
                (out_big_ref, out_big_hbm),
                (out_small_ref, out_small_hbm),
                (grad_big_ref, grad_big_hbm),
                (grad_small_ref, grad_small_hbm),
            )
        )
    ]
    for copy in leaving:
        copy.start()
    for weight in range(4):
        arrived(red_back[weight])
    up_out[...] = flat(final[0])
    down_out[...] = flat(final[1])
    strided_out[:, :C] = flat(final[2])
    strided_out[:, C:] = flat(final[3])
    arrived(kv_back)
    kv_out[...] = kv_sum[0] + kv_sum[1] + kv_sum[2] + kv_sum[3]
    for copy in made:
        copy.wait_send()
    for copy in leaving:
        copy.wait()


def finish_kernel(rates, *refs):
    sources, outs, held, fresh, sems = refs[:23], refs[23:42], refs[42:65], refs[65:80], refs[80]
    inward = [pltpu.make_async_copy(source, target, sems.at[index]) for index, (source, target) in enumerate(zip(sources, held))]
    outward = [
        pltpu.make_async_copy(source, target, sems.at[23 + index])
        for index, (source, target) in enumerate(zip((*held[19:], *fresh), outs))
    ]
    order = (4, 3, 2, 1, 0)
    for index in (19, 21):
        inward[index].start()
    for position in order:
        if position:
            inward[position - 1].start()
        for index in range(4 + 3 * position, 7 + 3 * position):
            inward[index].start()
    for index in (20, 22):
        inward[index].start()
    for index in (19, 21):
        inward[index].wait()
        outward[index - 19].start()
    for position in order:
        state = range(4 + 3 * position, 7 + 3 * position)
        for index in state:
            inward[index].wait()
        if position >= 2:
            inward[position - 1].wait()
            gradient = held[position - 1][...].astype(F32)
        elif position == 1:
            inward[0].wait()
            gradient = jnp.transpose(held[0][...])[TAPS : TAPS + 13]
        else:
            gradient = held[0][:, :TAPS]
        weight, moment, average = (held[index][...] for index in state)
        moment_next = MOMENTUM * moment + gradient
        weight_next = weight - rates[position] * (gradient + MOMENTUM * moment_next)
        results = (weight_next, moment_next, AVERAGING * average + (1.0 - AVERAGING) * weight_next)
        for index, value in enumerate(results):
            fresh[3 * position + index][...] = value
            outward[4 + 3 * position + index].start()
    for index in (20, 22):
        inward[index].wait()
        outward[index - 19].start()
    for copy in outward:
        copy.wait()


def finish(rates, grads, state, images):
    any_spec = pl.BlockSpec(memory_space=pl.ANY)
    inputs = (*grads, *state, *images)
    return pl.pallas_call(
        functools.partial(finish_kernel, rates),
        out_shape=[jax.ShapeDtypeStruct(array.shape, F32) for array in (*images, *state)],
        in_specs=[any_spec] * 23,
        out_specs=[any_spec] * 19,
        scratch_shapes=[pltpu.VMEM(array.shape, array.dtype) for array in inputs]
        + [pltpu.VMEM(array.shape, F32) for array in state]
        + [pltpu.SemaphoreType.DMA((42,))],
        compiler_params=pltpu.CompilerParams(vmem_limit_bytes=(63 << 20) + (1 << 19)),
    )(*inputs)


def fused_step(big_crops, small_crops, big_cot, small_cot, keep, kernel_t, vector, up_t, down, strided):
    any_spec = pl.BlockSpec(memory_space=pl.ANY)
    vmem = pl.BlockSpec(memory_space=pltpu.VMEM)
    shape = jax.ShapeDtypeStruct
    big_order, small_order = (0, 2, 3, 1, 4), (1, 2, 3, 0, 4)
    results = pl.pallas_call(
        step_kernel,
        out_shape=(
            shape((2, 7, 7, 2, C2), F32),
            shape((6, 3, 3, 2, C2), F32),
            shape((2, 14, 14, 2, C), F32),
            shape((6, 6, 6, 2, C), F32),
            shape((PIECE, 128), F32),
            shape((192, C), BF16),
            shape((192, C), BF16),
            shape((192, C2), BF16),
        ),
        in_specs=[any_spec] * 4 + [pl.BlockSpec(memory_space=pltpu.SMEM)] + [vmem] * 5,
        out_specs=[any_spec] * 4 + [vmem] * 4,
        scratch_shapes=[
            pltpu.VMEM((2, 7, 7, 2, C2), F32),
            pltpu.VMEM((6, 3, 3, 2, C2), F32),
            pltpu.VMEM((2, 14, 14, 2, C), F32),
            pltpu.VMEM((6, 6, 6, 2, C), F32),
            pltpu.VMEM((2, 14, 14, 2, C), BF16),
            pltpu.VMEM((6, 6, 6, 8, C), BF16),
            pltpu.VMEM((2, 7, 7, 2, C2), BF16),
            pltpu.VMEM((6, 3, 3, 8, C2), BF16),
            pltpu.VMEM((HALO_BIG, C), F32),
            pltpu.VMEM((UNITS * HALO_SMALL, C), F32),
            pltpu.VMEM((TAPS, 8, C), F32),
            pltpu.VMEM((16, C), F32),
            pltpu.VMEM((ROWS, C), F32),
            pltpu.VMEM((ROWS, 128), F32),
            pltpu.VMEM((ROWS, C), BF16),
            pltpu.VMEM((ROWS, FF), BF16),
            pltpu.VMEM((ROWS, FF), F32),
            pltpu.VMEM((ROWS, C), F32),
            pltpu.VMEM((ROWS, C), F32),
            pltpu.VMEM((ROWS, 128), F32),
            pltpu.VMEM((ROWS, C), BF16),
            pltpu.VMEM((BLOCKS, 4 * C), BF16),
            pltpu.VMEM((BLOCKS, 4 * C), BF16),
            pltpu.VMEM((BLOCKS, C2), F32),
            pltpu.VMEM((BLOCKS, C2), BF16),
            pltpu.VMEM((ROWS, C), BF16),
            pltpu.VMEM((ROWS, FF), BF16),
            pltpu.VMEM((HALO_BIG, C), F32),
            pltpu.VMEM((UNITS * HALO_SMALL, C), F32),
            pltpu.VMEM((TAPS, 8, C), F32),
            pltpu.VMEM((13, 8, C), F32),
            pltpu.VMEM((8, FF), F32),
            pltpu.VMEM((4, 2, 48, 128), BF16),
            pltpu.VMEM((4, 4, 2, 192, C), BF16),
            pltpu.VMEM((4, 4, 2, 2, 2, PIECE, C), BF16),
            pltpu.VMEM((4, 4, 2, 2, PIECE, C), BF16),
            pltpu.VMEM((4, 3, 4, PIECE, C), BF16),
            pltpu.VMEM((4, 4, PIECE, C), BF16),
            pltpu.VMEM((4, 3, PIECE, C), BF16),
            pltpu.VMEM((4, 4, PIECE, C), BF16),
            pltpu.VMEM((128, C), F32),
            pltpu.VMEM((8, PIECE, 128), BF16),
            pltpu.VMEM((7, PIECE, 128), BF16),
            pltpu.VMEM((4, PIECE, 128), F32),
            pltpu.SemaphoreType.DMA((8,)),
            pltpu.SemaphoreType.DMA((COPIES,)),
            pltpu.SemaphoreType.DMA((COPIES,)),
        ],
        compiler_params=pltpu.CompilerParams(vmem_limit_bytes=(63 << 20) + (1 << 19), collective_id=0, has_side_effects=True),
    )(
        big_crops.transpose(big_order),
        small_crops.transpose(small_order),
        big_cot.transpose(big_order),
        small_cot.transpose(small_order),
        keep,
        kernel_t,
        vector,
        up_t,
        down,
        strided,
    )
    return results[4:], results[:4]


def body(big_crops, small_crops, big_cot, small_cot, drop_mask, *state):
    sections, rank = lax.axis_size("section"), lax.axis_index("section")
    micro_count = big_crops.shape[0]
    fits = (
        micro_count == 2 * sections
        and big_crops.shape[1:] == (BIG_IMG, BIG_SIDE, BIG_SIDE, C)
        and small_crops.shape[1:] == (SMALL_IMG, SMALL_SIDE, SMALL_SIDE, C)
        and drop_mask.shape[1] == 1
        and (sections, lax.axis_size("dp")) == (4, 8)
    )
    if not fits:
        return plain_body(big_crops, small_crops, big_cot, small_cot, drop_mask, *state)
    masters, moments, averages = state[0::3], state[1::3], state[2::3]
    turned = (True, False, True, False, False)
    masters, moments, averages = (
        [jnp.transpose(array) if turn else array for array, turn in zip(group, turned)]
        for group in (masters, moments, averages)
    )
    grads, images = fused_step(big_crops, small_crops, big_cot, small_cot, drop_mask.T, *masters)
    pixel_total = (
        lax.axis_size("dp")
        * micro_count
        * (math.prod(big_crops.shape[1:4]) + math.prod(small_crops.shape[1:4]))
    )
    rates = tuple(rate * math.sqrt(fan / pixel_total) for rate, fan in zip(RATES, FANS))
    state = [array for group in zip(masters, moments, averages) for array in group]
    results = finish(rates, grads, state, images)
    order_big, order_small = (0, 3, 1, 2, 4), (3, 0, 1, 2, 4)
    return (
        results[0].transpose(order_big),
        results[1].transpose(order_small),
        results[2].transpose(order_big),
        results[3].transpose(order_small),
        *(array.T if turned[index // 3] else array for index, array in enumerate(results[4:])),
    )


def solution(mesh):
    crops = P(None, "dp", None, None, None)
    owned = P("section", "dp", None, None, None)
    weights = (P(None, "dp"),) * 9 + (P("dp", None),) * 6
    return jax.shard_map(
        body,
        mesh=mesh,
        in_specs=(crops,) * 4 + (P(None, "dp"),) + weights,
        out_specs=(owned,) * 4 + weights,
        check_vma=False,
    )
```
